32 devices in a mesh: gx: 4 (over y, x), gy: 8 (over z, core).
Axes of the slice: x: 2, y: 2, z: 4, core: 2. Of those that a mesh axis runs over, the one named last changes fastest.
Arguments:
- displacement: float32 [2, 3, 8, 512, 1024], P(None, None, None, 'gx', 'gy'), may hold values from -0.6 to 0.6
- velocity: float32 [2, 3, 8, 512, 1024], P(None, None, None, 'gx', 'gy'), may hold values from -3 to 3
- modulus: float32 [2, 8, 512, 1024], P(None, None, 'gx', 'gy'), may hold values from 0.5 to 2
- density: float32 [2, 8, 512, 1024], P(None, None, 'gx', 'gy'), may hold values from 1 to 4
- clearance: float32 [512, 1024], P('gx', 'gy'), may hold values from -0.3 to 0.3
- mortar_coupling: float32 [128, 128], replicated, may hold values from -0.5 to 0.5
- pair_owner: int32 [4, 2048, 1], P('gx', 'gy'), may hold values from 0 to 7; in each aligned block of 256 rows (0 to 255, 256 to 511, ..., all dimensions but the last counted through in order) at most 128 rows name the same one
- pair_row: int32 [4, 2048, 1], P('gx', 'gy'), may hold values from 0 to 127
- pair_offset: int32 [4, 2048, 1], P('gx', 'gy'), may hold values from 0 to 127
- pair_active: int32 [4, 2048, 1], P('gx', 'gy'), may hold values 0 or 1
Outputs:
- new_displacement: float32 [2, 3, 8, 512, 1024], P(None, None, None, 'gx', 'gy')
- new_velocity: float32 [2, 3, 8, 512, 1024], P(None, None, None, 'gx', 'gy')
The draws below stay inside these ranges and needn't reach their ends.
Inputs may be any that keep to these rules, and one draw needn't show every extreme that they name: `pair_owner`: in the pairs of one device, at most 128 name one owner, and one owner is named by exactly 128 pairs of some device.
All inputs are finite; a program needn't handle non-finite values. No bound on the sum of `pair_active` on one device may be relied on, other than what follows from the above.
Results may differ from the reference program's by a relative error of at most 0.0001.
Values sent between devices are 32-bit elements; how exact they have to be, the bound alone decides.
No kernel may reach another device: no remote copies, remote signals or barrier semaphores. Data moves between devices by JAX's collectives and lax.ppermute only.
A program may use at most 192 MiB of HBM per device.

```python
import math
import jax
import jax.numpy as jnp
import numpy as np
from jax import lax

CX = 128
TILE = 128
LAYERS = 8
INTERSECTIONS = 2
STEPS = 2
NX = 512
NY = 1024
PAIRS = 256
CAP = 128
N_GX = 4
N_GY = 8


def plant(entries, rng, least, largest):
    shape = entries.shape
    spot = [jax.random.randint(jax.random.fold_in(rng, axis), (), 0, shape[axis]) for axis in range(len(shape))]
    entries = entries.at[tuple(spot)].set(least)
    longest = shape.index(max(shape))
    spot[longest] = (spot[longest] + 1) % shape[longest]
    return entries.at[tuple(spot)].set(largest)


def levels(own_key, dims, split, smallest, high):
    def one(dim, blocks):
        heights = jax.random.uniform(jax.random.fold_in(jax.random.fold_in(own_key, 6), dim), (blocks,), jnp.float32, smallest / len(split), high / len(split))
        return jnp.repeat(jnp.exp(heights), dims[dim] // blocks).reshape((-1,) + (1,) * (len(dims) - dim - 1))

    gain = one(*split[0])
    for cut in split[1:]:
        gain = gain * one(*cut)
    return gain


def deal_out(own_key, own, number, rows, count, top, reach, skew):
    sequence = jax.random.permutation(own_key, count)
    packed, usual = shares(count, rows * top, reach, skew, True), shares(count, rows * top, reach, skew, False)
    places = jnp.arange(count)

    def named(sizes, turn):
        used = int((sizes > 0).sum())
        fixed = max(1, used // 4)
        passed = fixed + (places - fixed + turn * (used - fixed)) % max(1, count - fixed)
        return jnp.zeros((count,), jnp.int32).at[sequence[jnp.where(places < fixed, places, passed)]].set(jnp.asarray(sizes, jnp.int32))

    sizes = jnp.where(number % 4 == 0, named(packed, number // 4), named(usual, number - number // 4 - 1))
    mixed = jax.random.permutation(jax.random.fold_in(own, 3), count)
    source_of, sink = mixed[0:count // 2 * 2:2], mixed[1:count // 2 * 2:2]
    slack = jnp.minimum(sizes[source_of] - 1, reach - sizes[sink]) // 2
    slack = jnp.where((source_of == sequence[0]) | (sink == sequence[0]) | (sizes[sink] == 0), 0, jnp.maximum(slack, 0))
    passed = jax.random.randint(jax.random.fold_in(own, 4), (count // 2,), 0, 1 << 20) % (slack + 1)
    sizes = sizes.at[source_of].add(-passed).at[sink].add(passed)
    labels = jnp.searchsorted(jnp.cumsum(sizes), jnp.arange(rows * top), side="right").astype(jnp.int32)
    listing = labels.reshape(top, rows).T
    listing = listing[jax.random.permutation(jax.random.fold_in(own, 1), rows)]
    turn = jax.random.randint(jax.random.fold_in(own, 2), (rows, 1), 0, top)
    return jnp.take_along_axis(listing, (jnp.arange(top)[None, :] + turn) % top, axis=1)


def shares(amount, total, bound, skew, full):
    loads = [(1 << 20) // math.isqrt(grade ** skew) + 1 for grade in range(1, amount + 1)]
    largest = bound if full else min(bound, max(-(-total // amount), total * loads[0] // sum(loads)))
    least = 1 if total - largest >= amount - 1 else 0
    counts, spare = [largest] + [least] * (amount - 1), total - largest - least * (amount - 1)
    while spare > 0:
        movable = [i for i in range(1, amount) if counts[i] < largest] or [i for i in range(1, amount) if counts[i] < bound]
        whole, left = sum([loads[i] for i in movable]), spare
        for i in movable:
            addition = min(bound - counts[i], max(1, left * loads[i] // whole), spare)
            counts[i] = counts[i] + addition
            spare = spare - addition
    return np.array(counts)


def centred(stream_key, dims, deviation, bound, split=(), kind=jnp.bfloat16):
    result = jax.random.normal(stream_key, dims, jnp.float32) * deviation
    if len(split) > 0:
        result = levels(stream_key, dims, split, -0.22, 0.18) * result
    return jnp.clip(result, min=-bound, max=bound).astype(kind)


def setup_inputs(seed: int = 0) -> dict:
    splits = jax.random.split(jax.random.key(seed), 11)
    displacement = centred(splits[0], (2, 3, LAYERS, NX, NY), 0.1, 0.6, ((3, 4), (4, 8)), jnp.float32)
    velocity = centred(splits[1], (2, 3, LAYERS, NX, NY), 0.5, 3.0, ((3, 4), (4, 8)), jnp.float32)
    modulus = jnp.clip(jnp.exp(math.log(2.0) - 1.3862944 * jax.random.uniform(splits[2], (2, LAYERS, NX, NY), jnp.float32) ** levels(splits[2], (2, LAYERS, NX, NY), ((2, 4), (3, 8)), -0.2, 0.2)), 0.5, 2.0)
    density = jnp.clip(jnp.exp(math.log(4.0) - 1.3862944 * jax.random.uniform(splits[3], (2, LAYERS, NX, NY), jnp.float32) ** levels(splits[3], (2, LAYERS, NX, NY), ((2, 4), (3, 8)), -0.2, 0.2)), 1.0, 4.0)
    clearance = jnp.clip(jax.random.uniform(splits[4], (NX, NY), jnp.float32, -0.3, 0.3) * levels(splits[4], (NX, NY), ((0, 4), (1, 8)), -0.4, 0.0), -0.3, 0.3)
    mortar_coupling = centred(splits[5], (TILE, TILE), TILE ** -0.5, 0.5, (), jnp.float32)
    pair_owner_keys = jax.random.split(jax.random.fold_in(splits[6], 1), N_GX * (N_GY * PAIRS) // PAIRS)
    pair_owner_turns = jax.random.permutation(jax.random.fold_in(splits[6], 3), N_GX * (N_GY * PAIRS) // PAIRS)
    pair_owner = jax.vmap(lambda own, number: deal_out(jax.random.fold_in(splits[6], 2), own, number, PAIRS, N_GY, 1, CAP, 2))(pair_owner_keys, pair_owner_turns).reshape((N_GX, N_GY * PAIRS, 1))
    pair_row = plant(jax.random.randint(splits[7], (N_GX, N_GY * PAIRS, 1), 0, CX), jax.random.fold_in(splits[7], 1), 0, CX - 1).astype(jnp.int32)
    pair_offset = plant(jax.random.randint(splits[8], (N_GX, N_GY * PAIRS, 1), 0, TILE), jax.random.fold_in(splits[8], 1), 0, TILE - 1).astype(jnp.int32)
    pair_active = plant((jax.random.randint(splits[9], (N_GX, N_GY * PAIRS, 1), 0, 4) < 3).astype(jnp.int32), jax.random.fold_in(splits[9], 1), 0, 1)
    return {"displacement": displacement, "velocity": velocity, "modulus": modulus, "density": density, "clearance": clearance, "mortar_coupling": mortar_coupling, "pair_owner": pair_owner, "pair_row": pair_row, "pair_offset": pair_offset, "pair_active": pair_active}


time_step = 0.2
penalty_stiffness = 4.0


def internal_force(padded_disp, padded_mod, layers, xcount, ycount):
    centre_disp = padded_disp[:, :, 1:1 + layers, 1:1 + xcount, 1:1 + ycount]
    centre_mod = padded_mod[:, 1:1 + layers, 1:1 + xcount, 1:1 + ycount]
    stencil_sum = jnp.zeros_like(centre_disp)
    for depth_step in (-1, 0, 1):
        for row_step in (-1, 0, 1):
            for col_step in (-1, 0, 1):
                nonzero = abs(depth_step) + abs(row_step) + abs(col_step)
                if nonzero == 0:
                    continue
                weight_value = 0.5 ** (nonzero - 1)
                near_mod = padded_mod[:, 1 + depth_step:1 + depth_step + layers, 1 + row_step:1 + row_step + xcount, 1 + col_step:1 + col_step + ycount]
                near_disp = padded_disp[:, :, 1 + depth_step:1 + depth_step + layers, 1 + row_step:1 + row_step + xcount, 1 + col_step:1 + col_step + ycount]
                coupling = weight_value * 2.0 * centre_mod * near_mod / (centre_mod + near_mod)
                stencil_sum = stencil_sum + coupling[:, None] * (near_disp - centre_disp)
    return stencil_sum


def reference(displacement, velocity, modulus, density, clearance, mortar_coupling, pair_owner, pair_row, pair_offset, pair_active):
    owners = pair_owner[..., 0].reshape(N_GX, N_GY, PAIRS).astype(jnp.int32)
    row_ids = pair_row[..., 0].reshape(N_GX, N_GY, PAIRS).astype(jnp.int32)
    offsets = pair_offset[..., 0].reshape(N_GX, N_GY, PAIRS).astype(jnp.int32)
    active_weight = pair_active[..., 0].reshape(N_GX, N_GY, PAIRS).astype(jnp.float32)
    gx_index = jnp.arange(N_GX, dtype=jnp.int32)[:, None, None]
    gy_index = jnp.arange(N_GY, dtype=jnp.int32)[None, :, None]
    slave_tile = (jnp.arange(PAIRS, dtype=jnp.int32) // INTERSECTIONS)[None, None, :]
    lane_ids = jnp.arange(TILE, dtype=jnp.int32)
    forward_index = (lane_ids[None, None, None, :] + offsets[..., None]) % TILE
    backward_index = (lane_ids[None, None, None, :] - offsets[..., None] + TILE) % TILE
    clear_tiles = clearance.reshape(N_GX, CX, N_GY, TILE)[gx_index, slave_tile, gy_index]
    padded_mod = jnp.pad(modulus, ((0, 0), (1, 1), (1, 1), (1, 1)))
    for step_count in range(STEPS):
        padded_disp = jnp.pad(displacement, ((0, 0), (0, 0), (1, 1), (1, 1), (1, 1)))
        net_force = internal_force(padded_disp, padded_mod, LAYERS, NX, NY)
        master_face = displacement[0, 2, 0].reshape(N_GX, CX, N_GY, TILE)
        slave_face = displacement[1, 2, 0].reshape(N_GX, CX, N_GY, TILE)
        master_rows = master_face[gx_index, row_ids, owners]
        shifted = jnp.take_along_axis(master_rows, forward_index, axis=3)
        projected = shifted + jnp.einsum("abpj,jk->abpk", shifted, mortar_coupling, precision=lax.Precision.HIGHEST)
        gap_width = clear_tiles + slave_face[gx_index, slave_tile, gy_index] - projected
        traction = penalty_stiffness * active_weight[..., None] * jnp.maximum(0.0, -gap_width)
        back_proj = traction + jnp.einsum("abpk,jk->abpj", traction, mortar_coupling, precision=lax.Precision.HIGHEST)
        master_part = jnp.take_along_axis(back_proj, backward_index, axis=3)
        master_force = jnp.zeros((N_GX, CX, N_GY, TILE), jnp.float32).at[gx_index, row_ids, owners].add(master_part)
        slave_force = jnp.zeros((N_GX, CX, N_GY, TILE), jnp.float32).at[gx_index, slave_tile, gy_index].add(traction)
        net_force = net_force.at[0, 2, 0].add(-master_force.reshape(NX, NY))
        net_force = net_force.at[1, 2, 0].add(slave_force.reshape(NX, NY))
        velocity = velocity + time_step * net_force / density[:, None]
        displacement = displacement + time_step * velocity
    return displacement, velocity
```

```python
import functools

import jax
import jax.numpy as jnp
from jax import lax
from jax.experimental import pallas as pl
from jax.experimental.pallas import tpu as pltpu
from jax.sharding import PartitionSpec as P

F32 = jnp.float32
BF16 = jnp.bfloat16
INTERSECTIONS = 2
STEPS = 2
time_step = 0.2
penalty_stiffness = 4.0

SUB = 8
LANES = 128
FLAT = [(0, 1, 0), (1, -1, 0), (1, 0, 0), (1, 1, 0)]
SIDE = [(dz, dx, 1) for dz in (-1, 0, 1) for dx in (-1, 0, 1)]
HALF = FLAT + SIDE
NSIDE = len(SIDE)
NHALF = len(HALF)
NCOEF = NHALF + NSIDE

VMEM = pl.BlockSpec(memory_space=pltpu.VMEM)
SMEM = pl.BlockSpec(memory_space=pltpu.SMEM)


def twice_weight(nonzero):
    return 2.0 * 0.5 ** (nonzero - 1)


def lane_ids(rows=SUB):
    return lax.broadcasted_iota(jnp.int32, (rows, LANES), 1)


def sub_ids(rows=SUB):
    return lax.broadcasted_iota(jnp.int32, (rows, LANES), 0)


def take_lanes(values, index):
    return jnp.take_along_axis(values, index, axis=1)


def call(kernel, out_shape, args, specs=None, scratch=(), limit=None, flops=0, name=None):
    nbytes = sum(a.size * 4 for a in args)
    return pl.pallas_call(
        kernel,
        out_shape=out_shape,
        in_specs=specs or [VMEM] * len(args),
        out_specs=jax.tree.map(lambda _: VMEM, out_shape),
        scratch_shapes=scratch,
        name=name,
        cost_estimate=pl.CostEstimate(flops=flops, bytes_accessed=nbytes, transcendentals=0),
        compiler_params=pltpu.CompilerParams(vmem_limit_bytes=limit),
    )(*args)


def sds(*shape):
    return jax.ShapeDtypeStruct(shape, F32)


def coupling_kernel(L, X, e_ref, c_ref, d_ref, ep, ey):
    rows, pad, nt = 2 * L * X, X + SUB, X // SUB
    zero = jnp.zeros((pad, LANES), F32)
    for s in (ep, ey):
        s[pl.ds(0, pad), :] = zero
        s[pl.ds(pad + rows, pad), :] = zero
    for j in range(NHALF):
        c_ref[j, pl.ds(0, pad), :] = zero
        c_ref[j, pl.ds(pad + rows, pad), :] = zero
    lane, sub = lane_ids(), sub_ids()

    def fill(i, _):
        for k in range(nt):
            r = pl.multiple_of(i * X, X) + k * SUB
            e = e_ref[pl.ds(r, SUB), :]
            ep[pl.ds(r + pad, SUB), :] = e
            ey[pl.ds(r + pad, SUB), :] = jnp.where(
                lane == LANES - 1, 0.0, pltpu.roll(e, LANES - 1, 1)
            )
        return 0

    lax.fori_loop(0, 2 * L, fill, 0)

    def block(i, _):
        layer = lax.rem(i, L)
        up = jnp.where(layer < L - 1, 1.0, 0.0).astype(F32)
        down = jnp.where(layer > 0, 1.0, 0.0).astype(F32)
        for k in range(nt):
            r = pl.multiple_of(i * X, X) + k * SUB + pad
            e = ep[pl.ds(r, SUB), :]
            for j, (dz, dx, dy) in enumerate(HALF):
                o = (ey if dy else ep)[pl.ds(r + dz * X + dx, SUB), :]
                c = (e * twice_weight(abs(dz) + abs(dx) + dy)) * o / (e + o)
                if dz == 1:
                    c = c * up
                if dz == -1:
                    c = c * down
                if dx == 1 and k == nt - 1:
                    c = jnp.where(sub == SUB - 1, 0.0, c)
                if dx == -1 and k == 0:
                    c = jnp.where(sub == 0, 0.0, c)
                c_ref[j, pl.ds(r, SUB), :] = c
                if dy:
                    c_ref[NSIDE + j, pl.ds(r, SUB), :] = pltpu.roll(c, 1, 1)
        return 0

    lax.fori_loop(0, 2 * L, block, 0)

    def total(i, _):
        for k in range(nt):
            r = pl.multiple_of(i * X, X) + k * SUB + pad
            own, back = None, None
            for j, (dz, dx, dy) in enumerate(HALF):
                f = c_ref[j, pl.ds(r, SUB), :]
                b = c_ref[j, pl.ds(r - dz * X - dx, SUB), :]
                own = f if own is None else own + f
                if dy:
                    back = b if back is None else back + b
                else:
                    own = own + b
            d_ref[pl.ds(r - pad, SUB), :] = own + pltpu.roll(back, 1, 1)
        return 0

    lax.fori_loop(0, 2 * L, total, 0)


def coupling(modulus, L, X):
    rows, pad = 2 * L * X, X + SUB
    return call(
        functools.partial(coupling_kernel, L, X),
        [sds(NCOEF, rows + 2 * pad, LANES), sds(rows, LANES)],
        [modulus],
        scratch=[pltpu.VMEM((rows + 2 * pad, LANES), F32)] * 2,
        limit=5 << 20,
        flops=200 * rows * LANES,
        name="coupling",
    )


def stencil_kernel(L, X, group, u_ref, c_ref, d_ref, f_ref, up):
    rows, pad, nt = 6 * L * X, X + SUB, X // SUB
    zero = jnp.zeros((pad, LANES), F32)
    up[pl.ds(0, pad), :] = zero
    up[pl.ds(pad + rows, pad), :] = zero

    def fill(i, _):
        for k in range(nt):
            r = pl.multiple_of(i * X, X) + k * SUB
            up[pl.ds(r + pad, SUB), :] = u_ref[pl.ds(r, SUB), :]
        return 0

    lax.fori_loop(0, 6 * L, fill, 0)

    def block(i, _):
        bc = i // (nt // group)
        first = lax.rem(i, nt // group) * group * SUB
        body = bc // 3
        for k in range(group):
            for layer in range(L):
                ru = pl.multiple_of(bc * L * X + layer * X + first, SUB) + k * SUB
                rc = pl.multiple_of(body * L * X + layer * X + first, SUB) + k * SUB + pad
                t = {
                    (dz, dx): up[pl.ds(ru + pad + dz * X + dx, SUB), :]
                    for dz in (-1, 0, 1)
                    for dx in (-1, 0, 1)
                }
                acc = -d_ref[pl.ds(rc - pad, SUB), :] * t[0, 0]
                ahead, behind = None, None
                for j, (dz, dx, dy) in enumerate(HALF):
                    back = c_ref[j, pl.ds(rc - dz * X - dx, SUB), :] * t[-dz, -dx]
                    near = c_ref[j + NSIDE * dy, pl.ds(rc, SUB), :] * t[dz, dx]
                    if dy:
                        ahead = near if ahead is None else ahead + near
                        behind = back if behind is None else behind + back
                    else:
                        acc = acc + near
                        acc = acc + back
                f_ref[pl.ds(ru, SUB), :] = (
                    acc + pltpu.roll(ahead, LANES - 1, 1) + pltpu.roll(behind, 1, 1)
                )
        return 0

    lax.fori_loop(0, 6 * (nt // group), block, 0)


def stencil(u, coef, diag, L, X):
    rows, pad = 6 * L * X, X + SUB
    return call(
        functools.partial(stencil_kernel, L, X, 4),
        sds(rows, LANES),
        [u, coef, diag],
        scratch=[pltpu.VMEM((rows + 2 * pad, LANES), F32)],
        limit=8 << 20,
        flops=60 * rows * LANES,
        name="stencil",
    )


def edge_index():
    return jnp.where(lane_ids() < LANES // 2, 0, LANES - 1)


def pack_kernel(L, X, u_ref, e_ref, xl_ref, xh_ref, y_ref, w_ref):
    nt = X // SUB
    for bc in range(8):
        src, base = (u_ref, bc * L * X) if bc < 6 else (e_ref, (bc - 6) * L * X)
        xl_ref[pl.ds(bc * L, L), :] = src[pl.ds(base, L, stride=X), :]
        xh_ref[pl.ds(bc * L, L), :] = src[pl.ds(base + X - 1, L, stride=X), :]
    index = edge_index()
    slot = lane_ids() % (LANES // 2)

    def tile(k, _):
        r = pl.multiple_of(k * SUB, SUB)
        w = jnp.zeros((SUB, LANES), F32)
        for f in range(8 * L):
            src, row = (u_ref, f) if f < 6 * L else (e_ref, f - 6 * L)
            v = src[pl.ds(row * X + r, SUB), :]
            w = jnp.where(slot == f, take_lanes(v, index), w)
        w_ref[pl.ds(r, SUB), :] = w
        return 0

    lax.fori_loop(0, nt, tile, 0)
    y_ref[...] = w_ref[...].T


def pack(u, e, L, X):
    return call(
        functools.partial(pack_kernel, L, X),
        [sds(8 * L, LANES), sds(8 * L, LANES), sds(LANES, LANES)],
        [u, e],
        scratch=[pltpu.VMEM((X, LANES), F32)],
        limit=1 << 20,
        flops=u.size,
        name="pack",
    )


def corner_kernel(n, y_ref, xl_ref, xh_ref, ml_ref, mh_ref):
    half = LANES // 2
    ml_ref[pl.ds(0, n), :] = y_ref[pl.ds(0, n), :]
    mh_ref[pl.ds(0, n), :] = y_ref[pl.ds(half, n), :]
    lane = lane_ids(n)
    low, high = xl_ref[pl.ds(0, n), :], xh_ref[pl.ds(0, n), :]
    ml_ref[pl.ds(n, n), :] = jnp.where(lane == 0, low, pltpu.roll(high, LANES - 1, 1))
    mh_ref[pl.ds(n, n), :] = jnp.where(lane == 0, pltpu.roll(low, 1, 1), high)


def corners(n, y, xl, xh):
    return call(
        functools.partial(corner_kernel, n),
        [sds(2 * n, LANES), sds(2 * n, LANES)],
        [y, xl, xh],
        limit=1 << 20,
        name="corners",
    )


def split(x):
    high = x.astype(BF16)
    return high, (x - high.astype(F32)).astype(BF16)


def dot(a, b, dims=((1,), (0,))):
    return lax.dot_general(a, b, (dims, ((), ())), preferred_element_type=F32)


def project(x, pair, dims):
    high, low = split(x)
    return x + (dot(high, pair[0], dims) + dot(high, pair[1], dims) + dot(low, pair[0], dims))


def update_kernel(
    L,
    X,
    NY,
    n,
    last,
    scal,
    idx,
    f_ref,
    v_ref,
    u_ref,
    rho_ref,
    face_ref,
    pairs_ref,
    m_ref,
    oxl,
    oxh,
    oy,
    rxl,
    rxh,
    ryl,
    ryh,
    exl,
    exh,
    ey,
    erxl,
    erxh,
    eryl,
    eryh,
    *rest,
):
    u1_ref, v1_ref = rest[:2]
    outs = () if last else rest[2:6]
    whole, grow, shifted_s, trac_s, back_s, ct_s, xc, yc, cm, w_s = rest[2 + len(outs) :]
    nt, half, ne = X // SUB, LANES // 2, 8 * L
    me = scal[0]
    lane, sub = lane_ids(), sub_ids()
    lane_t = lane_ids(X)

    mh, ml = split(m_ref[...])
    straight, flipped = ((1,), (0,)), ((1,), (1,))
    columns = pairs_ref[...].T
    my_chip, my_core = me // 2, me % 2
    for q in range(NY):
        chip = lax.rem(my_chip + NY // 2 - q // 2, NY // 2)
        core = my_core if q % 2 == 0 else 1 - my_core
        owner = chip * 2 + core
        whole[pl.ds(pl.multiple_of(owner * X, X), X), :] = face_ref[q, pl.ds(0, X), :]

    def gather(i, _):
        for k in range(SUB):
            p = i * SUB + k
            grow[pl.ds(p, 1), :] = whole[pl.ds(idx[p], 1), :]
        return 0

    lax.fori_loop(0, INTERSECTIONS * X // SUB, gather, 0)

    def column(f):
        return jnp.broadcast_to(columns[:, f : f + 1], (X, LANES))

    slave = None
    for e in range(INTERSECTIONS):
        off = column(2 + e).astype(jnp.int32)
        moved = take_lanes(grow[pl.ds(e * X, X), :], (lane_t + off) & (LANES - 1))
        gap = face_ref[0, pl.ds(X, X), :] - project(moved, (mh, ml), straight)
        t = column(4 + e) * (penalty_stiffness * jnp.maximum(0.0, -gap))
        slave = t if slave is None else slave + t
    cm[1] = slave

    fh, fl = split(face_ref[0, pl.ds(0, X), :])
    me_f = me.astype(F32)
    node = lax.broadcasted_iota(jnp.int32, (X, X), 0).astype(F32)
    master = jnp.zeros((X, LANES), F32)
    blocks = [(q, e) for q in range(NY) for e in range(INTERSECTIONS)]
    for s, (q, e) in enumerate(blocks):
        base = q * SUB
        hot = jnp.where(node == pairs_ref[base + e : base + e + 1, :], 1.0, 0.0).astype(BF16)
        rows = dot(hot, fh, ((0,), (0,))) + dot(hot, fl, ((0,), (0,)))
        off = column(base + 2 + e).astype(jnp.int32)
        shifted_s[pl.ds(s * X, X), :] = take_lanes(rows, (lane_t + off) & (LANES - 1))
    for s, (q, e) in enumerate(blocks):
        gap = face_ref[q, pl.ds(X, X), :] - project(
            shifted_s[pl.ds(s * X, X), :], (mh, ml), straight
        )
        trac_s[pl.ds(s * X, X), :] = penalty_stiffness * jnp.maximum(0.0, -gap)
    for s, (q, e) in enumerate(blocks):
        base = q * SUB
        back = project(trac_s[pl.ds(s * X, X), :], (mh, ml), flipped)
        off = column(base + 2 + e).astype(jnp.int32)
        back_s[pl.ds(s * X, X), :] = take_lanes(back, (lane_t - off) & (LANES - 1))
    for s, (q, e) in enumerate(blocks):
        base = q * SUB
        weight = jnp.where(
            pairs_ref[base + 6 + e : base + 7 + e, :] == me_f,
            pairs_ref[base + 4 + e : base + 5 + e, :],
            0.0,
        )
        hot = jnp.where(node == pairs_ref[base + e : base + e + 1, :], weight, 0.0).astype(BF16)
        bh, bl = split(back_s[pl.ds(s * X, X), :])
        master = master + (dot(hot, bh) + dot(hot, bl))
    cm[0] = -master

    ok = [scal[1 + s].astype(F32) for s in range(4)]

    def edge(own_e, own_u, near_e, near_u, corner_e, corner_u, put):
        near = {}
        for d in (-1, 0, 1):
            value_e, value_u = near_e, list(near_u)
            if d:
                value_e = pltpu.roll(near_e, (-d) % LANES, 1)
                value_u = [pltpu.roll(x, (-d) % LANES, 1) for x in near_u]
                at = lane == (0 if d < 0 else LANES - 1)
                if corner_e is None:
                    value_e = jnp.where(at, 0.0, value_e)
                else:
                    value_e = jnp.where(at, corner_e, value_e)
                    value_u = [jnp.where(at, c, x) for c, x in zip(corner_u, value_u)]
            near[d] = (value_e, value_u)
        sums = [None] * 3
        for dz in (-1, 0, 1):
            for d in (-1, 0, 1):
                o, us = near[d]
                if dz:
                    o = pltpu.roll(o, (-dz) % SUB, 0)
                    o = jnp.where(sub == (0 if dz < 0 else SUB - 1), 0.0, o)
                    us = [pltpu.roll(x, (-dz) % SUB, 0) for x in us]
                c = (own_e * twice_weight(1 + abs(dz) + abs(d))) * o / (own_e + o)
                for comp in range(3):
                    term = c * (us[comp] - own_u[comp])
                    sums[comp] = term if sums[comp] is None else sums[comp] + term
        for comp in range(3):
            put(comp, sums[comp])

    def rows(ref, k):
        return ref[pl.ds(k, L), :]

    yc[...] = jnp.zeros((LANES, LANES), F32)
    for b in range(2):
        ue = [(b * 3 + c) * L for c in range(3)]
        ee = (6 + b) * L
        for s, (own_x, got_x, own_xe, got_xe) in enumerate(
            ((oxl, rxl, exl, erxl), (oxh, rxh, exh, erxh))
        ):
            edge(
                rows(own_xe, ee),
                [rows(own_x, k) for k in ue],
                rows(got_xe, ee) * ok[s],
                [rows(got_x, k) for k in ue],
                None,
                None,
                lambda c, v, s=s, ue=ue: xc.__setitem__((s, pl.ds(ue[c], L), slice(None)), v),
            )
        for s, (got_y, got_ye) in enumerate(((ryl, eryl), (ryh, eryh))):
            corner_ok = jnp.where(lane == 0, ok[0], ok[1]) * ok[2 + s]
            edge(
                rows(ey, s * half + ee),
                [rows(oy, s * half + k) for k in ue],
                rows(got_ye, ee) * ok[2 + s],
                [rows(got_y, k) for k in ue],
                rows(got_ye, ne + ee) * corner_ok,
                [rows(got_y, n + k) for k in ue],
                lambda c, v, s=s, ue=ue: yc.__setitem__((pl.ds(s * half + ue[c], L), slice(None)), v),
            )
    ct_s[...] = yc[...].T

    if not last:
        w_s[...] = jnp.zeros((X, LANES), F32)
    index = edge_index()
    slot = lane % half

    def advance(i, _):
        b, layer = i // L, lax.rem(i, L)
        face = jnp.where(layer == 0, 1.0, 0.0).astype(F32)
        for k in range(nt):
            rr = pl.multiple_of(i * X, X) + k * SUB
            scale = time_step / rho_ref[pl.ds(rr, SUB), :]
            ct = ct_s[pl.ds(k * SUB, SUB), :]
            if not last:
                w = w_s[pl.ds(k * SUB, SUB), :]
            for c in range(3):
                f = (b * 3 + c) * L + layer
                r = pl.multiple_of(f * X, X) + k * SUB
                pick = jnp.where(
                    lane == 0, f, jnp.where(lane == LANES - 1, half + f, half - 1)
                )
                force = f_ref[pl.ds(r, SUB), :] + take_lanes(ct, pick)
                if k == 0:
                    force = force + jnp.where(sub == 0, xc[0, pl.ds(f, 1), :], 0.0)
                if k == nt - 1:
                    force = force + jnp.where(sub == SUB - 1, xc[1, pl.ds(f, 1), :], 0.0)
                if c == 2:
                    force = force + face * cm[b, pl.ds(k * SUB, SUB), :]
                vel = v_ref[pl.ds(r, SUB), :] + scale * force
                disp = u_ref[pl.ds(r, SUB), :] + time_step * vel
                v1_ref[pl.ds(r, SUB), :] = vel
                u1_ref[pl.ds(r, SUB), :] = disp
                if not last:
                    w = jnp.where(slot == f, take_lanes(disp, index), w)
            if not last:
                w_s[pl.ds(k * SUB, SUB), :] = w
        return 0

    lax.fori_loop(0, 2 * L, advance, 0)
    if not last:
        xl_out, xh_out, y_out, face_out = outs
        for bc in range(6):
            xl_out[pl.ds(bc * L, L), :] = u1_ref[pl.ds(bc * L * X, L, stride=X), :]
            xh_out[pl.ds(bc * L, L), :] = u1_ref[pl.ds(bc * L * X + X - 1, L, stride=X), :]
        y_out[...] = w_s[...].T
        face_out[pl.ds(0, X), :] = u1_ref[pl.ds(2 * L * X, X), :]
        face_out[pl.ds(X, X), :] = u1_ref[pl.ds(5 * L * X, X), :] + (
            face_ref[0, pl.ds(X, X), :] - u_ref[pl.ds(5 * L * X, X), :]
        )


def update(L, X, NY, n, last, *args):
    R, total = 6 * L * X, NY * INTERSECTIONS * X
    out = [sds(R, LANES), sds(R, LANES)]
    if not last:
        out += [sds(6 * L, LANES), sds(6 * L, LANES), sds(LANES, LANES), sds(2 * X, LANES)]
    vm = pltpu.VMEM
    return call(
        functools.partial(update_kernel, L, X, NY, n, last),
        out,
        args,
        specs=[SMEM, SMEM] + [VMEM] * (len(args) - 2),
        scratch=[
            vm((NY * X, LANES), F32),
            vm((INTERSECTIONS * X, LANES), F32),
            vm((total, LANES), F32),
            vm((total, LANES), F32),
            vm((total, LANES), F32),
            vm((X, LANES), F32),
            vm((2, 6 * L, LANES), F32),
            vm((LANES, LANES), F32),
            vm((2, X, LANES), F32),
            vm((X, LANES), F32),
        ],
        limit=(8 << 20) + 3 * total * LANES * 4,
        flops=20 * R * LANES,
        name="update",
    )


def turn(x, axis, by):
    count = lax.axis_size(axis)
    return lax.ppermute(x, axis, [(i, (i + by) % count) for i in range(count)])


def swap(x):
    return lax.ppermute(x, "gy", [(i, i ^ 1) for i in range(lax.axis_size("gy"))])


def everyone(x):
    count = lax.axis_size("gy")
    parts = [x] + [turn(x, "gy", 2 * k) for k in range(1, count // 2)]
    out = []
    for part in parts:
        out += [part, swap(part)]
    return jnp.stack(out)


def halos(n, xl, xh, y):
    rxl, rxh = turn(xh, "gx", 1), turn(xl, "gx", -1)
    ml, mh = corners(n, y, rxl, rxh)
    return rxl, rxh, turn(mh, "gy", 1), turn(ml, "gy", -1)


def body(
    displacement,
    velocity,
    modulus,
    density,
    clearance,
    mortar_coupling,
    pair_owner,
    pair_row,
    pair_offset,
    pair_active,
):
    L, X, Y = displacement.shape[2:]
    assert Y == LANES and L == SUB and X == LANES
    GX, NY = lax.axis_size("gx"), lax.axis_size("gy")
    gx, gy = lax.axis_index("gx"), lax.axis_index("gy")
    flags = [gy, gx > 0, gx < GX - 1, gy > 0, gy < NY - 1]
    scal = jnp.stack([jnp.asarray(f, jnp.int32) for f in flags])

    def lanes(a):
        return a.reshape(X, INTERSECTIONS).T

    own, row, off, act = (
        lanes(a) for a in (pair_owner, pair_row, pair_offset, pair_active)
    )
    idx = (own * X + row).reshape(-1)
    u, v = displacement.reshape(-1, Y), velocity.reshape(-1, Y)
    e, rho = modulus.reshape(-1, Y), density.reshape(-1, Y)
    info = jnp.concatenate([row, off, act, own]).astype(F32)
    message = jnp.concatenate(
        [displacement[0, 2, 0], clearance + displacement[1, 2, 0], info]
    )
    got = everyone(message)
    faces, pairs = got[:, : 2 * X], got[:, 2 * X :].reshape(-1, LANES)
    pairs = jnp.pad(pairs, ((0, LANES - pairs.shape[0]), (0, 0)))
    xl, xh, y = pack(u, e, L, X)
    edges = (xl, xh, y) + halos(8 * L, xl, xh, y)
    coef, diag = coupling(e, L, X)
    f = stencil(u, coef, diag, L, X)
    stiff = (edges[0], edges[1], edges[2]) + edges[3:]
    u, v, xl, xh, y, face = update(
        L, X, NY, 8 * L, False, scal, idx, f, v, u, rho, faces, pairs, mortar_coupling, *edges, *stiff
    )
    faces = everyone(face)
    edges = (xl, xh, y) + halos(6 * L, xl, xh, y)
    f = stencil(u, coef, diag, L, X)
    u, v = update(
        L, X, NY, 6 * L, True, scal, idx, f, v, u, rho, faces, pairs, mortar_coupling, *edges, *stiff
    )
    return u.reshape(displacement.shape), v.reshape(velocity.shape)


def solution(mesh):
    return jax.shard_map(
        body,
        mesh=mesh,
        in_specs=(
            P(None, None, None, "gx", "gy"),
            P(None, None, None, "gx", "gy"),
            P(None, None, "gx", "gy"),
            P(None, None, "gx", "gy"),
            P("gx", "gy"),
            P(),
            P("gx", "gy", None),
            P("gx", "gy", None),
            P("gx", "gy", None),
            P("gx", "gy", None),
        ),
        out_specs=(P(None, None, None, "gx", "gy"), P(None, None, None, "gx", "gy")),
        check_vma=False,
    )
```

```python
import functools

import jax
import jax.numpy as jnp
from jax import lax
from jax.experimental import pallas as pl
from jax.experimental.pallas import tpu as pltpu
from jax.sharding import PartitionSpec as P

F32 = jnp.float32
BF16 = jnp.bfloat16
INTERSECTIONS = 2
STEPS = 2
time_step = 0.2
penalty_stiffness = 4.0

SUB = 8
LANES = 128
FLAT = [(0, 1, 0), (1, -1, 0), (1, 0, 0), (1, 1, 0)]
SIDE = [(dz, dx, 1) for dz in (-1, 0, 1) for dx in (-1, 0, 1)]
HALF = FLAT + SIDE
NSIDE = len(SIDE)
NHALF = len(HALF)
NCOEF = NHALF + NSIDE

VMEM = pl.BlockSpec(memory_space=pltpu.VMEM)
SMEM = pl.BlockSpec(memory_space=pltpu.SMEM)


def twice_weight(nonzero):
    return 2.0 * 0.5 ** (nonzero - 1)


def lane_ids(rows=SUB):
    return lax.broadcasted_iota(jnp.int32, (rows, LANES), 1)


def sub_ids(rows=SUB):
    return lax.broadcasted_iota(jnp.int32, (rows, LANES), 0)


def take_lanes(values, index):
    return jnp.take_along_axis(values, index, axis=1)


def call(
    kernel, out_shape, args, specs=None, scratch=(), limit=None, flops=0, name=None, out_spec=VMEM
):
    nbytes = sum(a.size * 4 for a in args)
    return pl.pallas_call(
        kernel,
        out_shape=out_shape,
        in_specs=specs or [VMEM] * len(args),
        out_specs=jax.tree.map(lambda _: out_spec, out_shape),
        scratch_shapes=scratch,
        name=name,
        cost_estimate=pl.CostEstimate(flops=flops, bytes_accessed=nbytes, transcendentals=0),
        compiler_params=pltpu.CompilerParams(vmem_limit_bytes=limit),
    )(*args)


def sds(*shape):
    return jax.ShapeDtypeStruct(shape, F32)


def coupling_kernel(L, X, e_ref, c_ref, d_ref, ep, ey):
    rows, pad, nt = 2 * L * X, X + SUB, X // SUB
    zero = jnp.zeros((pad, LANES), F32)
    for s in (ep, ey):
        s[pl.ds(0, pad), :] = zero
        s[pl.ds(pad + rows, pad), :] = zero
    for j in range(NHALF):
        c_ref[j, pl.ds(0, pad), :] = zero
        c_ref[j, pl.ds(pad + rows, pad), :] = zero
    lane, sub = lane_ids(), sub_ids()

    def fill(i, _):
        for k in range(nt):
            r = pl.multiple_of(i * X, X) + k * SUB
            e = e_ref[pl.ds(r, SUB), :]
            ep[pl.ds(r + pad, SUB), :] = e
            ey[pl.ds(r + pad, SUB), :] = jnp.where(
                lane == LANES - 1, 0.0, pltpu.roll(e, LANES - 1, 1)
            )
        return 0

    lax.fori_loop(0, 2 * L, fill, 0)

    def block(i, _):
        layer = lax.rem(i, L)
        up = jnp.where(layer < L - 1, 1.0, 0.0).astype(F32)
        down = jnp.where(layer > 0, 1.0, 0.0).astype(F32)
        for k in range(nt):
            r = pl.multiple_of(i * X, X) + k * SUB + pad
            e = ep[pl.ds(r, SUB), :]
            for j, (dz, dx, dy) in enumerate(HALF):
                o = (ey if dy else ep)[pl.ds(r + dz * X + dx, SUB), :]
                c = (e * twice_weight(abs(dz) + abs(dx) + dy)) * o / (e + o)
                if dz == 1:
                    c = c * up
                if dz == -1:
                    c = c * down
                if dx == 1 and k == nt - 1:
                    c = jnp.where(sub == SUB - 1, 0.0, c)
                if dx == -1 and k == 0:
                    c = jnp.where(sub == 0, 0.0, c)
                c_ref[j, pl.ds(r, SUB), :] = c
                if dy:
                    c_ref[NSIDE + j, pl.ds(r, SUB), :] = pltpu.roll(c, 1, 1)
        return 0

    lax.fori_loop(0, 2 * L, block, 0)

    def total(i, _):
        for k in range(nt):
            r = pl.multiple_of(i * X, X) + k * SUB + pad
            own, back = None, None
            for j, (dz, dx, dy) in enumerate(HALF):
                f = c_ref[j, pl.ds(r, SUB), :]
                b = c_ref[j, pl.ds(r - dz * X - dx, SUB), :]
                own = f if own is None else own + f
                if dy:
                    back = b if back is None else back + b
                else:
                    own = own + b
            d_ref[pl.ds(r - pad, SUB), :] = own + pltpu.roll(back, 1, 1)
        return 0

    lax.fori_loop(0, 2 * L, total, 0)


def coupling(modulus, L, X):
    rows, pad = 2 * L * X, X + SUB
    return call(
        functools.partial(coupling_kernel, L, X),
        [sds(NCOEF, rows + 2 * pad, LANES), sds(rows, LANES)],
        [modulus],
        scratch=[pltpu.VMEM((rows + 2 * pad, LANES), F32)] * 2,
        limit=5 << 20,
        flops=200 * rows * LANES,
        name="coupling",
    )


def stencil_kernel(L, X, group, comps, padded, u_ref, c_ref, d_ref, *rest):
    pad, nt = X + SUB, X // SUB
    f_ref = rest[-1] if padded else rest[-2]
    if padded:
        up = u_ref
    else:
        up = rest[-1]
        zero = jnp.zeros((pad, LANES), F32)
        up[pl.ds(0, pad), :] = zero
        up[pl.ds(pad + 6 * L * X, pad), :] = zero

        def fill(i, _):
            for k in range(nt):
                r = pl.multiple_of(i * X, X) + k * SUB
                up[pl.ds(r + pad, SUB), :] = u_ref[pl.ds(r, SUB), :]
            return 0

        lax.fori_loop(0, 6 * L, fill, 0)
    count, lowest = len(comps), comps[0]

    def block(i, _):
        which = i // (nt // group)
        first = lax.rem(i, nt // group) * group * SUB
        body = which // count
        bc = body * 3 + lowest + lax.rem(which, count)
        for k in range(group):
            for layer in range(L):
                ru = pl.multiple_of(bc * L * X + layer * X + first, SUB) + k * SUB
                rf = pl.multiple_of(which * L * X + layer * X + first, SUB) + k * SUB
                rc = pl.multiple_of(body * L * X + layer * X + first, SUB) + k * SUB + pad
                t = {
                    (dz, dx): up[pl.ds(ru + pad + dz * X + dx, SUB), :]
                    for dz in (-1, 0, 1)
                    for dx in (-1, 0, 1)
                }
                acc = -d_ref[pl.ds(rc - pad, SUB), :] * t[0, 0]
                ahead, behind = None, None
                for j, (dz, dx, dy) in enumerate(HALF):
                    back = c_ref[j, pl.ds(rc - dz * X - dx, SUB), :] * t[-dz, -dx]
                    near = c_ref[j + NSIDE * dy, pl.ds(rc, SUB), :] * t[dz, dx]
                    if dy:
                        ahead = near if ahead is None else ahead + near
                        behind = back if behind is None else behind + back
                    else:
                        acc = acc + near
                        acc = acc + back
                f_ref[pl.ds(rf, SUB), :] = (
                    acc + pltpu.roll(ahead, LANES - 1, 1) + pltpu.roll(behind, 1, 1)
                )
        return 0

    lax.fori_loop(0, 2 * count * (nt // group), block, 0)


def stencil(u, coef, diag, L, X, comps, padded, after=()):
    pad = X + SUB
    rows = 2 * len(comps) * L * X
    return call(
        functools.partial(stencil_kernel, L, X, 4, comps, padded),
        sds(rows, LANES),
        [u, coef, diag, *after],
        specs=[VMEM] * 3 + [pl.BlockSpec(memory_space=pl.ANY)] * len(after),
        scratch=[] if padded else [pltpu.VMEM((6 * L * X + 2 * pad, LANES), F32)],
        limit=(1 << 20) if padded else (5 << 20),
        flops=60 * rows * LANES,
        name="stencil",
    )


def message_kernel(L, X, u_ref, gap_ref, own, row, off, act, out_ref, tile, sems):
    copies = [
        pltpu.make_async_copy(u_ref.at[pl.ds(2 * L * X, X)], out_ref.at[pl.ds(0, X)], sems.at[0]),
        pltpu.make_async_copy(u_ref.at[pl.ds(5 * L * X, X)], tile, sems.at[1]),
    ]
    for c in copies:
        c.start()
    lane = lane_ids()
    for k, ref in enumerate((row, off, act, own)):
        both = [
            jnp.broadcast_to(ref[:, pl.ds(h * LANES, LANES)].astype(F32), (SUB, LANES))
            for h in range(INTERSECTIONS)
        ]
        for e in range(INTERSECTIONS):
            index = (lane * INTERSECTIONS + e) & (LANES - 1)
            picked = [take_lanes(x, index) for x in both]
            value = jnp.where(lane < LANES // INTERSECTIONS, picked[0], picked[1])
            out_ref[pl.ds(2 * X + INTERSECTIONS * k + e, 1), :] = value[:1]
    for c in copies:
        c.wait()
    out_ref[pl.ds(X, X), :] = tile[...] + gap_ref[...]


def first_message(u, clearance, pairs, L, X):
    return call(
        functools.partial(message_kernel, L, X),
        sds(2 * X + 4 * INTERSECTIONS, LANES),
        [u, clearance, *pairs],
        specs=[pl.BlockSpec(memory_space=pl.ANY)] + [VMEM] * 5,
        scratch=[pltpu.VMEM((X, LANES), F32), pltpu.SemaphoreType.DMA((2,))],
        limit=1 << 20,
        name="message",
    )


def edge_index():
    return jnp.where(lane_ids() < LANES // 2, 0, LANES - 1)


def pack_kernel(L, X, u_ref, e_ref, xl_ref, xh_ref, y_ref, w_ref):
    nt = X // SUB
    for bc in range(8):
        src, base = (u_ref, bc * L * X) if bc < 6 else (e_ref, (bc - 6) * L * X)
        xl_ref[pl.ds(bc * L, L), :] = src[pl.ds(base, L, stride=X), :]
        xh_ref[pl.ds(bc * L, L), :] = src[pl.ds(base + X - 1, L, stride=X), :]
    index = edge_index()
    slot = lane_ids() % (LANES // 2)

    def tile(k, _):
        r = pl.multiple_of(k * SUB, SUB)
        w = jnp.zeros((SUB, LANES), F32)
        for f in range(8 * L):
            src, row = (u_ref, f) if f < 6 * L else (e_ref, f - 6 * L)
            v = src[pl.ds(row * X + r, SUB), :]
            w = jnp.where(slot == f, take_lanes(v, index), w)
        w_ref[pl.ds(r, SUB), :] = w
        return 0

    lax.fori_loop(0, nt, tile, 0)
    y_ref[...] = w_ref[...].T


def pack(u, e, L, X):
    return call(
        functools.partial(pack_kernel, L, X),
        [sds(8 * L, LANES), sds(8 * L, LANES), sds(LANES, LANES)],
        [u, e],
        scratch=[pltpu.VMEM((X, LANES), F32)],
        limit=1 << 20,
        flops=u.size,
        name="pack",
    )


def corner_kernel(n, y_ref, xl_ref, xh_ref, ml_ref, mh_ref):
    half = LANES // 2
    ml_ref[pl.ds(0, n), :] = y_ref[pl.ds(0, n), :]
    mh_ref[pl.ds(0, n), :] = y_ref[pl.ds(half, n), :]
    lane = lane_ids(n)
    low, high = xl_ref[pl.ds(0, n), :], xh_ref[pl.ds(0, n), :]
    ml_ref[pl.ds(n, n), :] = jnp.where(lane == 0, low, pltpu.roll(high, LANES - 1, 1))
    mh_ref[pl.ds(n, n), :] = jnp.where(lane == 0, pltpu.roll(low, 1, 1), high)


def corners(n, y, xl, xh):
    return call(
        functools.partial(corner_kernel, n),
        [sds(2 * n, LANES), sds(2 * n, LANES)],
        [y, xl, xh],
        limit=1 << 20,
        name="corners",
    )


def split(x):
    high = x.astype(BF16)
    return high, (x - high.astype(F32)).astype(BF16)


def dot(a, b, dims=((1,), (0,))):
    return lax.dot_general(a, b, (dims, ((), ())), preferred_element_type=F32)


def project(x, pair, dims):
    high, low = split(x)
    return x + (dot(high, pair[0], dims) + dot(high, pair[1], dims) + dot(low, pair[0], dims))


def update_kernel(
    L,
    X,
    NY,
    n,
    last,
    scal,
    own_s,
    row_s,
    v_ref,
    u_ref,
    rho_ref,
    m_ref,
    gap_ref,
    oxl,
    oxh,
    oy,
    rxl,
    rxh,
    ryl,
    ryh,
    exl,
    exh,
    ey,
    erxl,
    erxh,
    eryl,
    eryh,
    *rest,
):
    first, rest = rest[:NY], rest[NY:]
    later, rest = (rest[:NY], rest[NY:]) if last else (first, rest)
    forces, rest = (rest[:2], rest[2:]) if last else (rest[:1] * 2, rest[1:])
    u1_ref, v1_ref = rest[:2]
    outs = () if last else rest[2:6]
    if last:
        sinks, (u1_ref, v1_ref, sems) = rest[:2], rest[11:]
    whole, grow, work, pairs_ref, ct_s, xc, yc, cm, w_s = rest[2 + len(outs) : 11 + len(outs)]
    nt, half, ne = X // SUB, LANES // 2, 8 * L
    pad = X + SUB
    shift_in, shift_out = (pad, 0) if last else (0, pad)
    me = scal[0]
    lane, sub = lane_ids(), sub_ids()
    lane_t = lane_ids(X)

    mh, ml = split(m_ref[...])
    straight, flipped = ((1,), (0,)), ((1,), (1,))
    pairs_ref[...] = jnp.zeros((LANES, LANES), F32)
    for q in range(NY):
        pairs_ref[pl.ds(q * SUB, SUB), :] = first[q][pl.ds(2 * X, SUB), :]
    columns = pairs_ref[...].T
    my_chip, my_core = me // 2, me % 2
    for q in range(NY):
        chip = lax.rem(my_chip + NY // 2 - q // 2, NY // 2)
        core = my_core if q % 2 == 0 else 1 - my_core
        owner = chip * 2 + core
        whole[pl.ds(pl.multiple_of(owner * X, X), X), :] = later[q][pl.ds(0, X), :]

    def gather(i, _):
        for k in range(SUB):
            p = i * SUB + k
            at = own_s[0, p] * X + row_s[0, p]
            to = (k % INTERSECTIONS) * X + i * (SUB // INTERSECTIONS) + k // INTERSECTIONS
            grow[pl.ds(to, 1), :] = whole[pl.ds(at, 1), :]
        return 0

    lax.fori_loop(0, INTERSECTIONS * X // SUB, gather, 0)

    def column(f):
        return jnp.broadcast_to(columns[:, f : f + 1], (X, LANES))

    slave = None
    for e in range(INTERSECTIONS):
        off = column(2 + e).astype(jnp.int32)
        moved = take_lanes(grow[pl.ds(e * X, X), :], (lane_t + off) & (LANES - 1))
        gap = later[0][pl.ds(X, X), :] - project(moved, (mh, ml), straight)
        t = column(4 + e) * (penalty_stiffness * jnp.maximum(0.0, -gap))
        slave = t if slave is None else slave + t
    cm[1] = slave

    fh, fl = split(later[0][pl.ds(0, X), :])
    me_f = me.astype(F32)
    node = lax.broadcasted_iota(jnp.int32, (X, X), 0).astype(F32)
    master = jnp.zeros((X, LANES), F32)
    blocks = [(q, e) for q in range(NY) for e in range(INTERSECTIONS)]
    for s, (q, e) in enumerate(blocks):
        base = q * SUB
        hot = jnp.where(node == pairs_ref[base + e : base + e + 1, :], 1.0, 0.0).astype(BF16)
        rows = dot(hot, fh, ((0,), (0,))) + dot(hot, fl, ((0,), (0,)))
        off = column(base + 2 + e).astype(jnp.int32)
        work[pl.ds(s * X, X), :] = take_lanes(rows, (lane_t + off) & (LANES - 1))
    for s, (q, e) in enumerate(blocks):
        gap = later[q][pl.ds(X, X), :] - project(
            work[pl.ds(s * X, X), :], (mh, ml), straight
        )
        work[pl.ds(s * X, X), :] = penalty_stiffness * jnp.maximum(0.0, -gap)
    for s, (q, e) in enumerate(blocks):
        base = q * SUB
        back = project(work[pl.ds(s * X, X), :], (mh, ml), flipped)
        off = column(base + 2 + e).astype(jnp.int32)
        work[pl.ds(s * X, X), :] = take_lanes(back, (lane_t - off) & (LANES - 1))
    for s, (q, e) in enumerate(blocks):
        base = q * SUB
        weight = jnp.where(
            pairs_ref[base + 6 + e : base + 7 + e, :] == me_f,
            pairs_ref[base + 4 + e : base + 5 + e, :],
            0.0,
        )
        hot = jnp.where(node == pairs_ref[base + e : base + e + 1, :], weight, 0.0).astype(BF16)
        bh, bl = split(work[pl.ds(s * X, X), :])
        master = master + (dot(hot, bh) + dot(hot, bl))
    cm[0] = -master

    ok = [scal[1 + s].astype(F32) for s in range(4)]

    def edge(own_e, own_u, near_e, near_u, corner_e, corner_u, put):
        near = {}
        for d in (-1, 0, 1):
            value_e, value_u = near_e, list(near_u)
            if d:
                value_e = pltpu.roll(near_e, (-d) % LANES, 1)
                value_u = [pltpu.roll(x, (-d) % LANES, 1) for x in near_u]
                at = lane == (0 if d < 0 else LANES - 1)
                if corner_e is None:
                    value_e = jnp.where(at, 0.0, value_e)
                else:
                    value_e = jnp.where(at, corner_e, value_e)
                    value_u = [jnp.where(at, c, x) for c, x in zip(corner_u, value_u)]
            near[d] = (value_e, value_u)
        sums = [None] * 3
        for dz in (-1, 0, 1):
            for d in (-1, 0, 1):
                o, us = near[d]
                if dz:
                    o = pltpu.roll(o, (-dz) % SUB, 0)
                    o = jnp.where(sub == (0 if dz < 0 else SUB - 1), 0.0, o)
                    us = [pltpu.roll(x, (-dz) % SUB, 0) for x in us]
                c = (own_e * twice_weight(1 + abs(dz) + abs(d))) * o / (own_e + o)
                for comp in range(3):
                    term = c * (us[comp] - own_u[comp])
                    sums[comp] = term if sums[comp] is None else sums[comp] + term
        for comp in range(3):
            put(comp, sums[comp])

    def rows(ref, k):
        return ref[pl.ds(k, L), :]

    yc[...] = jnp.zeros((LANES, LANES), F32)
    for b in range(2):
        ue = [(b * 3 + c) * L for c in range(3)]
        ee = (6 + b) * L
        for s, (own_x, got_x, own_xe, got_xe) in enumerate(
            ((oxl, rxl, exl, erxl), (oxh, rxh, exh, erxh))
        ):
            edge(
                rows(own_xe, ee),
                [rows(own_x, k) for k in ue],
                rows(got_xe, ee) * ok[s],
                [rows(got_x, k) for k in ue],
                None,
                None,
                lambda c, v, s=s, ue=ue: xc.__setitem__((s, pl.ds(ue[c], L), slice(None)), v),
            )
        for s, (got_y, got_ye) in enumerate(((ryl, eryl), (ryh, eryh))):
            corner_ok = jnp.where(lane == 0, ok[0], ok[1]) * ok[2 + s]
            edge(
                rows(ey, s * half + ee),
                [rows(oy, s * half + k) for k in ue],
                rows(got_ye, ee) * ok[2 + s],
                [rows(got_y, k) for k in ue],
                rows(got_ye, ne + ee) * corner_ok,
                [rows(got_y, n + k) for k in ue],
                lambda c, v, s=s, ue=ue: yc.__setitem__((pl.ds(s * half + ue[c], L), slice(None)), v),
            )
    ct_s[...] = yc[...].T

    if not last:
        w_s[...] = jnp.zeros((X, LANES), F32)
    index = edge_index()
    slot = lane % half

    def advance(i, _):
        b, layer = i // L, lax.rem(i, L)
        face = jnp.where(layer == 0, 1.0, 0.0).astype(F32)
        for k in range(nt):
            rr = pl.multiple_of(i * X, X) + k * SUB
            scale = time_step / rho_ref[pl.ds(rr, SUB), :]
            ct = ct_s[pl.ds(k * SUB, SUB), :]
            if not last:
                w = w_s[pl.ds(k * SUB, SUB), :]
            for c in range(3):
                f = (b * 3 + c) * L + layer
                r = pl.multiple_of(f * X, X) + k * SUB
                pick = jnp.where(
                    lane == 0, f, jnp.where(lane == LANES - 1, half + f, half - 1)
                )
                if last:
                    fr = pl.multiple_of(((b * 2 + c) if c < 2 else b) * L * X + layer * X, X)
                    base_force = forces[0 if c < 2 else 1][pl.ds(fr + k * SUB, SUB), :]
                else:
                    base_force = forces[0][pl.ds(r, SUB), :]
                force = base_force + take_lanes(ct, pick)
                if k == 0:
                    force = force + jnp.where(sub == 0, xc[0, pl.ds(f, 1), :], 0.0)
                if k == nt - 1:
                    force = force + jnp.where(sub == SUB - 1, xc[1, pl.ds(f, 1), :], 0.0)
                if c == 2:
                    force = force + face * cm[b, pl.ds(k * SUB, SUB), :]
                vel = v_ref[pl.ds(r, SUB), :] + scale * force
                disp = u_ref[pl.ds(r + shift_in, SUB), :] + time_step * vel
                v1_ref[pl.ds(r, SUB), :] = vel
                u1_ref[pl.ds(r + shift_out, SUB), :] = disp
                if not last:
                    w = jnp.where(slot == f, take_lanes(disp, index), w)
            if not last:
                w_s[pl.ds(k * SUB, SUB), :] = w
        if last:
            for c in range(3):
                at = pl.ds(pl.multiple_of(((b * 3 + c) * L + layer) * X, X), X)
                for s, ref in enumerate((u1_ref, v1_ref)):
                    pltpu.make_async_copy(ref.at[at], sinks[s].at[at], sems.at[s]).start()
        return 0

    lax.fori_loop(0, 2 * L, advance, 0)
    if last:
        for s, ref in enumerate((u1_ref, v1_ref)):
            pltpu.make_async_copy(ref, sinks[s], sems.at[s]).wait()
    if not last:
        xl_out, xh_out, y_out, face_out = outs
        zero = jnp.zeros((pad, LANES), F32)
        u1_ref[pl.ds(0, pad), :] = zero
        u1_ref[pl.ds(pad + 6 * L * X, pad), :] = zero
        for bc in range(6):
            at = pad + bc * L * X
            xl_out[pl.ds(bc * L, L), :] = u1_ref[pl.ds(at, L, stride=X), :]
            xh_out[pl.ds(bc * L, L), :] = u1_ref[pl.ds(at + X - 1, L, stride=X), :]
        y_out[...] = w_s[...].T
        face_out[pl.ds(0, X), :] = u1_ref[pl.ds(pad + 2 * L * X, X), :]
        face_out[pl.ds(X, X), :] = u1_ref[pl.ds(pad + 5 * L * X, X), :] + gap_ref[...]


def update(L, X, NY, n, last, *args):
    R, total = 6 * L * X, NY * INTERSECTIONS * X
    grown = R if last else R + 2 * (X + SUB)
    out = [sds(grown, LANES), sds(R, LANES)]
    if not last:
        out += [sds(6 * L, LANES), sds(6 * L, LANES), sds(LANES, LANES), sds(2 * X, LANES)]
    vm = pltpu.VMEM
    return call(
        functools.partial(update_kernel, L, X, NY, n, last),
        out,
        args,
        specs=[SMEM] * 3 + [VMEM] * (len(args) - 3),
        scratch=[
            vm((NY * X, LANES), F32),
            vm((INTERSECTIONS * X, LANES), F32),
            vm((total, LANES), F32),
            vm((LANES, LANES), F32),
            vm((X, LANES), F32),
            vm((2, 6 * L, LANES), F32),
            vm((LANES, LANES), F32),
            vm((2, X, LANES), F32),
            vm((X, LANES), F32),
        ]
        + ([vm((R, LANES), F32)] * 2 + [pltpu.SemaphoreType.DMA((2,))] if last else []),
        limit=(3 << 20) + 2 * total * LANES * 4 * max(1, NY // 8) + (2 * R * LANES * 4 if last else 0),
        out_spec=pl.BlockSpec(memory_space=pl.ANY) if last else VMEM,
        flops=20 * R * LANES,
        name="update",
    )


def turn(x, axis, by):
    count = lax.axis_size(axis)
    return lax.ppermute(x, axis, [(i, (i + by) % count) for i in range(count)])


def swap(x):
    return lax.ppermute(x, "gy", [(i, i ^ 1) for i in range(lax.axis_size("gy"))])


def far(x):
    return [x] + [turn(x, "gy", 2 * k) for k in range(1, lax.axis_size("gy") // 2)]


def both(parts):
    return [p for part in parts for p in (part, swap(part))]


def body(
    displacement,
    velocity,
    modulus,
    density,
    clearance,
    mortar_coupling,
    pair_owner,
    pair_row,
    pair_offset,
    pair_active,
):
    L, X, Y = displacement.shape[2:]
    assert Y == LANES and L == SUB and X == LANES
    GX, NY = lax.axis_size("gx"), lax.axis_size("gy")
    gx, gy = lax.axis_index("gx"), lax.axis_index("gy")
    flags = [gy, gx > 0, gx < GX - 1, gy > 0, gy < NY - 1]
    scal = jnp.stack([jnp.asarray(f, jnp.int32) for f in flags])

    u, v = displacement.reshape(-1, Y), velocity.reshape(-1, Y)
    e, rho = modulus.reshape(-1, Y), density.reshape(-1, Y)
    own, row, off, act = (
        a.transpose(0, 2, 1).reshape(1, -1)
        for a in (pair_owner, pair_row, pair_offset, pair_active)
    )
    parts = far(first_message(u, clearance, (own, row, off, act), L, X))
    xl, xh, y = pack(u, e, L, X)
    rxl, rxh = turn(xh, "gx", 1), turn(xl, "gx", -1)
    coef, diag = coupling(e, L, X)
    diag, rxl, rxh, *parts = lax.optimization_barrier((diag, rxl, rxh, *parts))
    ml, mh = corners(8 * L, y, rxl, rxh)
    f = stencil(u, coef, diag, L, X, (0, 1, 2), False, (ml, *parts[1:]))
    stiff = (xl, xh, y, rxl, rxh, turn(mh, "gy", 1), turn(ml, "gy", -1))
    messages = both(parts)
    fixed = (scal, own, row)
    u, v, xl, xh, y, face = update(
        L, X, NY, 8 * L, False, *fixed, v, u, rho, mortar_coupling, clearance, *stiff, *stiff, *messages, f
    )
    parts = far(face)
    rxl, rxh = turn(xh, "gx", 1), turn(xl, "gx", -1)
    f = stencil(u, coef, diag, L, X, (0, 1), True)
    f, rxl, rxh, *parts = lax.optimization_barrier((f, rxl, rxh, *parts))
    ml, mh = corners(6 * L, y, rxl, rxh)
    g = stencil(u, coef, diag, L, X, (2,), True, (ml, f, *parts[1:]))
    edges = (xl, xh, y, rxl, rxh, turn(mh, "gy", 1), turn(ml, "gy", -1))
    u, v = update(
        L, X, NY, 6 * L, True, *fixed, v, u, rho, mortar_coupling, clearance, *edges, *stiff,
        *messages, *both(parts), f, g
    )
    return u.reshape(displacement.shape), v.reshape(velocity.shape)


def solution(mesh):
    return jax.shard_map(
        body,
        mesh=mesh,
        in_specs=(
            P(None, None, None, "gx", "gy"),
            P(None, None, None, "gx", "gy"),
            P(None, None, "gx", "gy"),
            P(None, None, "gx", "gy"),
            P("gx", "gy"),
            P(),
            P("gx", "gy", None),
            P("gx", "gy", None),
            P("gx", "gy", None),
            P("gx", "gy", None),
        ),
        out_specs=(P(None, None, None, "gx", "gy"), P(None, None, None, "gx", "gy")),
        check_vma=False,
    )
```

```python
import functools

import jax
import jax.numpy as jnp
from jax import lax
from jax.experimental import pallas as pl
from jax.experimental.pallas import tpu as pltpu
from jax.sharding import PartitionSpec as P

F32 = jnp.float32
BF16 = jnp.bfloat16
INTERSECTIONS = 2
STEPS = 2
time_step = 0.2
penalty_stiffness = 4.0

SUB = 8
LANES = 128
FLAT = [(0, 1, 0), (1, -1, 0), (1, 0, 0), (1, 1, 0)]
SIDE = [(dz, dx, 1) for dz in (-1, 0, 1) for dx in (-1, 0, 1)]
HALF = FLAT + SIDE
NSIDE = len(SIDE)
NHALF = len(HALF)
NCOEF = NHALF + NSIDE

VMEM = pl.BlockSpec(memory_space=pltpu.VMEM)
SMEM = pl.BlockSpec(memory_space=pltpu.SMEM)


def twice_weight(nonzero):
    return 2.0 * 0.5 ** (nonzero - 1)


def lane_ids(rows=SUB):
    return lax.broadcasted_iota(jnp.int32, (rows, LANES), 1)


def sub_ids(rows=SUB):
    return lax.broadcasted_iota(jnp.int32, (rows, LANES), 0)


def take_lanes(values, index):
    return jnp.take_along_axis(values, index, axis=1)


def call(
    kernel, out_shape, args, specs=None, scratch=(), limit=None, flops=0, name=None, out_spec=VMEM
):
    nbytes = sum(a.size * 4 for a in args)
    return pl.pallas_call(
        kernel,
        out_shape=out_shape,
        in_specs=specs or [VMEM] * len(args),
        out_specs=jax.tree.map(lambda _: out_spec, out_shape),
        scratch_shapes=scratch,
        name=name,
        cost_estimate=pl.CostEstimate(flops=flops, bytes_accessed=nbytes, transcendentals=0),
        compiler_params=pltpu.CompilerParams(vmem_limit_bytes=limit),
    )(*args)


def sds(*shape):
    return jax.ShapeDtypeStruct(shape, F32)


def coupling_kernel(L, X, e_ref, c_ref, d_ref, ep, ey):
    rows, pad, nt = 2 * L * X, X + SUB, X // SUB
    zero = jnp.zeros((pad, LANES), F32)
    for s in (ep, ey):
        s[pl.ds(0, pad), :] = zero
        s[pl.ds(pad + rows, pad), :] = zero
    for j in range(NHALF):
        c_ref[j, pl.ds(0, pad), :] = zero
        c_ref[j, pl.ds(pad + rows, pad), :] = zero
    lane, sub = lane_ids(), sub_ids()

    def fill(i, _):
        for k in range(nt):
            r = pl.multiple_of(i * X, X) + k * SUB
            e = e_ref[pl.ds(r, SUB), :]
            ep[pl.ds(r + pad, SUB), :] = e
            ey[pl.ds(r + pad, SUB), :] = jnp.where(
                lane == LANES - 1, 0.0, pltpu.roll(e, LANES - 1, 1)
            )
        return 0

    lax.fori_loop(0, 2 * L, fill, 0)

    def block(i, _):
        layer = lax.rem(i, L)
        up = jnp.where(layer < L - 1, 1.0, 0.0).astype(F32)
        down = jnp.where(layer > 0, 1.0, 0.0).astype(F32)
        for k in range(nt):
            r = pl.multiple_of(i * X, X) + k * SUB + pad
            e = ep[pl.ds(r, SUB), :]
            for j, (dz, dx, dy) in enumerate(HALF):
                o = (ey if dy else ep)[pl.ds(r + dz * X + dx, SUB), :]
                c = (e * twice_weight(abs(dz) + abs(dx) + dy)) * o / (e + o)
                if dz == 1:
                    c = c * up
                if dz == -1:
                    c = c * down
                if dx == 1 and k == nt - 1:
                    c = jnp.where(sub == SUB - 1, 0.0, c)
                if dx == -1 and k == 0:
                    c = jnp.where(sub == 0, 0.0, c)
                c_ref[j, pl.ds(r, SUB), :] = c
                if dy:
                    c_ref[NSIDE + j, pl.ds(r, SUB), :] = pltpu.roll(c, 1, 1)
        return 0

    lax.fori_loop(0, 2 * L, block, 0)

    def total(i, _):
        for k in range(nt):
            r = pl.multiple_of(i * X, X) + k * SUB + pad
            own, back = None, None
            for j, (dz, dx, dy) in enumerate(HALF):
                f = c_ref[j, pl.ds(r, SUB), :]
                b = c_ref[j, pl.ds(r - dz * X - dx, SUB), :]
                own = f if own is None else own + f
                if dy:
                    back = b if back is None else back + b
                else:
                    own = own + b
            d_ref[pl.ds(r - pad, SUB), :] = own + pltpu.roll(back, 1, 1)
        return 0

    lax.fori_loop(0, 2 * L, total, 0)


def coupling(modulus, L, X):
    rows, pad = 2 * L * X, X + SUB
    return call(
        functools.partial(coupling_kernel, L, X),
        [sds(NCOEF, rows + 2 * pad, LANES), sds(rows, LANES)],
        [modulus],
        scratch=[pltpu.VMEM((rows + 2 * pad, LANES), F32)] * 2,
        limit=5 << 20,
        flops=200 * rows * LANES,
        name="coupling",
    )


def stencil_kernel(L, X, group, comps, padded, u_ref, c_ref, d_ref, *rest):
    pad, nt = X + SUB, X // SUB
    f_ref = rest[-1] if padded else rest[-2]
    if padded:
        up = u_ref
    else:
        up = rest[-1]
        zero = jnp.zeros((pad, LANES), F32)
        up[pl.ds(0, pad), :] = zero
        up[pl.ds(pad + 6 * L * X, pad), :] = zero

        def fill(i, _):
            for k in range(nt):
                r = pl.multiple_of(i * X, X) + k * SUB
                up[pl.ds(r + pad, SUB), :] = u_ref[pl.ds(r, SUB), :]
            return 0

        lax.fori_loop(0, 6 * L, fill, 0)
    count, lowest = len(comps), comps[0]

    def block(i, _):
        which = i // (nt // group)
        first = lax.rem(i, nt // group) * group * SUB
        body = which // count
        bc = body * 3 + lowest + lax.rem(which, count)
        for k in range(group):
            for layer in range(L):
                ru = pl.multiple_of(bc * L * X + layer * X + first, SUB) + k * SUB
                rf = pl.multiple_of(which * L * X + layer * X + first, SUB) + k * SUB
                rc = pl.multiple_of(body * L * X + layer * X + first, SUB) + k * SUB + pad
                t = {
                    (dz, dx): up[pl.ds(ru + pad + dz * X + dx, SUB), :]
                    for dz in (-1, 0, 1)
                    for dx in (-1, 0, 1)
                }
                acc = -d_ref[pl.ds(rc - pad, SUB), :] * t[0, 0]
                ahead, behind = None, None
                for j, (dz, dx, dy) in enumerate(HALF):
                    back = c_ref[j, pl.ds(rc - dz * X - dx, SUB), :] * t[-dz, -dx]
                    near = c_ref[j + NSIDE * dy, pl.ds(rc, SUB), :] * t[dz, dx]
                    if dy:
                        ahead = near if ahead is None else ahead + near
                        behind = back if behind is None else behind + back
                    else:
                        acc = acc + near
                        acc = acc + back
                f_ref[pl.ds(rf, SUB), :] = (
                    acc + pltpu.roll(ahead, LANES - 1, 1) + pltpu.roll(behind, 1, 1)
                )
        return 0

    lax.fori_loop(0, 2 * count * (nt // group), block, 0)


def stencil(u, coef, diag, L, X, comps, padded, after=()):
    pad = X + SUB
    rows = 2 * len(comps) * L * X
    return call(
        functools.partial(stencil_kernel, L, X, 4, comps, padded),
        sds(rows, LANES),
        [u, coef, diag, *after],
        specs=[VMEM] * 3 + [pl.BlockSpec(memory_space=pl.ANY)] * len(after),
        scratch=[] if padded else [pltpu.VMEM((6 * L * X + 2 * pad, LANES), F32)],
        limit=(1 << 20) if padded else (5 << 20),
        flops=60 * rows * LANES,
        name="stencil",
    )


def message_kernel(L, X, u_ref, gap_ref, own, row, off, act, out_ref, tile, gap, words, sems):
    copies = [
        pltpu.make_async_copy(u_ref.at[pl.ds(2 * L * X, X)], out_ref.at[pl.ds(0, X)], sems.at[0]),
        pltpu.make_async_copy(u_ref.at[pl.ds(5 * L * X, X)], tile, sems.at[1]),
        pltpu.make_async_copy(gap_ref, gap, sems.at[2]),
    ]
    small = [
        pltpu.make_async_copy(ref, words.at[pl.ds(k, 1)], sems.at[3 + k])
        for k, ref in enumerate((row, off, act, own))
    ]
    for c in small + copies:
        c.start()
    for c in small:
        c.wait()
    lane = lane_ids()
    for k in range(4):
        halves = [
            jnp.broadcast_to(words[pl.ds(k, 1), pl.ds(h * LANES, LANES)].astype(F32), (SUB, LANES))
            for h in range(INTERSECTIONS)
        ]
        for e in range(INTERSECTIONS):
            index = (lane * INTERSECTIONS + e) & (LANES - 1)
            picked = [take_lanes(x, index) for x in halves]
            value = jnp.where(lane < LANES // INTERSECTIONS, picked[0], picked[1])
            out_ref[pl.ds(2 * X + INTERSECTIONS * k + e, 1), :] = value[:1]
    for c in copies:
        c.wait()
    out_ref[pl.ds(X, X), :] = tile[...] + gap[...]


def first_message(u, clearance, pairs, L, X):
    return call(
        functools.partial(message_kernel, L, X),
        sds(2 * X + 4 * INTERSECTIONS, LANES),
        [u, clearance, *pairs],
        specs=[pl.BlockSpec(memory_space=pl.ANY)] * 6,
        scratch=[
            pltpu.VMEM((X, LANES), F32),
            pltpu.VMEM((X, LANES), F32),
            pltpu.VMEM((4, INTERSECTIONS * X), jnp.int32),
            pltpu.SemaphoreType.DMA((7,)),
        ],
        limit=58 << 20,
        name="message",
    )


def edge_index():
    return jnp.where(lane_ids() < LANES // 2, 0, LANES - 1)


def pack_kernel(L, X, u_ref, e_ref, xl_ref, xh_ref, y_ref, w_ref):
    nt = X // SUB
    for bc in range(8):
        src, base = (u_ref, bc * L * X) if bc < 6 else (e_ref, (bc - 6) * L * X)
        xl_ref[pl.ds(bc * L, L), :] = src[pl.ds(base, L, stride=X), :]
        xh_ref[pl.ds(bc * L, L), :] = src[pl.ds(base + X - 1, L, stride=X), :]
    index = edge_index()
    slot = lane_ids() % (LANES // 2)

    def tile(k, _):
        r = pl.multiple_of(k * SUB, SUB)
        w = jnp.zeros((SUB, LANES), F32)
        for f in range(8 * L):
            src, row = (u_ref, f) if f < 6 * L else (e_ref, f - 6 * L)
            v = src[pl.ds(row * X + r, SUB), :]
            w = jnp.where(slot == f, take_lanes(v, index), w)
        w_ref[pl.ds(r, SUB), :] = w
        return 0

    lax.fori_loop(0, nt, tile, 0)
    y_ref[...] = w_ref[...].T


def pack(u, e, L, X):
    return call(
        functools.partial(pack_kernel, L, X),
        [sds(8 * L, LANES), sds(8 * L, LANES), sds(LANES, LANES)],
        [u, e],
        scratch=[pltpu.VMEM((X, LANES), F32)],
        limit=1 << 20,
        flops=u.size,
        name="pack",
    )


def corner_kernel(n, y_ref, xl_ref, xh_ref, ml_ref, mh_ref):
    half = LANES // 2
    ml_ref[pl.ds(0, n), :] = y_ref[pl.ds(0, n), :]
    mh_ref[pl.ds(0, n), :] = y_ref[pl.ds(half, n), :]
    lane = lane_ids(n)
    low, high = xl_ref[pl.ds(0, n), :], xh_ref[pl.ds(0, n), :]
    ml_ref[pl.ds(n, n), :] = jnp.where(lane == 0, low, pltpu.roll(high, LANES - 1, 1))
    mh_ref[pl.ds(n, n), :] = jnp.where(lane == 0, pltpu.roll(low, 1, 1), high)


def corners(n, y, xl, xh):
    return call(
        functools.partial(corner_kernel, n),
        [sds(2 * n, LANES), sds(2 * n, LANES)],
        [y, xl, xh],
        limit=1 << 20,
        name="corners",
    )


def split(x):
    high = x.astype(BF16)
    return high, (x - high.astype(F32)).astype(BF16)


def dot(a, b, dims=((1,), (0,))):
    return lax.dot_general(a, b, (dims, ((), ())), preferred_element_type=F32)


def project(x, pair, dims):
    high, low = split(x)
    return x + (dot(high, pair[0], dims) + dot(high, pair[1], dims) + dot(low, pair[0], dims))


def update_kernel(
    L,
    X,
    GX,
    NY,
    n,
    last,
    own_s,
    row_s,
    v_ref,
    u_ref,
    rho_ref,
    m_ref,
    gap_ref,
    oxl,
    oxh,
    oy,
    rxl,
    rxh,
    ryl,
    ryh,
    exl,
    exh,
    ey,
    erxl,
    erxh,
    eryl,
    eryh,
    *rest,
):
    first, rest = rest[:NY], rest[NY:]
    later, rest = (rest[:NY], rest[NY:]) if last else (first, rest)
    forces, rest = (rest[:2], rest[2:]) if last else (rest[:1] * 2, rest[1:])
    u1_ref, v1_ref = rest[:2]
    outs = () if last else rest[2:6]
    if last:
        sinks, (u1_ref, v1_ref, sems) = rest[:2], rest[11:]
    whole, grow, work, pairs_ref, ct_s, xc, yc, cm, w_s = rest[2 + len(outs) : 11 + len(outs)]
    nt, half, ne = X // SUB, LANES // 2, 8 * L
    pad = X + SUB
    shift_in, shift_out = (pad, 0) if last else (0, pad)
    gx, me = lax.axis_index("gx"), lax.axis_index("gy")
    lane, sub = lane_ids(), sub_ids()
    lane_t = lane_ids(X)

    mh, ml = split(m_ref[...])
    straight, flipped = ((1,), (0,)), ((1,), (1,))
    pairs_ref[...] = jnp.zeros((LANES, LANES), F32)
    for q in range(NY):
        pairs_ref[pl.ds(q * SUB, SUB), :] = first[q][pl.ds(2 * X, SUB), :]
    columns = pairs_ref[...].T
    my_chip, my_core = me // 2, me % 2
    for q in range(NY):
        chip = lax.rem(my_chip + NY // 2 - q // 2, NY // 2)
        core = my_core if q % 2 == 0 else 1 - my_core
        owner = chip * 2 + core
        whole[pl.ds(pl.multiple_of(owner * X, X), X), :] = later[q][pl.ds(0, X), :]

    def gather(i, _):
        for k in range(SUB):
            p = i * SUB + k
            at = own_s[0, p] * X + row_s[0, p]
            to = (k % INTERSECTIONS) * X + i * (SUB // INTERSECTIONS) + k // INTERSECTIONS
            grow[pl.ds(to, 1), :] = whole[pl.ds(at, 1), :]
        return 0

    lax.fori_loop(0, INTERSECTIONS * X // SUB, gather, 0)

    def column(f):
        return jnp.broadcast_to(columns[:, f : f + 1], (X, LANES))

    slave = None
    for e in range(INTERSECTIONS):
        off = column(2 + e).astype(jnp.int32)
        moved = take_lanes(grow[pl.ds(e * X, X), :], (lane_t + off) & (LANES - 1))
        gap = later[0][pl.ds(X, X), :] - project(moved, (mh, ml), straight)
        t = column(4 + e) * (penalty_stiffness * jnp.maximum(0.0, -gap))
        slave = t if slave is None else slave + t
    cm[1] = slave

    fh, fl = split(later[0][pl.ds(0, X), :])
    me_f = me.astype(F32)
    node = lax.broadcasted_iota(jnp.int32, (X, X), 0).astype(F32)
    master = jnp.zeros((X, LANES), F32)
    blocks = [(q, e) for q in range(NY) for e in range(INTERSECTIONS)]
    for s, (q, e) in enumerate(blocks):
        base = q * SUB
        hot = jnp.where(node == pairs_ref[base + e : base + e + 1, :], 1.0, 0.0).astype(BF16)
        rows = dot(hot, fh, ((0,), (0,))) + dot(hot, fl, ((0,), (0,)))
        off = column(base + 2 + e).astype(jnp.int32)
        work[pl.ds(s * X, X), :] = take_lanes(rows, (lane_t + off) & (LANES - 1))
    for s, (q, e) in enumerate(blocks):
        gap = later[q][pl.ds(X, X), :] - project(
            work[pl.ds(s * X, X), :], (mh, ml), straight
        )
        work[pl.ds(s * X, X), :] = penalty_stiffness * jnp.maximum(0.0, -gap)
    for s, (q, e) in enumerate(blocks):
        base = q * SUB
        back = project(work[pl.ds(s * X, X), :], (mh, ml), flipped)
        off = column(base + 2 + e).astype(jnp.int32)
        work[pl.ds(s * X, X), :] = take_lanes(back, (lane_t - off) & (LANES - 1))
    for s, (q, e) in enumerate(blocks):
        base = q * SUB
        weight = jnp.where(
            pairs_ref[base + 6 + e : base + 7 + e, :] == me_f,
            pairs_ref[base + 4 + e : base + 5 + e, :],
            0.0,
        )
        hot = jnp.where(node == pairs_ref[base + e : base + e + 1, :], weight, 0.0).astype(BF16)
        bh, bl = split(work[pl.ds(s * X, X), :])
        master = master + (dot(hot, bh) + dot(hot, bl))
    cm[0] = -master

    inside = (gx > 0, gx < GX - 1, me > 0, me < NY - 1)
    ok = [jnp.where(x, 1.0, 0.0).astype(F32) for x in inside]

    def edge(own_e, own_u, near_e, near_u, corner_e, corner_u, put):
        near = {}
        for d in (-1, 0, 1):
            value_e, value_u = near_e, list(near_u)
            if d:
                value_e = pltpu.roll(near_e, (-d) % LANES, 1)
                value_u = [pltpu.roll(x, (-d) % LANES, 1) for x in near_u]
                at = lane == (0 if d < 0 else LANES - 1)
                if corner_e is None:
                    value_e = jnp.where(at, 0.0, value_e)
                else:
                    value_e = jnp.where(at, corner_e, value_e)
                    value_u = [jnp.where(at, c, x) for c, x in zip(corner_u, value_u)]
            near[d] = (value_e, value_u)
        sums = [None] * 3
        for dz in (-1, 0, 1):
            for d in (-1, 0, 1):
                o, us = near[d]
                if dz:
                    o = pltpu.roll(o, (-dz) % SUB, 0)
                    o = jnp.where(sub == (0 if dz < 0 else SUB - 1), 0.0, o)
                    us = [pltpu.roll(x, (-dz) % SUB, 0) for x in us]
                c = (own_e * twice_weight(1 + abs(dz) + abs(d))) * o / (own_e + o)
                for comp in range(3):
                    term = c * (us[comp] - own_u[comp])
                    sums[comp] = term if sums[comp] is None else sums[comp] + term
        for comp in range(3):
            put(comp, sums[comp])

    def rows(ref, k):
        return ref[pl.ds(k, L), :]

    yc[...] = jnp.zeros((LANES, LANES), F32)
    for b in range(2):
        ue = [(b * 3 + c) * L for c in range(3)]
        ee = (6 + b) * L
        for s, (own_x, got_x, own_xe, got_xe) in enumerate(
            ((oxl, rxl, exl, erxl), (oxh, rxh, exh, erxh))
        ):
            edge(
                rows(own_xe, ee),
                [rows(own_x, k) for k in ue],
                rows(got_xe, ee) * ok[s],
                [rows(got_x, k) for k in ue],
                None,
                None,
                lambda c, v, s=s, ue=ue: xc.__setitem__((s, pl.ds(ue[c], L), slice(None)), v),
            )
        for s, (got_y, got_ye) in enumerate(((ryl, eryl), (ryh, eryh))):
            corner_ok = jnp.where(lane == 0, ok[0], ok[1]) * ok[2 + s]
            edge(
                rows(ey, s * half + ee),
                [rows(oy, s * half + k) for k in ue],
                rows(got_ye, ee) * ok[2 + s],
                [rows(got_y, k) for k in ue],
                rows(got_ye, ne + ee) * corner_ok,
                [rows(got_y, n + k) for k in ue],
                lambda c, v, s=s, ue=ue: yc.__setitem__((pl.ds(s * half + ue[c], L), slice(None)), v),
            )
    ct_s[...] = yc[...].T

    if not last:
        w_s[...] = jnp.zeros((X, LANES), F32)
    index = edge_index()
    slot = lane % half

    def advance(i, _):
        b, layer = i // L, lax.rem(i, L)
        face = jnp.where(layer == 0, 1.0, 0.0).astype(F32)
        for k in range(nt):
            rr = pl.multiple_of(i * X, X) + k * SUB
            scale = time_step / rho_ref[pl.ds(rr, SUB), :]
            ct = ct_s[pl.ds(k * SUB, SUB), :]
            if not last:
                w = w_s[pl.ds(k * SUB, SUB), :]
            for c in range(3):
                f = (b * 3 + c) * L + layer
                r = pl.multiple_of(f * X, X) + k * SUB
                pick = jnp.where(
                    lane == 0, f, jnp.where(lane == LANES - 1, half + f, half - 1)
                )
                if last:
                    fr = pl.multiple_of(((b * 2 + c) if c < 2 else b) * L * X + layer * X, X)
                    base_force = forces[0 if c < 2 else 1][pl.ds(fr + k * SUB, SUB), :]
                else:
                    base_force = forces[0][pl.ds(r, SUB), :]
                force = base_force + take_lanes(ct, pick)
                if k == 0:
                    force = force + jnp.where(sub == 0, xc[0, pl.ds(f, 1), :], 0.0)
                if k == nt - 1:
                    force = force + jnp.where(sub == SUB - 1, xc[1, pl.ds(f, 1), :], 0.0)
                if c == 2:
                    force = force + face * cm[b, pl.ds(k * SUB, SUB), :]
                vel = v_ref[pl.ds(r, SUB), :] + scale * force
                disp = u_ref[pl.ds(r + shift_in, SUB), :] + time_step * vel
                v1_ref[pl.ds(r, SUB), :] = vel
                u1_ref[pl.ds(r + shift_out, SUB), :] = disp
                if not last:
                    w = jnp.where(slot == f, take_lanes(disp, index), w)
            if not last:
                w_s[pl.ds(k * SUB, SUB), :] = w
        if last:
            for c in range(3):
                at = pl.ds(pl.multiple_of(((b * 3 + c) * L + layer) * X, X), X)
                for s, ref in enumerate((u1_ref, v1_ref)):
                    pltpu.make_async_copy(ref.at[at], sinks[s].at[at], sems.at[s]).start()
        return 0

    lax.fori_loop(0, 2 * L, advance, 0)
    if last:
        for s, ref in enumerate((u1_ref, v1_ref)):
            pltpu.make_async_copy(ref, sinks[s], sems.at[s]).wait()
    if not last:
        xl_out, xh_out, y_out, face_out = outs
        zero = jnp.zeros((pad, LANES), F32)
        u1_ref[pl.ds(0, pad), :] = zero
        u1_ref[pl.ds(pad + 6 * L * X, pad), :] = zero
        for bc in range(6):
            at = pad + bc * L * X
            xl_out[pl.ds(bc * L, L), :] = u1_ref[pl.ds(at, L, stride=X), :]
            xh_out[pl.ds(bc * L, L), :] = u1_ref[pl.ds(at + X - 1, L, stride=X), :]
        y_out[...] = w_s[...].T
        face_out[pl.ds(0, X), :] = u1_ref[pl.ds(pad + 2 * L * X, X), :]
        face_out[pl.ds(X, X), :] = u1_ref[pl.ds(pad + 5 * L * X, X), :] + gap_ref[...]


def update(L, X, GX, NY, n, last, *args):
    R, total = 6 * L * X, NY * INTERSECTIONS * X
    grown = R if last else R + 2 * (X + SUB)
    out = [sds(grown, LANES), sds(R, LANES)]
    if not last:
        out += [sds(6 * L, LANES), sds(6 * L, LANES), sds(LANES, LANES), sds(2 * X, LANES)]
    vm = pltpu.VMEM
    return call(
        functools.partial(update_kernel, L, X, GX, NY, n, last),
        out,
        args,
        specs=[SMEM] * 2 + [VMEM] * (len(args) - 2),
        scratch=[
            vm((NY * X, LANES), F32),
            vm((INTERSECTIONS * X, LANES), F32),
            vm((total, LANES), F32),
            vm((LANES, LANES), F32),
            vm((X, LANES), F32),
            vm((2, 6 * L, LANES), F32),
            vm((LANES, LANES), F32),
            vm((2, X, LANES), F32),
            vm((X, LANES), F32),
        ]
        + ([vm((R, LANES), F32)] * 2 + [pltpu.SemaphoreType.DMA((2,))] if last else []),
        limit=(3 << 20) + 2 * total * LANES * 4 * max(1, NY // 8) + (2 * R * LANES * 4 if last else 0),
        out_spec=pl.BlockSpec(memory_space=pl.ANY) if last else VMEM,
        flops=20 * R * LANES,
        name="update",
    )


def turn(x, axis, by):
    count = lax.axis_size(axis)
    return lax.ppermute(x, axis, [(i, (i + by) % count) for i in range(count)])


def swap(x):
    return lax.ppermute(x, "gy", [(i, i ^ 1) for i in range(lax.axis_size("gy"))])


def far(x):
    return [x] + [turn(x, "gy", 2 * k) for k in range(1, lax.axis_size("gy") // 2)]


def both(parts):
    return [p for part in parts for p in (part, swap(part))]


def body(
    displacement,
    velocity,
    modulus,
    density,
    clearance,
    mortar_coupling,
    pair_owner,
    pair_row,
    pair_offset,
    pair_active,
):
    L, X, Y = displacement.shape[2:]
    assert Y == LANES and L == SUB and X == LANES
    GX, NY = lax.axis_size("gx"), lax.axis_size("gy")

    u, v = displacement.reshape(-1, Y), velocity.reshape(-1, Y)
    e, rho = modulus.reshape(-1, Y), density.reshape(-1, Y)
    own, row, off, act = (
        a.transpose(0, 2, 1).reshape(1, -1)
        for a in (pair_owner, pair_row, pair_offset, pair_active)
    )
    parts = far(first_message(u, clearance, (own, row, off, act), L, X))
    xl, xh, y = pack(u, e, L, X)
    rxl, rxh = turn(xh, "gx", 1), turn(xl, "gx", -1)
    coef, diag = coupling(e, L, X)
    diag, rxl, rxh, *parts = lax.optimization_barrier((diag, rxl, rxh, *parts))
    ml, mh = corners(8 * L, y, rxl, rxh)
    f = stencil(u, coef, diag, L, X, (0, 1, 2), False, (ml, *parts[1:]))
    stiff = (xl, xh, y, rxl, rxh, turn(mh, "gy", 1), turn(ml, "gy", -1))
    messages = both(parts)
    fixed = (own, row)
    u, v, xl, xh, y, face = update(
        L, X, GX, NY, 8 * L, False, *fixed, v, u, rho, mortar_coupling, clearance, *stiff, *stiff, *messages, f
    )
    parts = far(face)
    rxl, rxh = turn(xh, "gx", 1), turn(xl, "gx", -1)
    f = stencil(u, coef, diag, L, X, (0, 1), True)
    f, rxl, rxh, *parts = lax.optimization_barrier((f, rxl, rxh, *parts))
    ml, mh = corners(6 * L, y, rxl, rxh)
    g = stencil(u, coef, diag, L, X, (2,), True, (ml, f, *parts[1:]))
    edges = (xl, xh, y, rxl, rxh, turn(mh, "gy", 1), turn(ml, "gy", -1))
    u, v = update(
        L, X, GX, NY, 6 * L, True, *fixed, v, u, rho, mortar_coupling, clearance, *edges, *stiff,
        *messages, *both(parts), f, g
    )
    return u.reshape(displacement.shape), v.reshape(velocity.shape)


def solution(mesh):
    return jax.shard_map(
        body,
        mesh=mesh,
        in_specs=(
            P(None, None, None, "gx", "gy"),
            P(None, None, None, "gx", "gy"),
            P(None, None, "gx", "gy"),
            P(None, None, "gx", "gy"),
            P("gx", "gy"),
            P(),
            P("gx", "gy", None),
            P("gx", "gy", None),
            P("gx", "gy", None),
            P("gx", "gy", None),
        ),
        out_specs=(P(None, None, None, "gx", "gy"), P(None, None, None, "gx", "gy")),
        check_vma=False,
    )
```

```python
import functools

import jax
import jax.numpy as jnp
from jax import lax
from jax.experimental import pallas as pl
from jax.experimental.pallas import tpu as pltpu
from jax.sharding import PartitionSpec as P

F32 = jnp.float32
BF16 = jnp.bfloat16
INTERSECTIONS = 2
STEPS = 2
time_step = 0.2
penalty_stiffness = 4.0

SUB = 8
LANES = 128
FLAT = [(0, 1, 0), (1, -1, 0), (1, 0, 0), (1, 1, 0)]
SIDE = [(dz, dx, 1) for dz in (-1, 0, 1) for dx in (-1, 0, 1)]
HALF = FLAT + SIDE
NSIDE = len(SIDE)
NHALF = len(HALF)
NCOEF = NHALF + NSIDE

VMEM = pl.BlockSpec(memory_space=pltpu.VMEM)
SMEM = pl.BlockSpec(memory_space=pltpu.SMEM)


def twice_weight(nonzero):
    return 2.0 * 0.5 ** (nonzero - 1)


def lane_ids(rows=SUB):
    return lax.broadcasted_iota(jnp.int32, (rows, LANES), 1)


def sub_ids(rows=SUB):
    return lax.broadcasted_iota(jnp.int32, (rows, LANES), 0)


def take_lanes(values, index):
    return jnp.take_along_axis(values, index, axis=1)


def call(
    kernel, out_shape, args, specs=None, scratch=(), limit=None, flops=0, name=None, out_spec=VMEM
):
    nbytes = sum(a.size * 4 for a in args)
    return pl.pallas_call(
        kernel,
        out_shape=out_shape,
        in_specs=specs or [VMEM] * len(args),
        out_specs=jax.tree.map(lambda _: out_spec, out_shape),
        scratch_shapes=scratch,
        name=name,
        cost_estimate=pl.CostEstimate(flops=flops, bytes_accessed=nbytes, transcendentals=0),
        compiler_params=pltpu.CompilerParams(vmem_limit_bytes=limit),
    )(*args)


def sds(*shape):
    return jax.ShapeDtypeStruct(shape, F32)


def coupling_kernel(L, X, e_ref, c_ref, d_ref, ep, ey):
    rows, pad, nt = 2 * L * X, X + SUB, X // SUB
    zero = jnp.zeros((pad, LANES), F32)
    for s in (ep, ey):
        s[pl.ds(0, pad), :] = zero
        s[pl.ds(pad + rows, pad), :] = zero
    for j in range(NHALF):
        c_ref[j, pl.ds(0, pad), :] = zero
        c_ref[j, pl.ds(pad + rows, pad), :] = zero
    lane, sub = lane_ids(), sub_ids()

    def fill(i, _):
        for k in range(nt):
            r = pl.multiple_of(i * X, X) + k * SUB
            e = e_ref[pl.ds(r, SUB), :]
            ep[pl.ds(r + pad, SUB), :] = e
            ey[pl.ds(r + pad, SUB), :] = jnp.where(
                lane == LANES - 1, 0.0, pltpu.roll(e, LANES - 1, 1)
            )
        return 0

    lax.fori_loop(0, 2 * L, fill, 0)

    def block(i, _):
        layer = lax.rem(i, L)
        up = jnp.where(layer < L - 1, 1.0, 0.0).astype(F32)
        down = jnp.where(layer > 0, 1.0, 0.0).astype(F32)
        for k in range(nt):
            r = pl.multiple_of(i * X, X) + k * SUB + pad
            e = ep[pl.ds(r, SUB), :]
            for j, (dz, dx, dy) in enumerate(HALF):
                o = (ey if dy else ep)[pl.ds(r + dz * X + dx, SUB), :]
                c = (e * twice_weight(abs(dz) + abs(dx) + dy)) * o / (e + o)
                if dz == 1:
                    c = c * up
                if dz == -1:
                    c = c * down
                if dx == 1 and k == nt - 1:
                    c = jnp.where(sub == SUB - 1, 0.0, c)
                if dx == -1 and k == 0:
                    c = jnp.where(sub == 0, 0.0, c)
                c_ref[j, pl.ds(r, SUB), :] = c
                if dy:
                    c_ref[NSIDE + j, pl.ds(r, SUB), :] = pltpu.roll(c, 1, 1)
        return 0

    lax.fori_loop(0, 2 * L, block, 0)

    def total(i, _):
        for k in range(nt):
            r = pl.multiple_of(i * X, X) + k * SUB + pad
            own, back = None, None
            for j, (dz, dx, dy) in enumerate(HALF):
                f = c_ref[j, pl.ds(r, SUB), :]
                b = c_ref[j, pl.ds(r - dz * X - dx, SUB), :]
                own = f if own is None else own + f
                if dy:
                    back = b if back is None else back + b
                else:
                    own = own + b
            d_ref[pl.ds(r - pad, SUB), :] = own + pltpu.roll(back, 1, 1)
        return 0

    lax.fori_loop(0, 2 * L, total, 0)


def coupling(modulus, L, X):
    rows, pad = 2 * L * X, X + SUB
    return call(
        functools.partial(coupling_kernel, L, X),
        [sds(NCOEF, rows + 2 * pad, LANES), sds(rows, LANES)],
        [modulus],
        scratch=[pltpu.VMEM((rows + 2 * pad, LANES), F32)] * 2,
        limit=5 << 20,
        flops=200 * rows * LANES,
        name="coupling",
    )


def stencil_kernel(L, X, group, comps, padded, u_ref, c_ref, d_ref, *rest):
    pad, nt = X + SUB, X // SUB
    f_ref = rest[-1] if padded else rest[-2]
    if padded:
        up = u_ref
    else:
        up = rest[-1]
        zero = jnp.zeros((pad, LANES), F32)
        up[pl.ds(0, pad), :] = zero
        up[pl.ds(pad + 6 * L * X, pad), :] = zero

        def fill(i, _):
            for k in range(nt):
                r = pl.multiple_of(i * X, X) + k * SUB
                up[pl.ds(r + pad, SUB), :] = u_ref[pl.ds(r, SUB), :]
            return 0

        lax.fori_loop(0, 6 * L, fill, 0)
    count, lowest = len(comps), comps[0]

    def block(i, _):
        which = i // (nt // group)
        first = lax.rem(i, nt // group) * group * SUB
        body = which // count
        bc = body * 3 + lowest + lax.rem(which, count)
        for k in range(group):
            for layer in range(L):
                ru = pl.multiple_of(bc * L * X + layer * X + first, SUB) + k * SUB
                rf = pl.multiple_of(which * L * X + layer * X + first, SUB) + k * SUB
                rc = pl.multiple_of(body * L * X + layer * X + first, SUB) + k * SUB + pad
                t = {
                    (dz, dx): up[pl.ds(ru + pad + dz * X + dx, SUB), :]
                    for dz in (-1, 0, 1)
                    for dx in (-1, 0, 1)
                }
                acc = -d_ref[pl.ds(rc - pad, SUB), :] * t[0, 0]
                ahead, behind = None, None
                for j, (dz, dx, dy) in enumerate(HALF):
                    back = c_ref[j, pl.ds(rc - dz * X - dx, SUB), :] * t[-dz, -dx]
                    near = c_ref[j + NSIDE * dy, pl.ds(rc, SUB), :] * t[dz, dx]
                    if dy:
                        ahead = near if ahead is None else ahead + near
                        behind = back if behind is None else behind + back
                    else:
                        acc = acc + near
                        acc = acc + back
                f_ref[pl.ds(rf, SUB), :] = (
                    acc + pltpu.roll(ahead, LANES - 1, 1) + pltpu.roll(behind, 1, 1)
                )
        return 0

    lax.fori_loop(0, 2 * count * (nt // group), block, 0)


def stencil(u, coef, diag, L, X, comps, padded, after=()):
    pad = X + SUB
    rows = 2 * len(comps) * L * X
    return call(
        functools.partial(stencil_kernel, L, X, 8, comps, padded),
        sds(rows, LANES),
        [u, coef, diag, *after],
        specs=[VMEM] * 3 + [pl.BlockSpec(memory_space=pl.ANY)] * len(after),
        scratch=[] if padded else [pltpu.VMEM((6 * L * X + 2 * pad, LANES), F32)],
        limit=(1 << 20) if padded else (5 << 20),
        flops=60 * rows * LANES,
        name="stencil",
    )


def message_kernel(L, X, u_ref, gap_ref, own, row, off, act, out_ref, tile, gap, words, sems):
    copies = [
        pltpu.make_async_copy(u_ref.at[pl.ds(2 * L * X, X)], out_ref.at[pl.ds(0, X)], sems.at[0]),
        pltpu.make_async_copy(u_ref.at[pl.ds(5 * L * X, X)], tile, sems.at[1]),
        pltpu.make_async_copy(gap_ref, gap, sems.at[2]),
    ]
    small = [
        pltpu.make_async_copy(ref, words.at[pl.ds(k, 1)], sems.at[3 + k])
        for k, ref in enumerate((row, off, act, own))
    ]
    for c in small + copies:
        c.start()
    for c in small:
        c.wait()
    lane = lane_ids()
    for k in range(4):
        halves = [
            jnp.broadcast_to(words[pl.ds(k, 1), pl.ds(h * LANES, LANES)].astype(F32), (SUB, LANES))
            for h in range(INTERSECTIONS)
        ]
        for e in range(INTERSECTIONS):
            index = (lane * INTERSECTIONS + e) & (LANES - 1)
            picked = [take_lanes(x, index) for x in halves]
            value = jnp.where(lane < LANES // INTERSECTIONS, picked[0], picked[1])
            out_ref[pl.ds(2 * X + INTERSECTIONS * k + e, 1), :] = value[:1]
    for c in copies:
        c.wait()
    out_ref[pl.ds(X, X), :] = tile[...] + gap[...]


def first_message(u, clearance, pairs, L, X):
    return call(
        functools.partial(message_kernel, L, X),
        sds(2 * X + 4 * INTERSECTIONS, LANES),
        [u, clearance, *pairs],
        specs=[pl.BlockSpec(memory_space=pl.ANY)] * 6,
        scratch=[
            pltpu.VMEM((X, LANES), F32),
            pltpu.VMEM((X, LANES), F32),
            pltpu.VMEM((4, INTERSECTIONS * X), jnp.int32),
            pltpu.SemaphoreType.DMA((7,)),
        ],
        limit=58 << 20,
        name="message",
    )


def edge_index():
    return jnp.where(lane_ids() < LANES // 2, 0, LANES - 1)


def choose(flag, a, b):
    return jnp.where(jnp.broadcast_to(flag, a.shape) == 1, a, b)


def pair_rows(odd, low, high, first_ref, second_ref):
    first_ref[...] = choose(odd, low, high)
    second_ref[...] = choose(odd, high, low)


def x_rows(L, X, start, count, src, xl_ref, xh_ref, at):
    for bc in range(count):
        base = start + bc * L * X
        xl_ref[pl.ds((at + bc) * L, L), :] = src[pl.ds(base, L, stride=X), :]
        xh_ref[pl.ds((at + bc) * L, L), :] = src[pl.ds(base + X - 1, L, stride=X), :]


def pack_kernel(L, X, u_ref, e_ref, xl_ref, xh_ref, x1_ref, x2_ref, y_ref, w_ref):
    nt = X // SUB
    x_rows(L, X, 0, 6, u_ref, xl_ref, xh_ref, 0)
    x_rows(L, X, 0, 2, e_ref, xl_ref, xh_ref, 6)
    pair_rows(lax.axis_index("gx") % 2, xl_ref[...], xh_ref[...], x1_ref, x2_ref)
    index = edge_index()
    slot = lane_ids() % (LANES // 2)

    def tile(k, _):
        r = pl.multiple_of(k * SUB, SUB)
        w = jnp.zeros((SUB, LANES), F32)
        for f in range(8 * L):
            src, row = (u_ref, f) if f < 6 * L else (e_ref, f - 6 * L)
            v = src[pl.ds(row * X + r, SUB), :]
            w = jnp.where(slot == f, take_lanes(v, index), w)
        w_ref[pl.ds(r, SUB), :] = w
        return 0

    lax.fori_loop(0, nt, tile, 0)
    y_ref[...] = w_ref[...].T


def pack(u, e, L, X):
    return call(
        functools.partial(pack_kernel, L, X),
        [sds(8 * L, LANES)] * 4 + [sds(LANES, LANES)],
        [u, e],
        scratch=[pltpu.VMEM((X, LANES), F32)],
        limit=1 << 20,
        flops=u.size,
        name="pack",
    )


def corner_kernel(n, y_ref, r1_ref, r2_ref, m1_ref, m2_ref):
    half = LANES // 2
    odd_x, odd_y = lax.axis_index("gx") % 2, lax.axis_index("gy") % 2
    lane = lane_ids(n)
    r1, r2 = r1_ref[...], r2_ref[...]
    low, high = choose(odd_x, r1, r2), choose(odd_x, r2, r1)
    left = y_ref[pl.ds(0, n), :], jnp.where(lane == 0, low, pltpu.roll(high, LANES - 1, 1))
    right = y_ref[pl.ds(half, n), :], jnp.where(lane == 0, pltpu.roll(low, 1, 1), high)
    for k in range(2):
        at = pl.ds(k * n, n)
        pair_rows(odd_y, left[k], right[k], m1_ref.at[at], m2_ref.at[at])


def corners(n, y, r1, r2):
    return call(
        functools.partial(corner_kernel, n),
        [sds(2 * n, LANES), sds(2 * n, LANES)],
        [y, r1, r2],
        limit=1 << 20,
        name="corners",
    )


def split(x):
    high = x.astype(BF16)
    return high, (x - high.astype(F32)).astype(BF16)


def dot(a, b, dims=((1,), (0,))):
    return lax.dot_general(a, b, (dims, ((), ())), preferred_element_type=F32)


def project(x, pair, dims):
    high, low = split(x)
    return x + (dot(high, pair[0], dims) + dot(high, pair[1], dims) + dot(low, pair[0], dims))


def contact_and_edges(L, X, GX, NY, n, first, later, own_s, row_s, m_ref, gathered, whole, grow, work, pairs_ref, yc, ct_s, xc, cm):
    oxl, oxh, oy, rx1, rx2, ry1, ry2, exl, exh, ey, erx1, erx2, ery1, ery2 = gathered
    nt, half, ne = X // SUB, LANES // 2, 8 * L
    gx, me = lax.axis_index("gx"), lax.axis_index("gy")
    lane, sub = lane_ids(), sub_ids()
    lane_t = lane_ids(X)

    mh, ml = split(m_ref[...])
    straight, flipped = ((1,), (0,)), ((1,), (1,))
    pairs_ref[...] = jnp.zeros((LANES, LANES), F32)
    for q in range(NY):
        pairs_ref[pl.ds(q * SUB, SUB), :] = first[q][pl.ds(2 * X, SUB), :]
    columns = pairs_ref[...].T
    my_chip, my_core = me // 2, me % 2
    for q in range(NY):
        chip = lax.bitwise_xor(my_chip, q // 2)
        core = my_core if q % 2 == 0 else 1 - my_core
        owner = chip * 2 + core
        whole[pl.ds(pl.multiple_of(owner * X, X), X), :] = later[q][pl.ds(0, X), :]

    def gather(i, _):
        for k in range(SUB):
            p = i * SUB + k
            at = own_s[0, p] * X + row_s[0, p]
            to = (k % INTERSECTIONS) * X + i * (SUB // INTERSECTIONS) + k // INTERSECTIONS
            grow[pl.ds(to, 1), :] = whole[pl.ds(at, 1), :]
        return 0

    lax.fori_loop(0, INTERSECTIONS * X // SUB, gather, 0)

    def column(f):
        return jnp.broadcast_to(columns[:, f : f + 1], (X, LANES))

    slave = None
    for e in range(INTERSECTIONS):
        off = column(2 + e).astype(jnp.int32)
        moved = take_lanes(grow[pl.ds(e * X, X), :], (lane_t + off) & (LANES - 1))
        gap = later[0][pl.ds(X, X), :] - project(moved, (mh, ml), straight)
        t = column(4 + e) * (penalty_stiffness * jnp.maximum(0.0, -gap))
        slave = t if slave is None else slave + t
    cm[1] = slave

    fh, fl = split(later[0][pl.ds(0, X), :])
    me_f = me.astype(F32)
    node = lax.broadcasted_iota(jnp.int32, (X, X), 0).astype(F32)
    master = jnp.zeros((X, LANES), F32)
    blocks = [(q, e) for q in range(NY) for e in range(INTERSECTIONS)]
    for s, (q, e) in enumerate(blocks):
        base = q * SUB
        hot = jnp.where(node == pairs_ref[base + e : base + e + 1, :], 1.0, 0.0).astype(BF16)
        rows = dot(hot, fh, ((0,), (0,))) + dot(hot, fl, ((0,), (0,)))
        off = column(base + 2 + e).astype(jnp.int32)
        work[pl.ds(s * X, X), :] = take_lanes(rows, (lane_t + off) & (LANES - 1))
    for s, (q, e) in enumerate(blocks):
        gap = later[q][pl.ds(X, X), :] - project(
            work[pl.ds(s * X, X), :], (mh, ml), straight
        )
        work[pl.ds(s * X, X), :] = penalty_stiffness * jnp.maximum(0.0, -gap)
    for s, (q, e) in enumerate(blocks):
        base = q * SUB
        back = project(work[pl.ds(s * X, X), :], (mh, ml), flipped)
        off = column(base + 2 + e).astype(jnp.int32)
        work[pl.ds(s * X, X), :] = take_lanes(back, (lane_t - off) & (LANES - 1))
    for s, (q, e) in enumerate(blocks):
        base = q * SUB
        weight = jnp.where(
            pairs_ref[base + 6 + e : base + 7 + e, :] == me_f,
            pairs_ref[base + 4 + e : base + 5 + e, :],
            0.0,
        )
        hot = jnp.where(node == pairs_ref[base + e : base + e + 1, :], weight, 0.0).astype(BF16)
        bh, bl = split(work[pl.ds(s * X, X), :])
        master = master + (dot(hot, bh) + dot(hot, bl))
    cm[0] = -master

    inside = (gx > 0, gx < GX - 1, me > 0, me < NY - 1)
    ok = [jnp.where(x, 1.0, 0.0).astype(F32) for x in inside]

    def edge(own_e, own_u, near_e, near_u, corner_e, corner_u, put):
        near = {}
        for d in (-1, 0, 1):
            value_e, value_u = near_e, list(near_u)
            if d:
                value_e = pltpu.roll(near_e, (-d) % LANES, 1)
                value_u = [pltpu.roll(x, (-d) % LANES, 1) for x in near_u]
                at = lane == (0 if d < 0 else LANES - 1)
                if corner_e is None:
                    value_e = jnp.where(at, 0.0, value_e)
                else:
                    value_e = jnp.where(at, corner_e, value_e)
                    value_u = [jnp.where(at, c, x) for c, x in zip(corner_u, value_u)]
            near[d] = (value_e, value_u)
        sums = [None] * 3
        for dz in (-1, 0, 1):
            for d in (-1, 0, 1):
                o, us = near[d]
                if dz:
                    o = pltpu.roll(o, (-dz) % SUB, 0)
                    o = jnp.where(sub == (0 if dz < 0 else SUB - 1), 0.0, o)
                    us = [pltpu.roll(x, (-dz) % SUB, 0) for x in us]
                c = (own_e * twice_weight(1 + abs(dz) + abs(d))) * o / (own_e + o)
                for comp in range(3):
                    term = c * (us[comp] - own_u[comp])
                    sums[comp] = term if sums[comp] is None else sums[comp] + term
        for comp in range(3):
            put(comp, sums[comp])

    def rows(ref, k):
        return ref[pl.ds(k, L), :]

    def got(refs, k, axis):
        return choose(odd[axis], rows(refs[0], k), rows(refs[1], k))

    odd = gx % 2, me % 2

    yc[...] = jnp.zeros((LANES, LANES), F32)
    for b in range(2):
        ue = [(b * 3 + c) * L for c in range(3)]
        ee = (6 + b) * L
        for s, (own_x, got_x, own_xe, got_xe) in enumerate(
            ((oxl, (rx1, rx2), exl, (erx1, erx2)), (oxh, (rx2, rx1), exh, (erx2, erx1)))
        ):
            edge(
                rows(own_xe, ee),
                [rows(own_x, k) for k in ue],
                got(got_xe, ee, 0) * ok[s],
                [got(got_x, k, 0) for k in ue],
                None,
                None,
                lambda c, v, s=s, ue=ue: xc.__setitem__((s, pl.ds(ue[c], L), slice(None)), v),
            )
        for s, (got_y, got_ye) in enumerate((((ry1, ry2), (ery1, ery2)), ((ry2, ry1), (ery2, ery1)))):
            corner_ok = jnp.where(lane == 0, ok[0], ok[1]) * ok[2 + s]
            edge(
                rows(ey, s * half + ee),
                [rows(oy, s * half + k) for k in ue],
                got(got_ye, ee, 1) * ok[2 + s],
                [got(got_y, k, 1) for k in ue],
                got(got_ye, ne + ee, 1) * corner_ok,
                [got(got_y, n + k, 1) for k in ue],
                lambda c, v, s=s, ue=ue: yc.__setitem__((pl.ds(s * half + ue[c], L), slice(None)), v),
            )
    ct_s[...] = yc[...].T


def forced(L, X, k, f, face, base, ct, xc, cm_tile):
    lane, sub = lane_ids(), sub_ids()
    half = LANES // 2
    pick = jnp.where(lane == 0, f, jnp.where(lane == LANES - 1, half + f, half - 1))
    force = base + take_lanes(ct, pick)
    if k == 0:
        force = force + jnp.where(sub == 0, xc[0, pl.ds(f, 1), :], 0.0)
    if k == X // SUB - 1:
        force = force + jnp.where(sub == SUB - 1, xc[1, pl.ds(f, 1), :], 0.0)
    if cm_tile is not None:
        force = force + face * cm_tile
    return force


def advance(L, X, last, v_ref, u_ref, rho_ref, forces, ct_s, xc, cm, u1_ref, v1_ref, w_s, sinks, sems):
    nt, half, pad = X // SUB, LANES // 2, X + SUB
    shift_in, shift_out = (pad, 0) if last else (0, pad)
    index = edge_index()
    slot = lane_ids() % half
    if not last:
        w_s[...] = jnp.zeros((X, LANES), F32)

    def layer_of(i, _):
        b, layer = i // L, lax.rem(i, L)
        face = jnp.where(layer == 0, 1.0, 0.0).astype(F32)
        for k in range(nt):
            rr = pl.multiple_of(i * X, X) + k * SUB
            scale = time_step / rho_ref[pl.ds(rr, SUB), :]
            ct = ct_s[pl.ds(k * SUB, SUB), :]
            if not last:
                w = w_s[pl.ds(k * SUB, SUB), :]
            for c in range(3):
                f = (b * 3 + c) * L + layer
                r = pl.multiple_of(f * X, X) + k * SUB
                if len(forces) == 2:
                    fr = pl.multiple_of(((b * 2 + c) if c < 2 else b) * L * X + layer * X, X)
                    base = forces[0 if c < 2 else 1][pl.ds(fr + k * SUB, SUB), :]
                else:
                    base = forces[0][pl.ds(r, SUB), :]
                tile = cm[b, pl.ds(k * SUB, SUB), :] if c == 2 else None
                vel = v_ref[pl.ds(r, SUB), :] + scale * forced(L, X, k, f, face, base, ct, xc, tile)
                disp = u_ref[pl.ds(r + shift_in, SUB), :] + time_step * vel
                v1_ref[pl.ds(r, SUB), :] = vel
                u1_ref[pl.ds(r + shift_out, SUB), :] = disp
                if not last:
                    w = jnp.where(slot == f, take_lanes(disp, index), w)
            if not last:
                w_s[pl.ds(k * SUB, SUB), :] = w
        if last:
            for c in range(3):
                at = pl.ds(pl.multiple_of(((b * 3 + c) * L + layer) * X, X), X)
                for s, ref in enumerate((u1_ref, v1_ref)):
                    pltpu.make_async_copy(ref.at[at], sinks[s].at[at], sems.at[s]).start()
        return 0

    lax.fori_loop(0, 2 * L, layer_of, 0)
    if last:
        for s, ref in enumerate((u1_ref, v1_ref)):
            pltpu.make_async_copy(ref, sinks[s], sems.at[s]).wait()


NGOT = 14


def contact_kernel(L, X, GX, NY, n, own_s, row_s, m_ref, gap_ref, v_ref, u_ref, rho_ref, f_ref, *rest):
    gathered, first = rest[:NGOT], rest[NGOT : NGOT + NY]
    cm, ct_s, xc, face_out, whole, grow, work, pairs_ref, yc = rest[NGOT + NY :]
    contact_and_edges(
        L, X, GX, NY, n, first, first, own_s, row_s, m_ref, gathered,
        whole, grow, work, pairs_ref, yc, ct_s, xc, cm,
    )
    for b in range(2):
        f = (b * 3 + 2) * L
        for k in range(X // SUB):
            at = pl.ds(f * X + k * SUB, SUB)
            part = pl.ds(k * SUB, SUB)
            force = forced(L, X, k, f, 1.0, f_ref[at, :], ct_s[part, :], xc, cm[b, part, :])
            scale = time_step / rho_ref[pl.ds(b * L * X + k * SUB, SUB), :]
            disp = u_ref[at, :] + time_step * (v_ref[at, :] + scale * force)
            if b == 1:
                disp = disp + gap_ref[part, :]
            face_out[pl.ds(b * X + k * SUB, SUB), :] = disp


def contact_scratch(L, X, NY):
    vm = pltpu.VMEM
    return [
        vm((NY * X, LANES), F32),
        vm((INTERSECTIONS * X, LANES), F32),
        vm((NY * INTERSECTIONS * X, LANES), F32),
        vm((LANES, LANES), F32),
        vm((LANES, LANES), F32),
    ]


def grant(X, NY):
    return (3 << 20) + 2 * NY * INTERSECTIONS * X * LANES * 4 * max(1, NY // 8)


def contact(L, X, GX, NY, n, args):
    return call(
        functools.partial(contact_kernel, L, X, GX, NY, n),
        [sds(2, X, LANES), sds(X, LANES), sds(2, 6 * L, LANES), sds(2 * X, LANES)],
        args,
        specs=[SMEM] * 2 + [VMEM] * (len(args) - 2),
        scratch=contact_scratch(L, X, NY),
        limit=grant(X, NY),
        flops=60 * NY * INTERSECTIONS * X * LANES,
        name="contact",
    )


def step_kernel(L, X, v_ref, u_ref, rho_ref, f_ref, cm, ct_s, xc, *rest):
    u1_ref, v1_ref, xl_ref, xh_ref, x1_ref, x2_ref, y_ref, w_s = rest
    pad = X + SUB
    advance(L, X, False, v_ref, u_ref, rho_ref, (f_ref,), ct_s, xc, cm, u1_ref, v1_ref, w_s, None, None)
    zero = jnp.zeros((pad, LANES), F32)
    u1_ref[pl.ds(0, pad), :] = zero
    u1_ref[pl.ds(pad + 6 * L * X, pad), :] = zero
    x_rows(L, X, pad, 6, u1_ref, xl_ref, xh_ref, 0)
    pair_rows(lax.axis_index("gx") % 2, xl_ref[...], xh_ref[...], x1_ref, x2_ref)
    y_ref[...] = w_s[...].T


def step(L, X, args):
    R = 6 * L * X
    return call(
        functools.partial(step_kernel, L, X),
        [sds(R + 2 * (X + SUB), LANES), sds(R, LANES)] + [sds(6 * L, LANES)] * 4 + [sds(LANES, LANES)],
        args,
        scratch=[pltpu.VMEM((X, LANES), F32)],
        limit=2 << 20,
        flops=20 * R * LANES,
        name="step",
    )


def last_kernel(L, X, GX, NY, n, own_s, row_s, m_ref, v_ref, u_ref, rho_ref, f_ref, g_ref, *rest):
    gathered, rest = rest[:NGOT], rest[NGOT:]
    first, later, rest = rest[:NY], rest[NY : 2 * NY], rest[2 * NY :]
    sinks, scratch = rest[:2], rest[2:]
    whole, grow, work, pairs_ref, yc, ct_s, xc, cm, u1_s, v1_s, sems = scratch
    contact_and_edges(
        L, X, GX, NY, n, first, later, own_s, row_s, m_ref, gathered,
        whole, grow, work, pairs_ref, yc, ct_s, xc, cm,
    )
    advance(
        L, X, True, v_ref, u_ref, rho_ref, (f_ref, g_ref), ct_s, xc, cm, u1_s, v1_s, None, sinks, sems
    )


def last_step(L, X, GX, NY, n, args):
    R = 6 * L * X
    vm = pltpu.VMEM
    return call(
        functools.partial(last_kernel, L, X, GX, NY, n),
        [sds(R, LANES), sds(R, LANES)],
        args,
        specs=[SMEM] * 2 + [VMEM] * (len(args) - 2),
        scratch=contact_scratch(L, X, NY)
        + [
            vm((X, LANES), F32),
            vm((2, 6 * L, LANES), F32),
            vm((2, X, LANES), F32),
            vm((R, LANES), F32),
            vm((R, LANES), F32),
            pltpu.SemaphoreType.DMA((2,)),
        ],
        limit=grant(X, NY) + 2 * R * LANES * 4,
        out_spec=pl.BlockSpec(memory_space=pl.ANY),
        flops=80 * R * LANES,
        name="last",
    )


def swap(x, axis="gy"):
    return lax.ppermute(x, axis, [(i, i ^ 1) for i in range(lax.axis_size(axis))])


def cross(x, axis="gy"):
    n = lax.axis_size(axis)
    return lax.ppermute(x, axis, [(i, (i + 1) % n if i % 2 else (i - 1) % n) for i in range(n)])


def far(x):
    n = lax.axis_size("gy")
    return [x] + [
        lax.ppermute(x, "gy", [(i, i ^ (2 * k)) for i in range(n)]) for k in range(1, n // 2)
    ]


def both(parts):
    return [p for part in parts for p in (part, swap(part))]


def body(
    displacement,
    velocity,
    modulus,
    density,
    clearance,
    mortar_coupling,
    pair_owner,
    pair_row,
    pair_offset,
    pair_active,
):
    L, X, Y = displacement.shape[2:]
    assert Y == LANES and L == SUB and X == LANES
    GX, NY = lax.axis_size("gx"), lax.axis_size("gy")

    u, v = displacement.reshape(-1, Y), velocity.reshape(-1, Y)
    e, rho = modulus.reshape(-1, Y), density.reshape(-1, Y)
    own, row, off, act = (
        a.transpose(0, 2, 1).reshape(1, -1)
        for a in (pair_owner, pair_row, pair_offset, pair_active)
    )
    parts = far(first_message(u, clearance, (own, row, off, act), L, X))
    xl, xh, x1, x2, y = pack(u, e, L, X)
    rx1, rx2 = swap(x1, "gx"), cross(x2, "gx")
    coef, diag = coupling(e, L, X)
    diag, rx1, rx2, *parts = lax.optimization_barrier((diag, rx1, rx2, *parts))
    m1, m2 = corners(8 * L, y, rx1, rx2)
    f = stencil(u, coef, diag, L, X, (0, 1, 2), False, (m1, *parts[1:]))
    stiff = (xl, xh, y, rx1, rx2, swap(m1), cross(m2))
    messages = both(parts)
    cm, ct, xc, face = contact(
        L, X, GX, NY, 8 * L,
        (own, row, mortar_coupling, clearance, v, u, rho, f, *stiff, *stiff, *messages),
    )
    parts = far(face)
    u, v, xl, xh, x1, x2, y = step(L, X, (v, u, rho, f, cm, ct, xc))
    rx1, rx2 = swap(x1, "gx"), cross(x2, "gx")
    f = stencil(u, coef, diag, L, X, (0, 1), True)
    f, rx1, rx2, *parts = lax.optimization_barrier((f, rx1, rx2, *parts))
    m1, m2 = corners(6 * L, y, rx1, rx2)
    g = stencil(u, coef, diag, L, X, (2,), True, (m1, f, *parts[1:]))
    edges = (xl, xh, y, rx1, rx2, swap(m1), cross(m2))
    u, v = last_step(
        L, X, GX, NY, 6 * L,
        (own, row, mortar_coupling, v, u, rho, f, g, *edges, *stiff, *messages, *both(parts)),
    )
    return u.reshape(displacement.shape), v.reshape(velocity.shape)


def solution(mesh):
    return jax.shard_map(
        body,
        mesh=mesh,
        in_specs=(
            P(None, None, None, "gx", "gy"),
            P(None, None, None, "gx", "gy"),
            P(None, None, "gx", "gy"),
            P(None, None, "gx", "gy"),
            P("gx", "gy"),
            P(),
            P("gx", "gy", None),
            P("gx", "gy", None),
            P("gx", "gy", None),
            P("gx", "gy", None),
        ),
        out_specs=(P(None, None, None, "gx", "gy"), P(None, None, None, "gx", "gy")),
        check_vma=False,
    )
```

```python
import functools

import jax
import jax.numpy as jnp
from jax import lax
from jax.experimental import pallas as pl
from jax.experimental.pallas import tpu as pltpu
from jax.sharding import PartitionSpec as P

F32 = jnp.float32
BF16 = jnp.bfloat16
INTERSECTIONS = 2
STEPS = 2
time_step = 0.2
penalty_stiffness = 4.0

SUB = 8
LANES = 128
FLAT = [(0, 1, 0), (1, -1, 0), (1, 0, 0), (1, 1, 0)]
SIDE = [(dz, dx, 1) for dz in (-1, 0, 1) for dx in (-1, 0, 1)]
HALF = FLAT + SIDE
NSIDE = len(SIDE)
NHALF = len(HALF)
NCOEF = NHALF + NSIDE

VMEM = pl.BlockSpec(memory_space=pltpu.VMEM)
SMEM = pl.BlockSpec(memory_space=pltpu.SMEM)


def twice_weight(nonzero):
    return 2.0 * 0.5 ** (nonzero - 1)


def lane_ids(rows=SUB):
    return lax.broadcasted_iota(jnp.int32, (rows, LANES), 1)


def sub_ids(rows=SUB):
    return lax.broadcasted_iota(jnp.int32, (rows, LANES), 0)


def take_lanes(values, index):
    return jnp.take_along_axis(values, index, axis=1)


def call(
    kernel, out_shape, args, specs=None, scratch=(), limit=None, flops=0, name=None, out_spec=VMEM
):
    nbytes = sum(a.size * 4 for a in args)
    return pl.pallas_call(
        kernel,
        out_shape=out_shape,
        in_specs=specs or [VMEM] * len(args),
        out_specs=jax.tree.map(lambda _: out_spec, out_shape),
        scratch_shapes=scratch,
        name=name,
        cost_estimate=pl.CostEstimate(flops=flops, bytes_accessed=nbytes, transcendentals=0),
        compiler_params=pltpu.CompilerParams(vmem_limit_bytes=limit),
    )(*args)


def sds(*shape):
    return jax.ShapeDtypeStruct(shape, F32)


def coupling_kernel(L, X, e_ref, c_ref, d_ref, ep, ey):
    rows, pad, nt = 2 * L * X, X + SUB, X // SUB
    zero = jnp.zeros((pad, LANES), F32)
    for s in (ep, ey):
        s[pl.ds(0, pad), :] = zero
        s[pl.ds(pad + rows, pad), :] = zero
    for j in range(NHALF):
        c_ref[j, pl.ds(0, pad), :] = zero
        c_ref[j, pl.ds(pad + rows, pad), :] = zero
    lane, sub = lane_ids(), sub_ids()

    def fill(i, _):
        for k in range(nt):
            r = pl.multiple_of(i * X, X) + k * SUB
            e = e_ref[pl.ds(r, SUB), :]
            ep[pl.ds(r + pad, SUB), :] = e
            ey[pl.ds(r + pad, SUB), :] = jnp.where(
                lane == LANES - 1, 0.0, pltpu.roll(e, LANES - 1, 1)
            )
        return 0

    lax.fori_loop(0, 2 * L, fill, 0)

    def block(i, _):
        layer = lax.rem(i, L)
        up = jnp.where(layer < L - 1, 1.0, 0.0).astype(F32)
        down = jnp.where(layer > 0, 1.0, 0.0).astype(F32)
        for k in range(nt):
            r = pl.multiple_of(i * X, X) + k * SUB + pad
            e = ep[pl.ds(r, SUB), :]
            for j, (dz, dx, dy) in enumerate(HALF):
                o = (ey if dy else ep)[pl.ds(r + dz * X + dx, SUB), :]
                c = (e * twice_weight(abs(dz) + abs(dx) + dy)) * o / (e + o)
                if dz == 1:
                    c = c * up
                if dz == -1:
                    c = c * down
                if dx == 1 and k == nt - 1:
                    c = jnp.where(sub == SUB - 1, 0.0, c)
                if dx == -1 and k == 0:
                    c = jnp.where(sub == 0, 0.0, c)
                c_ref[j, pl.ds(r, SUB), :] = c
                if dy:
                    c_ref[NSIDE + j, pl.ds(r, SUB), :] = pltpu.roll(c, 1, 1)
        return 0

    lax.fori_loop(0, 2 * L, block, 0)

    def total(i, _):
        for k in range(nt):
            r = pl.multiple_of(i * X, X) + k * SUB + pad
            own, back = None, None
            for j, (dz, dx, dy) in enumerate(HALF):
                f = c_ref[j, pl.ds(r, SUB), :]
                b = c_ref[j, pl.ds(r - dz * X - dx, SUB), :]
                own = f if own is None else own + f
                if dy:
                    back = b if back is None else back + b
                else:
                    own = own + b
            d_ref[pl.ds(r - pad, SUB), :] = own + pltpu.roll(back, 1, 1)
        return 0

    lax.fori_loop(0, 2 * L, total, 0)


def coupling(modulus, L, X):
    rows, pad = 2 * L * X, X + SUB
    return call(
        functools.partial(coupling_kernel, L, X),
        [sds(NCOEF, rows + 2 * pad, LANES), sds(rows, LANES)],
        [modulus],
        scratch=[pltpu.VMEM((rows + 2 * pad, LANES), F32)] * 2,
        limit=5 << 20,
        flops=200 * rows * LANES,
        name="coupling",
    )


def stencil_kernel(L, X, group, comps, padded, u_ref, c_ref, d_ref, *rest):
    pad, nt = X + SUB, X // SUB
    f_ref = rest[-1] if padded else rest[-2]
    if padded:
        up = u_ref
    else:
        up = rest[-1]
        zero = jnp.zeros((pad, LANES), F32)
        up[pl.ds(0, pad), :] = zero
        up[pl.ds(pad + 6 * L * X, pad), :] = zero

        def fill(i, _):
            for k in range(nt):
                r = pl.multiple_of(i * X, X) + k * SUB
                up[pl.ds(r + pad, SUB), :] = u_ref[pl.ds(r, SUB), :]
            return 0

        lax.fori_loop(0, 6 * L, fill, 0)
    count, lowest = len(comps), comps[0]

    def block(i, _):
        which = i // (nt // group)
        first = lax.rem(i, nt // group) * group * SUB
        body = which // count
        bc = body * 3 + lowest + lax.rem(which, count)
        for k in range(group):
            for layer in range(L):
                ru = pl.multiple_of(bc * L * X + layer * X + first, SUB) + k * SUB
                rf = pl.multiple_of(which * L * X + layer * X + first, SUB) + k * SUB
                rc = pl.multiple_of(body * L * X + layer * X + first, SUB) + k * SUB + pad
                t = {
                    (dz, dx): up[pl.ds(ru + pad + dz * X + dx, SUB), :]
                    for dz in (-1, 0, 1)
                    for dx in (-1, 0, 1)
                }
                acc = -d_ref[pl.ds(rc - pad, SUB), :] * t[0, 0]
                ahead, behind = None, None
                for j, (dz, dx, dy) in enumerate(HALF):
                    back = c_ref[j, pl.ds(rc - dz * X - dx, SUB), :] * t[-dz, -dx]
                    near = c_ref[j + NSIDE * dy, pl.ds(rc, SUB), :] * t[dz, dx]
                    if dy:
                        ahead = near if ahead is None else ahead + near
                        behind = back if behind is None else behind + back
                    else:
                        acc = acc + near
                        acc = acc + back
                f_ref[pl.ds(rf, SUB), :] = (
                    acc + pltpu.roll(ahead, LANES - 1, 1) + pltpu.roll(behind, 1, 1)
                )
        return 0

    lax.fori_loop(0, 2 * count * (nt // group), block, 0)


def stencil(u, coef, diag, L, X, comps, padded, after=()):
    pad = X + SUB
    rows = 2 * len(comps) * L * X
    return call(
        functools.partial(stencil_kernel, L, X, 8, comps, padded),
        sds(rows, LANES),
        [u, coef, diag, *after],
        specs=[VMEM] * 3 + [pl.BlockSpec(memory_space=pl.ANY)] * len(after),
        scratch=[] if padded else [pltpu.VMEM((6 * L * X + 2 * pad, LANES), F32)],
        limit=(1 << 20) if padded else (5 << 20),
        flops=60 * rows * LANES,
        name="stencil",
    )


def message_kernel(L, X, u_ref, gap_ref, own, row, off, act, out_ref, tile, gap, words, sems):
    copies = [
        pltpu.make_async_copy(u_ref.at[pl.ds(2 * L * X, X)], out_ref.at[pl.ds(0, X)], sems.at[0]),
        pltpu.make_async_copy(u_ref.at[pl.ds(5 * L * X, X)], tile, sems.at[1]),
        pltpu.make_async_copy(gap_ref, gap, sems.at[2]),
    ]
    small = [
        pltpu.make_async_copy(ref, words.at[pl.ds(k, 1)], sems.at[3 + k])
        for k, ref in enumerate((row, off, act, own))
    ]
    for c in small + copies:
        c.start()
    for c in small:
        c.wait()
    lane = lane_ids()
    for k in range(4):
        halves = [
            jnp.broadcast_to(words[pl.ds(k, 1), pl.ds(h * LANES, LANES)].astype(F32), (SUB, LANES))
            for h in range(INTERSECTIONS)
        ]
        for e in range(INTERSECTIONS):
            index = (lane * INTERSECTIONS + e) & (LANES - 1)
            picked = [take_lanes(x, index) for x in halves]
            value = jnp.where(lane < LANES // INTERSECTIONS, picked[0], picked[1])
            out_ref[pl.ds(2 * X + INTERSECTIONS * k + e, 1), :] = value[:1]
    for c in copies:
        c.wait()
    out_ref[pl.ds(X, X), :] = tile[...] + gap[...]


def first_message(u, clearance, pairs, L, X):
    return call(
        functools.partial(message_kernel, L, X),
        sds(2 * X + 4 * INTERSECTIONS, LANES),
        [u, clearance, *pairs],
        specs=[pl.BlockSpec(memory_space=pl.ANY)] * 6,
        scratch=[
            pltpu.VMEM((X, LANES), F32),
            pltpu.VMEM((X, LANES), F32),
            pltpu.VMEM((4, INTERSECTIONS * X), jnp.int32),
            pltpu.SemaphoreType.DMA((7,)),
        ],
        limit=58 << 20,
        name="message",
    )


def edge_index():
    return jnp.where(lane_ids() < LANES // 2, 0, LANES - 1)


def choose(flag, a, b):
    return jnp.where(jnp.broadcast_to(flag, a.shape) == 1, a, b)


def pair_rows(odd, low, high, first_ref, second_ref):
    first_ref[...] = choose(odd, low, high)
    second_ref[...] = choose(odd, high, low)


def x_rows(L, X, start, count, src, xl_ref, xh_ref, at):
    for bc in range(count):
        base = start + bc * L * X
        xl_ref[pl.ds((at + bc) * L, L), :] = src[pl.ds(base, L, stride=X), :]
        xh_ref[pl.ds((at + bc) * L, L), :] = src[pl.ds(base + X - 1, L, stride=X), :]


def columns_of(L, X, count, src, at, w_ref):
    index = edge_index()
    slot = lane_ids() % (LANES // 2)

    def tile(k, _):
        r = pl.multiple_of(k * SUB, SUB)
        w = w_ref[pl.ds(r, SUB), :]
        for f in range(count * L):
            v = src[pl.ds(f * X + r, SUB), :]
            w = jnp.where(slot == at + f, take_lanes(v, index), w)
        w_ref[pl.ds(r, SUB), :] = w
        return 0

    lax.fori_loop(0, X // SUB, tile, 0)


def pack_u_kernel(L, X, u_ref, xl_ref, xh_ref, w_ref):
    x_rows(L, X, 0, 6, u_ref, xl_ref, xh_ref, 0)
    w_ref[...] = jnp.zeros((X, LANES), F32)
    columns_of(L, X, 6, u_ref, 0, w_ref)


def pack_e_kernel(L, X, e_ref, xlu_ref, xhu_ref, wu_ref, xl_ref, xh_ref, x1_ref, x2_ref, y_ref, w_ref):
    xl_ref[pl.ds(0, 6 * L), :] = xlu_ref[...]
    xh_ref[pl.ds(0, 6 * L), :] = xhu_ref[...]
    x_rows(L, X, 0, 2, e_ref, xl_ref, xh_ref, 6)
    pair_rows(lax.axis_index("gx") % 2, xl_ref[...], xh_ref[...], x1_ref, x2_ref)
    w_ref[...] = wu_ref[...]
    columns_of(L, X, 2, e_ref, 6 * L, w_ref)
    y_ref[...] = w_ref[...].T


def pack(u, e, L, X):
    part = call(
        functools.partial(pack_u_kernel, L, X),
        [sds(6 * L, LANES)] * 2 + [sds(X, LANES)],
        [u],
        limit=1 << 20,
        flops=u.size,
        name="pack_u",
    )
    return call(
        functools.partial(pack_e_kernel, L, X),
        [sds(8 * L, LANES)] * 4 + [sds(LANES, LANES)],
        [e, *part],
        scratch=[pltpu.VMEM((X, LANES), F32)],
        limit=1 << 20,
        flops=e.size,
        name="pack_e",
    )


def corner_kernel(n, y_ref, r1_ref, r2_ref, m1_ref, m2_ref):
    half = LANES // 2
    odd_x, odd_y = lax.axis_index("gx") % 2, lax.axis_index("gy") % 2
    lane = lane_ids(n)
    r1, r2 = r1_ref[...], r2_ref[...]
    low, high = choose(odd_x, r1, r2), choose(odd_x, r2, r1)
    left = y_ref[pl.ds(0, n), :], jnp.where(lane == 0, low, pltpu.roll(high, LANES - 1, 1))
    right = y_ref[pl.ds(half, n), :], jnp.where(lane == 0, pltpu.roll(low, 1, 1), high)
    for k in range(2):
        at = pl.ds(k * n, n)
        pair_rows(odd_y, left[k], right[k], m1_ref.at[at], m2_ref.at[at])


def corners(n, y, r1, r2):
    return call(
        functools.partial(corner_kernel, n),
        [sds(2 * n, LANES), sds(2 * n, LANES)],
        [y, r1, r2],
        limit=1 << 20,
        name="corners",
    )


def split(x):
    high = x.astype(BF16)
    return high, (x - high.astype(F32)).astype(BF16)


def dot(a, b, dims=((1,), (0,))):
    return lax.dot_general(a, b, (dims, ((), ())), preferred_element_type=F32)


def project(x, pair, dims):
    high, low = split(x)
    return x + (dot(high, pair[0], dims) + dot(high, pair[1], dims) + dot(low, pair[0], dims))


def contact_and_edges(L, X, GX, NY, n, first, later, own_s, row_s, m_ref, gathered, whole, grow, work, pairs_ref, yc, ct_s, xc, cm):
    oxl, oxh, oy, rx1, rx2, ry1, ry2, exl, exh, ey, erx1, erx2, ery1, ery2 = gathered
    nt, half, ne = X // SUB, LANES // 2, 8 * L
    gx, me = lax.axis_index("gx"), lax.axis_index("gy")
    lane, sub = lane_ids(), sub_ids()
    lane_t = lane_ids(X)

    mh, ml = split(m_ref[...])
    straight, flipped = ((1,), (0,)), ((1,), (1,))
    pairs_ref[...] = jnp.zeros((LANES, LANES), F32)
    for q in range(NY):
        pairs_ref[pl.ds(q * SUB, SUB), :] = first[q][pl.ds(2 * X, SUB), :]
    columns = pairs_ref[...].T
    my_chip, my_core = me // 2, me % 2
    for q in range(NY):
        chip = lax.bitwise_xor(my_chip, q // 2)
        core = my_core if q % 2 == 0 else 1 - my_core
        owner = chip * 2 + core
        whole[pl.ds(pl.multiple_of(owner * X, X), X), :] = later[q][pl.ds(0, X), :]

    def gather(i, _):
        for k in range(SUB):
            p = i * SUB + k
            at = own_s[0, p] * X + row_s[0, p]
            to = (k % INTERSECTIONS) * X + i * (SUB // INTERSECTIONS) + k // INTERSECTIONS
            grow[pl.ds(to, 1), :] = whole[pl.ds(at, 1), :]
        return 0

    lax.fori_loop(0, INTERSECTIONS * X // SUB, gather, 0)

    def column(f):
        return jnp.broadcast_to(columns[:, f : f + 1], (X, LANES))

    slave = None
    for e in range(INTERSECTIONS):
        off = column(2 + e).astype(jnp.int32)
        moved = take_lanes(grow[pl.ds(e * X, X), :], (lane_t + off) & (LANES - 1))
        gap = later[0][pl.ds(X, X), :] - project(moved, (mh, ml), straight)
        t = column(4 + e) * (penalty_stiffness * jnp.maximum(0.0, -gap))
        slave = t if slave is None else slave + t
    cm[1] = slave

    fh, fl = split(later[0][pl.ds(0, X), :])
    me_f = me.astype(F32)
    node = lax.broadcasted_iota(jnp.int32, (X, X), 0).astype(F32)
    master = jnp.zeros((X, LANES), F32)
    blocks = [(q, e) for q in range(NY) for e in range(INTERSECTIONS)]
    for s, (q, e) in enumerate(blocks):
        base = q * SUB
        hot = jnp.where(node == pairs_ref[base + e : base + e + 1, :], 1.0, 0.0).astype(BF16)
        rows = dot(hot, fh, ((0,), (0,))) + dot(hot, fl, ((0,), (0,)))
        off = column(base + 2 + e).astype(jnp.int32)
        work[pl.ds(s * X, X), :] = take_lanes(rows, (lane_t + off) & (LANES - 1))
    for s, (q, e) in enumerate(blocks):
        gap = later[q][pl.ds(X, X), :] - project(
            work[pl.ds(s * X, X), :], (mh, ml), straight
        )
        work[pl.ds(s * X, X), :] = penalty_stiffness * jnp.maximum(0.0, -gap)
    for s, (q, e) in enumerate(blocks):
        base = q * SUB
        back = project(work[pl.ds(s * X, X), :], (mh, ml), flipped)
        off = column(base + 2 + e).astype(jnp.int32)
        work[pl.ds(s * X, X), :] = take_lanes(back, (lane_t - off) & (LANES - 1))
    for s, (q, e) in enumerate(blocks):
        base = q * SUB
        weight = jnp.where(
            pairs_ref[base + 6 + e : base + 7 + e, :] == me_f,
            pairs_ref[base + 4 + e : base + 5 + e, :],
            0.0,
        )
        hot = jnp.where(node == pairs_ref[base + e : base + e + 1, :], weight, 0.0).astype(BF16)
        bh, bl = split(work[pl.ds(s * X, X), :])
        master = master + (dot(hot, bh) + dot(hot, bl))
    cm[0] = -master

    inside = (gx > 0, gx < GX - 1, me > 0, me < NY - 1)
    ok = [jnp.where(x, 1.0, 0.0).astype(F32) for x in inside]

    def edge(own_e, own_u, near_e, near_u, corner_e, corner_u, put):
        near = {}
        for d in (-1, 0, 1):
            value_e, value_u = near_e, list(near_u)
            if d:
                value_e = pltpu.roll(near_e, (-d) % LANES, 1)
                value_u = [pltpu.roll(x, (-d) % LANES, 1) for x in near_u]
                at = lane == (0 if d < 0 else LANES - 1)
                if corner_e is None:
                    value_e = jnp.where(at, 0.0, value_e)
                else:
                    value_e = jnp.where(at, corner_e, value_e)
                    value_u = [jnp.where(at, c, x) for c, x in zip(corner_u, value_u)]
            near[d] = (value_e, value_u)
        sums = [None] * 3
        for dz in (-1, 0, 1):
            for d in (-1, 0, 1):
                o, us = near[d]
                if dz:
                    o = pltpu.roll(o, (-dz) % SUB, 0)
                    o = jnp.where(sub == (0 if dz < 0 else SUB - 1), 0.0, o)
                    us = [pltpu.roll(x, (-dz) % SUB, 0) for x in us]
                c = (own_e * twice_weight(1 + abs(dz) + abs(d))) * o / (own_e + o)
                for comp in range(3):
                    term = c * (us[comp] - own_u[comp])
                    sums[comp] = term if sums[comp] is None else sums[comp] + term
        for comp in range(3):
            put(comp, sums[comp])

    def rows(ref, k):
        return ref[pl.ds(k, L), :]

    def got(refs, k, axis):
        return choose(odd[axis], rows(refs[0], k), rows(refs[1], k))

    odd = gx % 2, me % 2

    yc[...] = jnp.zeros((LANES, LANES), F32)
    for b in range(2):
        ue = [(b * 3 + c) * L for c in range(3)]
        ee = (6 + b) * L
        for s, (own_x, got_x, own_xe, got_xe) in enumerate(
            ((oxl, (rx1, rx2), exl, (erx1, erx2)), (oxh, (rx2, rx1), exh, (erx2, erx1)))
        ):
            edge(
                rows(own_xe, ee),
                [rows(own_x, k) for k in ue],
                got(got_xe, ee, 0) * ok[s],
                [got(got_x, k, 0) for k in ue],
                None,
                None,
                lambda c, v, s=s, ue=ue: xc.__setitem__((s, pl.ds(ue[c], L), slice(None)), v),
            )
        for s, (got_y, got_ye) in enumerate((((ry1, ry2), (ery1, ery2)), ((ry2, ry1), (ery2, ery1)))):
            corner_ok = jnp.where(lane == 0, ok[0], ok[1]) * ok[2 + s]
            edge(
                rows(ey, s * half + ee),
                [rows(oy, s * half + k) for k in ue],
                got(got_ye, ee, 1) * ok[2 + s],
                [got(got_y, k, 1) for k in ue],
                got(got_ye, ne + ee, 1) * corner_ok,
                [got(got_y, n + k, 1) for k in ue],
                lambda c, v, s=s, ue=ue: yc.__setitem__((pl.ds(s * half + ue[c], L), slice(None)), v),
            )
    ct_s[...] = yc[...].T


def forced(L, X, k, f, face, base, ct, xc, cm_tile):
    lane, sub = lane_ids(), sub_ids()
    half = LANES // 2
    pick = jnp.where(lane == 0, f, jnp.where(lane == LANES - 1, half + f, half - 1))
    force = base + take_lanes(ct, pick)
    if k == 0:
        force = force + jnp.where(sub == 0, xc[0, pl.ds(f, 1), :], 0.0)
    if k == X // SUB - 1:
        force = force + jnp.where(sub == SUB - 1, xc[1, pl.ds(f, 1), :], 0.0)
    if cm_tile is not None:
        force = force + face * cm_tile
    return force


def advance(L, X, last, v_ref, u_ref, rho_ref, forces, ct_s, xc, cm, u1_ref, v1_ref, w_s, sinks, sems):
    nt, half, pad = X // SUB, LANES // 2, X + SUB
    shift_in, shift_out = (pad, 0) if last else (0, pad)
    index = edge_index()
    slot = lane_ids() % half
    if not last:
        w_s[...] = jnp.zeros((X, LANES), F32)

    def layer_of(i, _):
        b, layer = i // L, lax.rem(i, L)
        face = jnp.where(layer == 0, 1.0, 0.0).astype(F32)
        for k in range(nt):
            rr = pl.multiple_of(i * X, X) + k * SUB
            scale = time_step / rho_ref[pl.ds(rr, SUB), :]
            ct = ct_s[pl.ds(k * SUB, SUB), :]
            if not last:
                w = w_s[pl.ds(k * SUB, SUB), :]
            for c in range(3):
                f = (b * 3 + c) * L + layer
                r = pl.multiple_of(f * X, X) + k * SUB
                if len(forces) == 3:
                    base = forces[c][pl.ds(rr, SUB), :]
                else:
                    base = forces[0][pl.ds(r, SUB), :]
                tile = cm[b, pl.ds(k * SUB, SUB), :] if c == 2 else None
                vel = v_ref[pl.ds(r, SUB), :] + scale * forced(L, X, k, f, face, base, ct, xc, tile)
                disp = u_ref[pl.ds(r + shift_in, SUB), :] + time_step * vel
                v1_ref[pl.ds(r, SUB), :] = vel
                u1_ref[pl.ds(r + shift_out, SUB), :] = disp
                if not last:
                    w = jnp.where(slot == f, take_lanes(disp, index), w)
            if not last:
                w_s[pl.ds(k * SUB, SUB), :] = w
        if last:
            for c in range(3):
                at = pl.ds(pl.multiple_of(((b * 3 + c) * L + layer) * X, X), X)
                for s, ref in enumerate((u1_ref, v1_ref)):
                    pltpu.make_async_copy(ref.at[at], sinks[s].at[at], sems.at[s]).start()
        return 0

    lax.fori_loop(0, 2 * L, layer_of, 0)
    if last:
        for s, ref in enumerate((u1_ref, v1_ref)):
            pltpu.make_async_copy(ref, sinks[s], sems.at[s]).wait()


NGOT = 14


def contact_kernel(L, X, GX, NY, n, own_s, row_s, m_ref, gap_ref, v_ref, u_ref, rho_ref, f_ref, *rest):
    gathered, first = rest[:NGOT], rest[NGOT : NGOT + NY]
    cm, ct_s, xc, face_out, whole, grow, work, pairs_ref, yc = rest[NGOT + NY :]
    contact_and_edges(
        L, X, GX, NY, n, first, first, own_s, row_s, m_ref, gathered,
        whole, grow, work, pairs_ref, yc, ct_s, xc, cm,
    )
    for b in range(2):
        f = (b * 3 + 2) * L
        for k in range(X // SUB):
            at = pl.ds(f * X + k * SUB, SUB)
            part = pl.ds(k * SUB, SUB)
            force = forced(L, X, k, f, 1.0, f_ref[at, :], ct_s[part, :], xc, cm[b, part, :])
            scale = time_step / rho_ref[pl.ds(b * L * X + k * SUB, SUB), :]
            disp = u_ref[at, :] + time_step * (v_ref[at, :] + scale * force)
            if b == 1:
                disp = disp + gap_ref[part, :]
            face_out[pl.ds(b * X + k * SUB, SUB), :] = disp


def contact_scratch(L, X, NY):
    vm = pltpu.VMEM
    return [
        vm((NY * X, LANES), F32),
        vm((INTERSECTIONS * X, LANES), F32),
        vm((NY * INTERSECTIONS * X, LANES), F32),
        vm((LANES, LANES), F32),
        vm((LANES, LANES), F32),
    ]


def grant(X, NY):
    return (3 << 20) + 2 * NY * INTERSECTIONS * X * LANES * 4 * max(1, NY // 8)


def contact(L, X, GX, NY, n, args):
    return call(
        functools.partial(contact_kernel, L, X, GX, NY, n),
        [sds(2, X, LANES), sds(X, LANES), sds(2, 6 * L, LANES), sds(2 * X, LANES)],
        args,
        specs=[SMEM] * 2 + [VMEM] * (len(args) - 2),
        scratch=contact_scratch(L, X, NY),
        limit=grant(X, NY),
        flops=60 * NY * INTERSECTIONS * X * LANES,
        name="contact",
    )


def step_kernel(L, X, v_ref, u_ref, rho_ref, f_ref, cm, ct_s, xc, *rest):
    u1_ref, v1_ref, xl_ref, xh_ref, x1_ref, x2_ref, y_ref, w_s = rest
    pad = X + SUB
    advance(L, X, False, v_ref, u_ref, rho_ref, (f_ref,), ct_s, xc, cm, u1_ref, v1_ref, w_s, None, None)
    zero = jnp.zeros((pad, LANES), F32)
    u1_ref[pl.ds(0, pad), :] = zero
    u1_ref[pl.ds(pad + 6 * L * X, pad), :] = zero
    x_rows(L, X, pad, 6, u1_ref, xl_ref, xh_ref, 0)
    pair_rows(lax.axis_index("gx") % 2, xl_ref[...], xh_ref[...], x1_ref, x2_ref)
    y_ref[...] = w_s[...].T


def step(L, X, args):
    R = 6 * L * X
    return call(
        functools.partial(step_kernel, L, X),
        [sds(R + 2 * (X + SUB), LANES), sds(R, LANES)] + [sds(6 * L, LANES)] * 4 + [sds(LANES, LANES)],
        args,
        scratch=[pltpu.VMEM((X, LANES), F32)],
        limit=2 << 20,
        flops=20 * R * LANES,
        name="step",
    )


def last_kernel(L, X, GX, NY, n, own_s, row_s, m_ref, v_ref, u_ref, rho_ref, f0, f1, f2, *rest):
    gathered, rest = rest[:NGOT], rest[NGOT:]
    first, later, rest = rest[:NY], rest[NY : 2 * NY], rest[2 * NY :]
    sinks, scratch = rest[:2], rest[2:]
    whole, grow, work, pairs_ref, yc, ct_s, xc, cm, u1_s, v1_s, sems = scratch
    contact_and_edges(
        L, X, GX, NY, n, first, later, own_s, row_s, m_ref, gathered,
        whole, grow, work, pairs_ref, yc, ct_s, xc, cm,
    )
    advance(
        L, X, True, v_ref, u_ref, rho_ref, (f0, f1, f2), ct_s, xc, cm, u1_s, v1_s, None, sinks, sems
    )


def last_step(L, X, GX, NY, n, args):
    R = 6 * L * X
    vm = pltpu.VMEM
    return call(
        functools.partial(last_kernel, L, X, GX, NY, n),
        [sds(R, LANES), sds(R, LANES)],
        args,
        specs=[SMEM] * 2 + [VMEM] * (len(args) - 2),
        scratch=contact_scratch(L, X, NY)
        + [
            vm((X, LANES), F32),
            vm((2, 6 * L, LANES), F32),
            vm((2, X, LANES), F32),
            vm((R, LANES), F32),
            vm((R, LANES), F32),
            pltpu.SemaphoreType.DMA((2,)),
        ],
        limit=grant(X, NY) + 2 * R * LANES * 4,
        out_spec=pl.BlockSpec(memory_space=pl.ANY),
        flops=80 * R * LANES,
        name="last",
    )


def swap(x, axis="gy"):
    return lax.ppermute(x, axis, [(i, i ^ 1) for i in range(lax.axis_size(axis))])


def cross(x, axis="gy", wrap=False):
    n = lax.axis_size(axis)
    to = [i + 1 if i % 2 else i - 1 for i in range(n)]
    to = [t % n if wrap else min(max(t, 0), n - 1) for t in to]
    return lax.ppermute(x, axis, list(enumerate(to)))


def far(x):
    n = lax.axis_size("gy")
    return [x] + [
        lax.ppermute(x, "gy", [(i, i ^ (2 * k)) for i in range(n)]) for k in range(1, n // 2)
    ]


def both(parts):
    return [p for part in parts for p in (part, swap(part))]


def body(
    displacement,
    velocity,
    modulus,
    density,
    clearance,
    mortar_coupling,
    pair_owner,
    pair_row,
    pair_offset,
    pair_active,
):
    L, X, Y = displacement.shape[2:]
    assert Y == LANES and L == SUB and X == LANES
    GX, NY = lax.axis_size("gx"), lax.axis_size("gy")

    u, v = displacement.reshape(-1, Y), velocity.reshape(-1, Y)
    e, rho = modulus.reshape(-1, Y), density.reshape(-1, Y)
    own, row, off, act = (
        a.transpose(0, 2, 1).reshape(1, -1)
        for a in (pair_owner, pair_row, pair_offset, pair_active)
    )
    parts = far(first_message(u, clearance, (own, row, off, act), L, X))
    xl, xh, x1, x2, y = pack(u, e, L, X)
    rx1, rx2 = swap(x1, "gx"), cross(x2, "gx", True)
    coef, diag = coupling(e, L, X)
    diag, rx1, rx2, *parts = lax.optimization_barrier((diag, rx1, rx2, *parts))
    m1, m2 = corners(8 * L, y, rx1, rx2)
    f = stencil(u, coef, diag, L, X, (0, 1, 2), False, (m1, *parts[1:]))
    stiff = (xl, xh, y, rx1, rx2, swap(m1), cross(m2))
    messages = both(parts)
    cm, ct, xc, face = contact(
        L, X, GX, NY, 8 * L,
        (own, row, mortar_coupling, clearance, v, u, rho, f, *stiff, *stiff, *messages),
    )
    parts = far(face)
    u, v, xl, xh, x1, x2, y = step(L, X, (v, u, rho, f, cm, ct, xc))
    rx1, rx2 = swap(x1, "gx"), cross(x2, "gx", True)
    f0 = stencil(u, coef, diag, L, X, (0,), True)
    f0, rx1, rx2 = lax.optimization_barrier((f0, rx1, rx2))
    m1, m2 = corners(6 * L, y, rx1, rx2)
    f1 = stencil(u, coef, diag, L, X, (1,), True, (m1,))
    f1, *parts = lax.optimization_barrier((f1, *parts))
    f2 = stencil(u, coef, diag, L, X, (2,), True, (f1, *parts[1:]))
    edges = (xl, xh, y, rx1, rx2, swap(m1), cross(m2))
    u, v = last_step(
        L, X, GX, NY, 6 * L,
        (own, row, mortar_coupling, v, u, rho, f0, f1, f2, *edges, *stiff, *messages, *both(parts)),
    )
    return u.reshape(displacement.shape), v.reshape(velocity.shape)


def solution(mesh):
    return jax.shard_map(
        body,
        mesh=mesh,
        in_specs=(
            P(None, None, None, "gx", "gy"),
            P(None, None, None, "gx", "gy"),
            P(None, None, "gx", "gy"),
            P(None, None, "gx", "gy"),
            P("gx", "gy"),
            P(),
            P("gx", "gy", None),
            P("gx", "gy", None),
            P("gx", "gy", None),
            P("gx", "gy", None),
        ),
        out_specs=(P(None, None, None, "gx", "gy"), P(None, None, None, "gx", "gy")),
        check_vma=False,
    )
```

```python
import functools

import jax
import jax.numpy as jnp
from jax import lax
from jax.experimental import pallas as pl
from jax.experimental.pallas import tpu as pltpu
from jax.sharding import PartitionSpec as P

F32 = jnp.float32
BF16 = jnp.bfloat16
INTERSECTIONS = 2
STEPS = 2
time_step = 0.2
penalty_stiffness = 4.0

SUB = 8
LANES = 128
FLAT = [(0, 1, 0), (1, -1, 0), (1, 0, 0), (1, 1, 0)]
SIDE = [(dz, dx, 1) for dz in (-1, 0, 1) for dx in (-1, 0, 1)]
HALF = FLAT + SIDE
NSIDE = len(SIDE)
NHALF = len(HALF)
NCOEF = NHALF + NSIDE

VMEM = pl.BlockSpec(memory_space=pltpu.VMEM)
SMEM = pl.BlockSpec(memory_space=pltpu.SMEM)


def twice_weight(nonzero):
    return 2.0 * 0.5 ** (nonzero - 1)


def lane_ids(rows=SUB):
    return lax.broadcasted_iota(jnp.int32, (rows, LANES), 1)


def sub_ids(rows=SUB):
    return lax.broadcasted_iota(jnp.int32, (rows, LANES), 0)


def take_lanes(values, index):
    return jnp.take_along_axis(values, index, axis=1)


def call(
    kernel, out_shape, args, specs=None, scratch=(), limit=None, flops=0, name=None, out_spec=VMEM
):
    nbytes = sum(a.size * 4 for a in args)
    return pl.pallas_call(
        kernel,
        out_shape=out_shape,
        in_specs=specs or [VMEM] * len(args),
        out_specs=jax.tree.map(lambda _: out_spec, out_shape),
        scratch_shapes=scratch,
        name=name,
        cost_estimate=pl.CostEstimate(flops=flops, bytes_accessed=nbytes, transcendentals=0),
        compiler_params=pltpu.CompilerParams(vmem_limit_bytes=limit),
    )(*args)


def sds(*shape):
    return jax.ShapeDtypeStruct(shape, F32)


def coupling_kernel(L, X, e_ref, c_ref, d_ref, ep, ey):
    rows, pad, nt = 2 * L * X, X + SUB, X // SUB
    zero = jnp.zeros((pad, LANES), F32)
    for s in (ep, ey):
        s[pl.ds(0, pad), :] = zero
        s[pl.ds(pad + rows, pad), :] = zero
    for j in range(NHALF):
        c_ref[j, pl.ds(0, pad), :] = zero
        c_ref[j, pl.ds(pad + rows, pad), :] = zero
    lane, sub = lane_ids(), sub_ids()

    def fill(i, _):
        for k in range(nt):
            r = pl.multiple_of(i * X, X) + k * SUB
            e = e_ref[pl.ds(r, SUB), :]
            ep[pl.ds(r + pad, SUB), :] = e
            ey[pl.ds(r + pad, SUB), :] = jnp.where(
                lane == LANES - 1, 0.0, pltpu.roll(e, LANES - 1, 1)
            )
        return 0

    lax.fori_loop(0, 2 * L, fill, 0)

    def block(i, _):
        layer = lax.rem(i, L)
        up = jnp.where(layer < L - 1, 1.0, 0.0).astype(F32)
        down = jnp.where(layer > 0, 1.0, 0.0).astype(F32)
        for k in range(nt):
            r = pl.multiple_of(i * X, X) + k * SUB + pad
            e = ep[pl.ds(r, SUB), :]
            for j, (dz, dx, dy) in enumerate(HALF):
                o = (ey if dy else ep)[pl.ds(r + dz * X + dx, SUB), :]
                c = (e * twice_weight(abs(dz) + abs(dx) + dy)) * o / (e + o)
                if dz == 1:
                    c = c * up
                if dz == -1:
                    c = c * down
                if dx == 1 and k == nt - 1:
                    c = jnp.where(sub == SUB - 1, 0.0, c)
                if dx == -1 and k == 0:
                    c = jnp.where(sub == 0, 0.0, c)
                c_ref[j, pl.ds(r, SUB), :] = c
                if dy:
                    c_ref[NSIDE + j, pl.ds(r, SUB), :] = pltpu.roll(c, 1, 1)
        return 0

    lax.fori_loop(0, 2 * L, block, 0)

    def total(i, _):
        for k in range(nt):
            r = pl.multiple_of(i * X, X) + k * SUB + pad
            own, back = None, None
            for j, (dz, dx, dy) in enumerate(HALF):
                f = c_ref[j, pl.ds(r, SUB), :]
                b = c_ref[j, pl.ds(r - dz * X - dx, SUB), :]
                own = f if own is None else own + f
                if dy:
                    back = b if back is None else back + b
                else:
                    own = own + b
            d_ref[pl.ds(r - pad, SUB), :] = own + pltpu.roll(back, 1, 1)
        return 0

    lax.fori_loop(0, 2 * L, total, 0)


def coupling(modulus, L, X):
    rows, pad = 2 * L * X, X + SUB
    return call(
        functools.partial(coupling_kernel, L, X),
        [sds(NCOEF, rows + 2 * pad + SUB, LANES), sds(rows, LANES)],
        [modulus],
        scratch=[pltpu.VMEM((rows + 2 * pad, LANES), F32)] * 2,
        limit=5 << 20,
        flops=200 * rows * LANES,
        name="coupling",
    )


def stencil_kernel(L, X, group, comps, padded, u_ref, c_ref, d_ref, *rest):
    pad, nt = X + SUB, X // SUB
    f_ref = rest[-1] if padded else rest[-2]
    if padded:
        up = u_ref
    else:
        up = rest[-1]
        zero = jnp.zeros((pad, LANES), F32)
        up[pl.ds(0, pad), :] = zero
        up[pl.ds(pad + 6 * L * X, pad), :] = zero

        def fill(i, _):
            for k in range(nt):
                r = pl.multiple_of(i * X, X) + k * SUB
                up[pl.ds(r + pad, SUB), :] = u_ref[pl.ds(r, SUB), :]
            return 0

        lax.fori_loop(0, 6 * L, fill, 0)
    count, lowest = len(comps), comps[0]

    def block(i, _):
        which = i // (nt // group)
        first = lax.rem(i, nt // group) * group * SUB
        body = which // count
        bc = body * 3 + lowest + lax.rem(which, count)
        for k in range(group):
            for layer in range(L):
                ru = pl.multiple_of(bc * L * X + layer * X + first, SUB) + k * SUB
                rf = pl.multiple_of(which * L * X + layer * X + first, SUB) + k * SUB
                rc = pl.multiple_of(body * L * X + layer * X + first, SUB) + k * SUB + pad
                t = {
                    (dz, dx): up[pl.ds(ru + pad + dz * X + dx, SUB), :]
                    for dz in (-1, 0, 1)
                    for dx in (-1, 0, 1)
                }
                acc = -d_ref[pl.ds(rc - pad, SUB), :] * t[0, 0]
                ahead, behind = None, None
                for j, (dz, dx, dy) in enumerate(HALF):
                    back = c_ref[j, pl.ds(rc - dz * X - dx, SUB), :] * t[-dz, -dx]
                    near = c_ref[j + NSIDE * dy, pl.ds(rc, SUB), :] * t[dz, dx]
                    if dy:
                        ahead = near if ahead is None else ahead + near
                        behind = back if behind is None else behind + back
                    else:
                        acc = acc + near
                        acc = acc + back
                f_ref[pl.ds(rf, SUB), :] = (
                    acc + pltpu.roll(ahead, LANES - 1, 1) + pltpu.roll(behind, 1, 1)
                )
        return 0

    lax.fori_loop(0, 2 * count * (nt // group), block, 0)


def stencil(u, coef, diag, L, X, comps, padded, after=()):
    pad = X + SUB
    rows = 2 * len(comps) * L * X
    return call(
        functools.partial(stencil_kernel, L, X, 16, comps, padded),
        sds(rows, LANES),
        [u, coef, diag, *after],
        specs=[VMEM] * 3 + [pl.BlockSpec(memory_space=pl.ANY)] * len(after),
        scratch=[] if padded else [pltpu.VMEM((6 * L * X + 2 * pad, LANES), F32)],
        limit=(1 << 20) if padded else (5 << 20),
        flops=60 * rows * LANES,
        name="stencil",
    )


def message_kernel(L, X, u_ref, gap_ref, own, row, off, act, out_ref, tile, gap, words, sems):
    copies = [
        pltpu.make_async_copy(u_ref.at[pl.ds(2 * L * X, X)], out_ref.at[pl.ds(0, X)], sems.at[0]),
        pltpu.make_async_copy(u_ref.at[pl.ds(5 * L * X, X)], tile, sems.at[1]),
        pltpu.make_async_copy(gap_ref, gap, sems.at[2]),
    ]
    small = [
        pltpu.make_async_copy(ref, words.at[pl.ds(k, 1)], sems.at[3 + k])
        for k, ref in enumerate((row, off, act, own))
    ]
    for c in small + copies:
        c.start()
    for c in small:
        c.wait()
    lane = lane_ids()
    for k in range(4):
        halves = [
            jnp.broadcast_to(words[pl.ds(k, 1), pl.ds(h * LANES, LANES)].astype(F32), (SUB, LANES))
            for h in range(INTERSECTIONS)
        ]
        for e in range(INTERSECTIONS):
            index = (lane * INTERSECTIONS + e) & (LANES - 1)
            picked = [take_lanes(x, index) for x in halves]
            value = jnp.where(lane < LANES // INTERSECTIONS, picked[0], picked[1])
            out_ref[pl.ds(2 * X + INTERSECTIONS * k + e, 1), :] = value[:1]
    for c in copies:
        c.wait()
    out_ref[pl.ds(X, X), :] = tile[...] + gap[...]


def first_message(u, clearance, pairs, L, X):
    return call(
        functools.partial(message_kernel, L, X),
        sds(2 * X + 4 * INTERSECTIONS, LANES),
        [u, clearance, *pairs],
        specs=[pl.BlockSpec(memory_space=pl.ANY)] * 6,
        scratch=[
            pltpu.VMEM((X, LANES), F32),
            pltpu.VMEM((X, LANES), F32),
            pltpu.VMEM((4, INTERSECTIONS * X), jnp.int32),
            pltpu.SemaphoreType.DMA((7,)),
        ],
        limit=58 << 20,
        name="message",
    )


def edge_index():
    return jnp.where(lane_ids() < LANES // 2, 0, LANES - 1)


def choose(flag, a, b):
    return jnp.where(jnp.broadcast_to(flag, a.shape) == 1, a, b)


def pair_rows(odd, low, high, first_ref, second_ref):
    first_ref[...] = choose(odd, low, high)
    second_ref[...] = choose(odd, high, low)


def x_rows(L, X, start, count, src, xl_ref, xh_ref, at):
    for bc in range(count):
        base = start + bc * L * X
        xl_ref[pl.ds((at + bc) * L, L), :] = src[pl.ds(base, L, stride=X), :]
        xh_ref[pl.ds((at + bc) * L, L), :] = src[pl.ds(base + X - 1, L, stride=X), :]


def pack_kernel(L, X, u_ref, e_ref, xl_ref, xh_ref, x1_ref, x2_ref, y_ref, w_ref):
    nt = X // SUB
    x_rows(L, X, 0, 6, u_ref, xl_ref, xh_ref, 0)
    x_rows(L, X, 0, 2, e_ref, xl_ref, xh_ref, 6)
    pair_rows(lax.axis_index("gx") % 2, xl_ref[...], xh_ref[...], x1_ref, x2_ref)
    index = edge_index()
    slot = lane_ids() % (LANES // 2)

    def tile(k, _):
        r = pl.multiple_of(k * SUB, SUB)
        w = jnp.zeros((SUB, LANES), F32)
        for f in range(8 * L):
            src, row = (u_ref, f) if f < 6 * L else (e_ref, f - 6 * L)
            v = src[pl.ds(row * X + r, SUB), :]
            w = jnp.where(slot == f, take_lanes(v, index), w)
        w_ref[pl.ds(r, SUB), :] = w
        return 0

    lax.fori_loop(0, nt, tile, 0)
    y_ref[...] = w_ref[...].T


def pack(u, e, L, X):
    return call(
        functools.partial(pack_kernel, L, X),
        [sds(8 * L, LANES)] * 4 + [sds(LANES, LANES)],
        [u, e],
        scratch=[pltpu.VMEM((X, LANES), F32)],
        limit=1 << 20,
        flops=u.size,
        name="pack",
    )


def corner_kernel(n, y_ref, r1_ref, r2_ref, m1_ref, m2_ref):
    half = LANES // 2
    odd_x, odd_y = lax.axis_index("gx") % 2, lax.axis_index("gy") % 2
    lane = lane_ids(n)
    r1, r2 = r1_ref[...], r2_ref[...]
    low, high = choose(odd_x, r1, r2), choose(odd_x, r2, r1)
    left = y_ref[pl.ds(0, n), :], jnp.where(lane == 0, low, pltpu.roll(high, LANES - 1, 1))
    right = y_ref[pl.ds(half, n), :], jnp.where(lane == 0, pltpu.roll(low, 1, 1), high)
    for k in range(2):
        at = pl.ds(k * n, n)
        pair_rows(odd_y, left[k], right[k], m1_ref.at[at], m2_ref.at[at])


def corners(n, y, r1, r2):
    return call(
        functools.partial(corner_kernel, n),
        [sds(2 * n, LANES), sds(2 * n, LANES)],
        [y, r1, r2],
        limit=1 << 20,
        name="corners",
    )


def split(x):
    high = x.astype(BF16)
    return high, (x - high.astype(F32)).astype(BF16)


def wide(x):
    return jnp.concatenate(split(x), axis=1)


def dot(a, b):
    return lax.dot_general(a, b, (((1,), (0,)), ((), ())), preferred_element_type=F32)


def halves(x):
    return x[:, :LANES] + x[:, LANES:]


def project(x, both):
    high, low = split(x)
    return x + (halves(dot(high, both)) + dot(low, both[:, :LANES]))


def pair_tables(L, X, NY, first, index, hot, hot_t, pairs_ref):
    me_f = lax.axis_index("gy").astype(F32)
    pairs_ref[...] = jnp.zeros((LANES, LANES), F32)
    for q in range(NY):
        pairs_ref[pl.ds(q * SUB, SUB), :] = first[q][pl.ds(2 * X, SUB), :]
    columns = pairs_ref[...].T
    lane_t = lane_ids(X)
    node = lax.broadcasted_iota(jnp.int32, (X, X), 0).astype(F32)
    for q in range(NY):
        for e in range(INTERSECTIONS):
            base, s = q * SUB, q * INTERSECTIONS + e
            off = jnp.broadcast_to(columns[:, base + 2 + e : base + 3 + e], (X, LANES))
            index[pl.ds(s * X, X), :] = (lane_t + off.astype(jnp.int32)) & (LANES - 1)
            weight = jnp.where(
                pairs_ref[base + 6 + e : base + 7 + e, :] == me_f,
                pairs_ref[base + 4 + e : base + 5 + e, :],
                0.0,
            )
            mark = jnp.where(node == pairs_ref[base + e : base + e + 1, :], weight, 0.0)
            hot[:, pl.ds(s * X, X)] = mark.astype(BF16)
            hot_t[pl.ds(s * X, X), :] = mark.T.astype(BF16)


def contact_and_edges(
    L, X, GX, NY, n, first, later, own_s, row_s, m_ref, tables, gathered, whole, grow, work, yc, ct_s, xc, cm
):
    oxl, oxh, oy, rx1, rx2, ry1, ry2, exl, exh, ey, erx1, erx2, ery1, ery2 = gathered
    index, hot, hot_t = tables
    nt, half, ne = X // SUB, LANES // 2, 8 * L
    gx, me = lax.axis_index("gx"), lax.axis_index("gy")
    lane, sub = lane_ids(), sub_ids()

    straight = wide(m_ref[...])
    flipped = wide(m_ref[...].T)
    my_chip, my_core = me // 2, me % 2
    for q in range(NY):
        chip = lax.bitwise_xor(my_chip, q // 2)
        core = my_core if q % 2 == 0 else 1 - my_core
        owner = chip * 2 + core
        whole[pl.ds(pl.multiple_of(owner * X, X), X), :] = later[q][pl.ds(0, X), :]

    def gather(i, _):
        for k in range(SUB):
            p = i * SUB + k
            at = own_s[0, p] * X + row_s[0, p]
            to = (k % INTERSECTIONS) * X + i * (SUB // INTERSECTIONS) + k // INTERSECTIONS
            grow[pl.ds(to, 1), :] = whole[pl.ds(at, 1), :]
        return 0

    lax.fori_loop(0, INTERSECTIONS * X // SUB, gather, 0)

    P2 = INTERSECTIONS * X

    def tractions(rows, gap):
        t = jnp.concatenate([gap] * INTERSECTIONS, axis=0) - project(rows, straight)
        return penalty_stiffness * jnp.maximum(0.0, -t)

    slave = None
    t = tractions(take_lanes(grow[...], index[pl.ds(0, P2), :]), later[0][pl.ds(X, X), :])
    active = first[0][pl.ds(2 * X + 2 * INTERSECTIONS, SUB - 2 * INTERSECTIONS), :]
    work[pl.ds(0, LANES), :] = jnp.zeros((LANES, LANES), F32)
    work[pl.ds(0, SUB - 2 * INTERSECTIONS), :] = active
    turned = work[pl.ds(0, LANES), :].T
    for e in range(INTERSECTIONS):
        part = jnp.broadcast_to(turned[:, e : e + 1], (X, LANES)) * t[e * X : (e + 1) * X]
        slave = part if slave is None else slave + part
    cm[1] = slave

    face = wide(later[0][pl.ds(0, X), :])
    for q in range(NY):
        at = pl.ds(q * P2, P2)
        work[at, :] = take_lanes(halves(dot(hot_t[at, :], face)), index[at, :])
    for q in range(NY):
        at = pl.ds(q * P2, P2)
        work[at, :] = tractions(work[at, :], later[q][pl.ds(X, X), :])
    master = None
    lane_2 = 2 * lane_ids(P2)
    for q in range(NY):
        at = pl.ds(q * P2, P2)
        back = project(work[at, :], flipped)
        back = take_lanes(back, (lane_2 - index[at, :]) & (LANES - 1))
        term = dot(hot[:, at], wide(back))
        master = term if master is None else master + term
    cm[0] = -halves(master)

    inside = (gx > 0, gx < GX - 1, me > 0, me < NY - 1)
    ok = [jnp.where(x, 1.0, 0.0).astype(F32) for x in inside]

    def edge(own_e, own_u, near_e, near_u, corner_e, corner_u, put):
        near = {}
        for d in (-1, 0, 1):
            value_e, value_u = near_e, list(near_u)
            if d:
                value_e = pltpu.roll(near_e, (-d) % LANES, 1)
                value_u = [pltpu.roll(x, (-d) % LANES, 1) for x in near_u]
                at = lane == (0 if d < 0 else LANES - 1)
                if corner_e is None:
                    value_e = jnp.where(at, 0.0, value_e)
                else:
                    value_e = jnp.where(at, corner_e, value_e)
                    value_u = [jnp.where(at, c, x) for c, x in zip(corner_u, value_u)]
            near[d] = (value_e, value_u)
        sums = [None] * 3
        for dz in (-1, 0, 1):
            for d in (-1, 0, 1):
                o, us = near[d]
                if dz:
                    o = pltpu.roll(o, (-dz) % SUB, 0)
                    o = jnp.where(sub == (0 if dz < 0 else SUB - 1), 0.0, o)
                    us = [pltpu.roll(x, (-dz) % SUB, 0) for x in us]
                c = (own_e * twice_weight(1 + abs(dz) + abs(d))) * o / (own_e + o)
                for comp in range(3):
                    term = c * (us[comp] - own_u[comp])
                    sums[comp] = term if sums[comp] is None else sums[comp] + term
        for comp in range(3):
            put(comp, sums[comp])

    def rows(ref, k):
        return ref[pl.ds(k, L), :]

    def got(refs, k, axis):
        return choose(odd[axis], rows(refs[0], k), rows(refs[1], k))

    odd = gx % 2, me % 2

    yc[...] = jnp.zeros((LANES, LANES), F32)
    for b in range(2):
        ue = [(b * 3 + c) * L for c in range(3)]
        ee = (6 + b) * L
        for s, (own_x, got_x, own_xe, got_xe) in enumerate(
            ((oxl, (rx1, rx2), exl, (erx1, erx2)), (oxh, (rx2, rx1), exh, (erx2, erx1)))
        ):
            edge(
                rows(own_xe, ee),
                [rows(own_x, k) for k in ue],
                got(got_xe, ee, 0) * ok[s],
                [got(got_x, k, 0) for k in ue],
                None,
                None,
                lambda c, v, s=s, ue=ue: xc.__setitem__((s, pl.ds(ue[c], L), slice(None)), v),
            )
        for s, (got_y, got_ye) in enumerate((((ry1, ry2), (ery1, ery2)), ((ry2, ry1), (ery2, ery1)))):
            corner_ok = jnp.where(lane == 0, ok[0], ok[1]) * ok[2 + s]
            edge(
                rows(ey, s * half + ee),
                [rows(oy, s * half + k) for k in ue],
                got(got_ye, ee, 1) * ok[2 + s],
                [got(got_y, k, 1) for k in ue],
                got(got_ye, ne + ee, 1) * corner_ok,
                [got(got_y, n + k, 1) for k in ue],
                lambda c, v, s=s, ue=ue: yc.__setitem__((pl.ds(s * half + ue[c], L), slice(None)), v),
            )
    ct_s[...] = yc[...].T


def forced(L, X, k, f, face, base, ct, xc, cm_tile):
    lane, sub = lane_ids(), sub_ids()
    half = LANES // 2
    pick = jnp.where(lane == 0, f, jnp.where(lane == LANES - 1, half + f, half - 1))
    force = base + take_lanes(ct, pick)
    if k == 0:
        force = force + jnp.where(sub == 0, xc[0, pl.ds(f, 1), :], 0.0)
    if k == X // SUB - 1:
        force = force + jnp.where(sub == SUB - 1, xc[1, pl.ds(f, 1), :], 0.0)
    if cm_tile is not None:
        force = force + face * cm_tile
    return force


def advance(L, X, last, v_ref, u_ref, rho_ref, forces, ct_s, xc, cm, u1_ref, v1_ref, w_s, sinks, sems):
    nt, half, pad = X // SUB, LANES // 2, X + SUB
    shift_in, shift_out = (pad, 0) if last else (0, pad)
    index = edge_index()
    slot = lane_ids() % half
    if not last:
        w_s[...] = jnp.zeros((X, LANES), F32)

    def layer_of(i, _):
        b, layer = i // L, lax.rem(i, L)
        face = jnp.where(layer == 0, 1.0, 0.0).astype(F32)
        for k in range(nt):
            rr = pl.multiple_of(i * X, X) + k * SUB
            scale = time_step / rho_ref[pl.ds(rr, SUB), :]
            ct = ct_s[pl.ds(k * SUB, SUB), :]
            if not last:
                w = w_s[pl.ds(k * SUB, SUB), :]
            for c in range(3):
                f = (b * 3 + c) * L + layer
                r = pl.multiple_of(f * X, X) + k * SUB
                if len(forces) == 2:
                    fr = pl.multiple_of(((b * 2 + c) if c < 2 else b) * L * X + layer * X, X)
                    base = forces[0 if c < 2 else 1][pl.ds(fr + k * SUB, SUB), :]
                else:
                    base = forces[0][pl.ds(r, SUB), :]
                tile = cm[b, pl.ds(k * SUB, SUB), :] if c == 2 else None
                vel = v_ref[pl.ds(r, SUB), :] + scale * forced(L, X, k, f, face, base, ct, xc, tile)
                disp = u_ref[pl.ds(r + shift_in, SUB), :] + time_step * vel
                v1_ref[pl.ds(r, SUB), :] = vel
                u1_ref[pl.ds(r + shift_out, SUB), :] = disp
                if not last:
                    w = jnp.where(slot == f, take_lanes(disp, index), w)
            if not last:
                w_s[pl.ds(k * SUB, SUB), :] = w
        if last:
            for c in range(3):
                at = pl.ds(pl.multiple_of(((b * 3 + c) * L + layer) * X, X), X)
                for s, ref in enumerate((u1_ref, v1_ref)):
                    pltpu.make_async_copy(ref.at[at], sinks[s].at[at], sems.at[s]).start()
        return 0

    lax.fori_loop(0, 2 * L, layer_of, 0)
    if last:
        for s, ref in enumerate((u1_ref, v1_ref)):
            pltpu.make_async_copy(ref, sinks[s], sems.at[s]).wait()


NGOT = 14


def contact_kernel(L, X, GX, NY, n, own_s, row_s, m_ref, gap_ref, v_ref, u_ref, rho_ref, f_ref, *rest):
    gathered, first = rest[:NGOT], rest[NGOT : NGOT + NY]
    cm, ct_s, xc, face_out, index, hot, hot_t, whole, grow, work, yc = rest[NGOT + NY :]
    tables = index, hot, hot_t
    pair_tables(L, X, NY, first, *tables, yc)
    contact_and_edges(
        L, X, GX, NY, n, first, first, own_s, row_s, m_ref, tables, gathered,
        whole, grow, work, yc, ct_s, xc, cm,
    )
    for b in range(2):
        f = (b * 3 + 2) * L
        for k in range(X // SUB):
            at = pl.ds(f * X + k * SUB, SUB)
            part = pl.ds(k * SUB, SUB)
            force = forced(L, X, k, f, 1.0, f_ref[at, :], ct_s[part, :], xc, cm[b, part, :])
            scale = time_step / rho_ref[pl.ds(b * L * X + k * SUB, SUB), :]
            disp = u_ref[at, :] + time_step * (v_ref[at, :] + scale * force)
            if b == 1:
                disp = disp + gap_ref[part, :]
            face_out[pl.ds(b * X + k * SUB, SUB), :] = disp


def contact_scratch(L, X, NY):
    vm = pltpu.VMEM
    return [
        vm((NY * X, LANES), F32),
        vm((INTERSECTIONS * X, LANES), F32),
        vm((NY * INTERSECTIONS * X, LANES), F32),
        vm((LANES, LANES), F32),
    ]


def grant(X, NY):
    return (3 << 20) + 2 * NY * INTERSECTIONS * X * LANES * 4 * max(1, NY // 8)


def contact(L, X, GX, NY, n, args):
    return call(
        functools.partial(contact_kernel, L, X, GX, NY, n),
        [sds(2, X, LANES), sds(X, LANES), sds(2, 6 * L, LANES), sds(2 * X, LANES)]
        + [
            jax.ShapeDtypeStruct((NY * INTERSECTIONS * X, LANES), jnp.int32),
            jax.ShapeDtypeStruct((X, NY * INTERSECTIONS * X), BF16),
            jax.ShapeDtypeStruct((NY * INTERSECTIONS * X, X), BF16),
        ],
        args,
        specs=[SMEM] * 2 + [VMEM] * (len(args) - 2),
        scratch=contact_scratch(L, X, NY),
        limit=grant(X, NY),
        flops=60 * NY * INTERSECTIONS * X * LANES,
        name="contact",
    )


def step_kernel(L, X, v_ref, u_ref, rho_ref, f_ref, cm, ct_s, xc, *rest):
    u1_ref, v1_ref, xl_ref, xh_ref, x1_ref, x2_ref, y_ref, w_s = rest
    pad = X + SUB
    advance(L, X, False, v_ref, u_ref, rho_ref, (f_ref,), ct_s, xc, cm, u1_ref, v1_ref, w_s, None, None)
    zero = jnp.zeros((pad, LANES), F32)
    u1_ref[pl.ds(0, pad), :] = zero
    u1_ref[pl.ds(pad + 6 * L * X, pad), :] = zero
    x_rows(L, X, pad, 6, u1_ref, xl_ref, xh_ref, 0)
    pair_rows(lax.axis_index("gx") % 2, xl_ref[...], xh_ref[...], x1_ref, x2_ref)
    y_ref[...] = w_s[...].T


def step(L, X, args):
    R = 6 * L * X
    return call(
        functools.partial(step_kernel, L, X),
        [sds(R + 2 * (X + SUB), LANES), sds(R, LANES)] + [sds(6 * L, LANES)] * 4 + [sds(LANES, LANES)],
        args,
        scratch=[pltpu.VMEM((X, LANES), F32)],
        limit=2 << 20,
        flops=20 * R * LANES,
        name="step",
    )


def last_kernel(L, X, GX, NY, n, own_s, row_s, m_ref, v_ref, u_ref, rho_ref, f_ref, g_ref, *rest):
    gathered, rest = rest[:NGOT], rest[NGOT:]
    tables, message, later, rest = rest[:3], rest[3], rest[4 : 4 + NY], rest[4 + NY :]
    sinks, scratch = rest[:2], rest[2:]
    whole, grow, work, yc, ct_s, xc, cm, u1_s, v1_s, sems = scratch
    contact_and_edges(
        L, X, GX, NY, n, (message,), later, own_s, row_s, m_ref, tables, gathered,
        whole, grow, work, yc, ct_s, xc, cm,
    )
    advance(
        L, X, True, v_ref, u_ref, rho_ref, (f_ref, g_ref), ct_s, xc, cm, u1_s, v1_s, None, sinks, sems
    )


def last_step(L, X, GX, NY, n, args):
    R = 6 * L * X
    vm = pltpu.VMEM
    return call(
        functools.partial(last_kernel, L, X, GX, NY, n),
        [sds(R, LANES), sds(R, LANES)],
        args,
        specs=[SMEM] * 2 + [VMEM] * (len(args) - 2),
        scratch=contact_scratch(L, X, NY)
        + [
            vm((X, LANES), F32),
            vm((2, 6 * L, LANES), F32),
            vm((2, X, LANES), F32),
            vm((R, LANES), F32),
            vm((R, LANES), F32),
            pltpu.SemaphoreType.DMA((2,)),
        ],
        limit=grant(X, NY) + 2 * R * LANES * 4,
        out_spec=pl.BlockSpec(memory_space=pl.ANY),
        flops=80 * R * LANES,
        name="last",
    )


def swap(x, axis="gy"):
    return lax.ppermute(x, axis, [(i, i ^ 1) for i in range(lax.axis_size(axis))])


def cross(x, axis="gy"):
    n = lax.axis_size(axis)
    return lax.ppermute(x, axis, [(i, (i + 1) % n if i % 2 else (i - 1) % n) for i in range(n)])


def far(x):
    n = lax.axis_size("gy")
    return [x] + [
        lax.ppermute(x, "gy", [(i, i ^ (2 * k)) for i in range(n)]) for k in range(1, n // 2)
    ]


def both(parts):
    return [p for part in parts for p in (part, swap(part))]


def body(
    displacement,
    velocity,
    modulus,
    density,
    clearance,
    mortar_coupling,
    pair_owner,
    pair_row,
    pair_offset,
    pair_active,
):
    L, X, Y = displacement.shape[2:]
    assert Y == LANES and L == SUB and X == LANES
    GX, NY = lax.axis_size("gx"), lax.axis_size("gy")

    u, v = displacement.reshape(-1, Y), velocity.reshape(-1, Y)
    e, rho = modulus.reshape(-1, Y), density.reshape(-1, Y)
    own, row, off, act = (
        a.transpose(0, 2, 1).reshape(1, -1)
        for a in (pair_owner, pair_row, pair_offset, pair_active)
    )
    parts = far(first_message(u, clearance, (own, row, off, act), L, X))
    xl, xh, x1, x2, y = pack(u, e, L, X)
    rx1, rx2 = swap(x1, "gx"), cross(x2, "gx")
    coef, diag = coupling(e, L, X)
    diag, rx1, rx2, *parts = lax.optimization_barrier((diag, rx1, rx2, *parts))
    m1, m2 = corners(8 * L, y, rx1, rx2)
    f = stencil(u, coef, diag, L, X, (0, 1, 2), False, (m1, *parts[1:]))
    stiff = (xl, xh, y, rx1, rx2, swap(m1), cross(m2))
    messages = both(parts)
    cm, ct, xc, face, *tables = contact(
        L, X, GX, NY, 8 * L,
        (own, row, mortar_coupling, clearance, v, u, rho, f, *stiff, *stiff, *messages),
    )
    parts = far(face)
    u, v, xl, xh, x1, x2, y = step(L, X, (v, u, rho, f, cm, ct, xc))
    rx1, rx2 = swap(x1, "gx"), cross(x2, "gx")
    f = stencil(u, coef, diag, L, X, (0, 1), True)
    f, rx1, rx2, *parts = lax.optimization_barrier((f, rx1, rx2, *parts))
    m1, m2 = corners(6 * L, y, rx1, rx2)
    g = stencil(u, coef, diag, L, X, (2,), True, (m1, f, *parts[1:]))
    edges = (xl, xh, y, rx1, rx2, swap(m1), cross(m2))
    u, v = last_step(
        L, X, GX, NY, 6 * L,
        (own, row, mortar_coupling, v, u, rho, f, g, *edges, *stiff, *tables, messages[0], *both(parts)),
    )
    return u.reshape(displacement.shape), v.reshape(velocity.shape)


def solution(mesh):
    return jax.shard_map(
        body,
        mesh=mesh,
        in_specs=(
            P(None, None, None, "gx", "gy"),
            P(None, None, None, "gx", "gy"),
            P(None, None, "gx", "gy"),
            P(None, None, "gx", "gy"),
            P("gx", "gy"),
            P(),
            P("gx", "gy", None),
            P("gx", "gy", None),
            P("gx", "gy", None),
            P("gx", "gy", None),
        ),
        out_specs=(P(None, None, None, "gx", "gy"), P(None, None, None, "gx", "gy")),
        check_vma=False,
    )
```

```python
import functools

import jax
import jax.numpy as jnp
from jax import lax
from jax.experimental import pallas as pl
from jax.experimental.pallas import tpu as pltpu
from jax.sharding import PartitionSpec as P

F32 = jnp.float32
BF16 = jnp.bfloat16
INTERSECTIONS = 2
STEPS = 2
time_step = 0.2
penalty_stiffness = 4.0

SUB = 8
LANES = 128
FLAT = [(0, 1, 0), (1, -1, 0), (1, 0, 0), (1, 1, 0)]
SIDE = [(dz, dx, 1) for dz in (-1, 0, 1) for dx in (-1, 0, 1)]
HALF = FLAT + SIDE
NSIDE = len(SIDE)
NHALF = len(HALF)
NCOEF = NHALF + NSIDE

VMEM = pl.BlockSpec(memory_space=pltpu.VMEM)
SMEM = pl.BlockSpec(memory_space=pltpu.SMEM)


def twice_weight(nonzero):
    return 2.0 * 0.5 ** (nonzero - 1)


def spaced(X):
    return X + SUB, X + 2 * SUB


def lane_ids(rows=SUB):
    return lax.broadcasted_iota(jnp.int32, (rows, LANES), 1)


def sub_ids(rows=SUB):
    return lax.broadcasted_iota(jnp.int32, (rows, LANES), 0)


def take_lanes(values, index):
    return jnp.take_along_axis(values, index, axis=1)


def call(
    kernel, out_shape, args, specs=None, scratch=(), limit=None, flops=0, name=None, out_spec=VMEM
):
    nbytes = sum(a.size * 4 for a in args)
    return pl.pallas_call(
        kernel,
        out_shape=out_shape,
        in_specs=specs or [VMEM] * len(args),
        out_specs=jax.tree.map(lambda _: out_spec, out_shape),
        scratch_shapes=scratch,
        name=name,
        cost_estimate=pl.CostEstimate(flops=flops, bytes_accessed=nbytes, transcendentals=0),
        compiler_params=pltpu.CompilerParams(vmem_limit_bytes=limit),
    )(*args)


def sds(*shape):
    return jax.ShapeDtypeStruct(shape, F32)


def coupling_kernel(L, X, e_ref, c_ref, d_ref, ep, ey):
    rows, pad, nt = 2 * L * X, X + SUB, X // SUB
    zero = jnp.zeros((pad, LANES), F32)
    for s in (ep, ey):
        s[pl.ds(0, pad), :] = zero
        s[pl.ds(pad + rows, pad), :] = zero
    for j in range(NHALF):
        c_ref[j, pl.ds(0, pad), :] = zero
        c_ref[j, pl.ds(pad + rows, pad), :] = zero
    lane, sub = lane_ids(), sub_ids()

    def fill(i, _):
        for k in range(nt):
            r = pl.multiple_of(i * X, X) + k * SUB
            e = e_ref[pl.ds(r, SUB), :]
            ep[pl.ds(r + pad, SUB), :] = e
            ey[pl.ds(r + pad, SUB), :] = jnp.where(
                lane == LANES - 1, 0.0, pltpu.roll(e, LANES - 1, 1)
            )
        return 0

    lax.fori_loop(0, 2 * L, fill, 0)

    def block(i, _):
        layer = lax.rem(i, L)
        up = jnp.where(layer < L - 1, 1.0, 0.0).astype(F32)
        down = jnp.where(layer > 0, 1.0, 0.0).astype(F32)
        for k in range(nt):
            r = pl.multiple_of(i * X, X) + k * SUB + pad
            e = ep[pl.ds(r, SUB), :]
            for j, (dz, dx, dy) in enumerate(HALF):
                o = (ey if dy else ep)[pl.ds(r + dz * X + dx, SUB), :]
                c = (e * twice_weight(abs(dz) + abs(dx) + dy)) * o / (e + o)
                if dz == 1:
                    c = c * up
                if dz == -1:
                    c = c * down
                if dx == 1 and k == nt - 1:
                    c = jnp.where(sub == SUB - 1, 0.0, c)
                if dx == -1 and k == 0:
                    c = jnp.where(sub == 0, 0.0, c)
                c_ref[j, pl.ds(r, SUB), :] = c
                if dy:
                    c_ref[NSIDE + j, pl.ds(r, SUB), :] = pltpu.roll(c, 1, 1)
        return 0

    lax.fori_loop(0, 2 * L, block, 0)

    def total(i, _):
        for k in range(nt):
            r = pl.multiple_of(i * X, X) + k * SUB + pad
            own, back = None, None
            for j, (dz, dx, dy) in enumerate(HALF):
                f = c_ref[j, pl.ds(r, SUB), :]
                b = c_ref[j, pl.ds(r - dz * X - dx, SUB), :]
                own = f if own is None else own + f
                if dy:
                    back = b if back is None else back + b
                else:
                    own = own + b
            d_ref[pl.ds(r - pad, SUB), :] = own + pltpu.roll(back, 1, 1)
        return 0

    lax.fori_loop(0, 2 * L, total, 0)


def coupling(modulus, L, X):
    rows, pad = 2 * L * X, X + SUB
    return call(
        functools.partial(coupling_kernel, L, X),
        [sds(NCOEF, rows + 2 * pad + SUB, LANES), sds(rows, LANES)],
        [modulus],
        scratch=[pltpu.VMEM((rows + 2 * pad, LANES), F32)] * 2,
        limit=5 << 20,
        flops=200 * rows * LANES,
        name="coupling",
    )


def stencil_kernel(L, X, group, comps, padded, u_ref, c_ref, d_ref, *rest):
    nt = X // SUB
    S, pad = spaced(X)
    f_ref = rest[-1] if padded else rest[-2]
    if padded:
        up = u_ref
    else:
        up = rest[-1]
        zero = jnp.zeros((pad, LANES), F32)
        up[pl.ds(0, pad), :] = zero
        up[pl.ds(pad + 6 * L * S, pad), :] = zero

        def fill(i, _):
            to = pl.multiple_of(i * S, SUB) + pad
            for k in range(nt):
                r = pl.multiple_of(i * X, X) + k * SUB
                up[pl.ds(to + k * SUB, SUB), :] = u_ref[pl.ds(r, SUB), :]
            up[pl.ds(to + X, SUB), :] = jnp.zeros((SUB, LANES), F32)
            return 0

        lax.fori_loop(0, 6 * L, fill, 0)
    count, lowest = len(comps), comps[0]

    def block(i, _):
        which = i // (nt // group)
        first = lax.rem(i, nt // group) * group * SUB
        body = which // count
        bc = body * 3 + lowest + lax.rem(which, count)
        for k in range(group):
            for layer in range(L):
                ru = pl.multiple_of(bc * L * S + layer * S + first, SUB) + k * SUB + pad
                rf = pl.multiple_of(which * L * X + layer * X + first, SUB) + k * SUB
                rd = pl.multiple_of(body * L * X + layer * X + first, SUB) + k * SUB
                rc = rd + X + SUB
                t = {
                    (dz, dx): up[pl.ds(ru + dz * S + dx, SUB), :]
                    for dz in (-1, 0, 1)
                    for dx in (-1, 0, 1)
                }
                acc = -d_ref[pl.ds(rd, SUB), :] * t[0, 0]
                ahead, behind = None, None
                for j, (dz, dx, dy) in enumerate(HALF):
                    back = c_ref[j, pl.ds(rc - dz * X - dx, SUB), :] * t[-dz, -dx]
                    near = c_ref[j + NSIDE * dy, pl.ds(rc, SUB), :] * t[dz, dx]
                    if dy:
                        ahead = near if ahead is None else ahead + near
                        behind = back if behind is None else behind + back
                    else:
                        acc = acc + near
                        acc = acc + back
                f_ref[pl.ds(rf, SUB), :] = (
                    acc + pltpu.roll(ahead, LANES - 1, 1) + pltpu.roll(behind, 1, 1)
                )
        return 0

    lax.fori_loop(0, 2 * count * (nt // group), block, 0)


def stencil(u, coef, diag, L, X, comps, padded, after=()):
    S, pad = spaced(X)
    rows = 2 * len(comps) * L * X
    return call(
        functools.partial(stencil_kernel, L, X, 16, comps, padded),
        sds(rows, LANES),
        [u, coef, diag, *after],
        specs=[VMEM] * 3 + [pl.BlockSpec(memory_space=pl.ANY)] * len(after),
        scratch=[] if padded else [pltpu.VMEM((6 * L * S + 2 * pad, LANES), F32)],
        limit=(1 << 20) if padded else (5 << 20),
        flops=60 * rows * LANES,
        name="stencil",
    )


def message_kernel(L, X, u_ref, gap_ref, own, row, off, act, out_ref, tile, gap, words, sems):
    copies = [
        pltpu.make_async_copy(u_ref.at[pl.ds(2 * L * X, X)], out_ref.at[pl.ds(0, X)], sems.at[0]),
        pltpu.make_async_copy(u_ref.at[pl.ds(5 * L * X, X)], tile, sems.at[1]),
        pltpu.make_async_copy(gap_ref, gap, sems.at[2]),
    ]
    small = [
        pltpu.make_async_copy(ref, words.at[pl.ds(k, 1)], sems.at[3 + k])
        for k, ref in enumerate((row, off, act, own))
    ]
    for c in small + copies:
        c.start()
    for c in small:
        c.wait()
    lane = lane_ids()
    for k in range(4):
        halves = [
            jnp.broadcast_to(words[pl.ds(k, 1), pl.ds(h * LANES, LANES)].astype(F32), (SUB, LANES))
            for h in range(INTERSECTIONS)
        ]
        for e in range(INTERSECTIONS):
            index = (lane * INTERSECTIONS + e) & (LANES - 1)
            picked = [take_lanes(x, index) for x in halves]
            value = jnp.where(lane < LANES // INTERSECTIONS, picked[0], picked[1])
            out_ref[pl.ds(2 * X + INTERSECTIONS * k + e, 1), :] = value[:1]
    for c in copies:
        c.wait()
    out_ref[pl.ds(X, X), :] = tile[...] + gap[...]


def first_message(u, clearance, pairs, L, X):
    return call(
        functools.partial(message_kernel, L, X),
        sds(2 * X + 4 * INTERSECTIONS, LANES),
        [u, clearance, *pairs],
        specs=[pl.BlockSpec(memory_space=pl.ANY)] * 6,
        scratch=[
            pltpu.VMEM((X, LANES), F32),
            pltpu.VMEM((X, LANES), F32),
            pltpu.VMEM((4, INTERSECTIONS * X), jnp.int32),
            pltpu.SemaphoreType.DMA((7,)),
        ],
        limit=58 << 20,
        name="message",
    )


def edge_index():
    return jnp.where(lane_ids() < LANES // 2, 0, LANES - 1)


def choose(flag, a, b):
    return jnp.where(jnp.broadcast_to(flag, a.shape) == 1, a, b)


def pair_rows(odd, low, high, first_ref, second_ref):
    first_ref[...] = choose(odd, low, high)
    second_ref[...] = choose(odd, high, low)


def x_rows(L, X, S, start, count, src, xl_ref, xh_ref, at):
    for bc in range(count):
        base = start + bc * L * S
        xl_ref[pl.ds((at + bc) * L, L), :] = src[pl.ds(base, L, stride=S), :]
        xh_ref[pl.ds((at + bc) * L, L), :] = src[pl.ds(base + X - 1, L, stride=S), :]


def pack_kernel(L, X, u_ref, e_ref, xl_ref, xh_ref, x1_ref, x2_ref, y_ref, w_ref):
    nt = X // SUB
    x_rows(L, X, X, 0, 6, u_ref, xl_ref, xh_ref, 0)
    x_rows(L, X, X, 0, 2, e_ref, xl_ref, xh_ref, 6)
    pair_rows(lax.axis_index("gx") % 2, xl_ref[...], xh_ref[...], x1_ref, x2_ref)
    index = edge_index()
    slot = lane_ids() % (LANES // 2)

    def tile(k, _):
        r = pl.multiple_of(k * SUB, SUB)
        w = jnp.zeros((SUB, LANES), F32)
        for f in range(8 * L):
            src, row = (u_ref, f) if f < 6 * L else (e_ref, f - 6 * L)
            v = src[pl.ds(row * X + r, SUB), :]
            w = jnp.where(slot == f, take_lanes(v, index), w)
        w_ref[pl.ds(r, SUB), :] = w
        return 0

    lax.fori_loop(0, nt, tile, 0)
    y_ref[...] = w_ref[...].T


def pack(u, e, L, X):
    return call(
        functools.partial(pack_kernel, L, X),
        [sds(8 * L, LANES)] * 4 + [sds(LANES, LANES)],
        [u, e],
        scratch=[pltpu.VMEM((X, LANES), F32)],
        limit=1 << 20,
        flops=u.size,
        name="pack",
    )


def corner_kernel(n, y_ref, r1_ref, r2_ref, m1_ref, m2_ref):
    half = LANES // 2
    odd_x, odd_y = lax.axis_index("gx") % 2, lax.axis_index("gy") % 2
    lane = lane_ids(n)
    r1, r2 = r1_ref[...], r2_ref[...]
    low, high = choose(odd_x, r1, r2), choose(odd_x, r2, r1)
    left = y_ref[pl.ds(0, n), :], jnp.where(lane == 0, low, pltpu.roll(high, LANES - 1, 1))
    right = y_ref[pl.ds(half, n), :], jnp.where(lane == 0, pltpu.roll(low, 1, 1), high)
    for k in range(2):
        at = pl.ds(k * n, n)
        pair_rows(odd_y, left[k], right[k], m1_ref.at[at], m2_ref.at[at])


def corners(n, y, r1, r2):
    return call(
        functools.partial(corner_kernel, n),
        [sds(2 * n, LANES), sds(2 * n, LANES)],
        [y, r1, r2],
        limit=1 << 20,
        name="corners",
    )


def split(x):
    high = x.astype(BF16)
    return high, (x - high.astype(F32)).astype(BF16)


def wide(x):
    return jnp.concatenate(split(x), axis=1)


def dot(a, b):
    return lax.dot_general(a, b, (((1,), (0,)), ((), ())), preferred_element_type=F32)


def halves(x):
    return x[:, :LANES] + x[:, LANES:]


def project(x, both):
    high, low = split(x)
    return x + (halves(dot(high, both)) + dot(low, both[:, :LANES]))


def pair_tables(L, X, NY, first, index, hot, hot_t, pairs_ref):
    me_f = lax.axis_index("gy").astype(F32)
    pairs_ref[...] = jnp.zeros((LANES, LANES), F32)
    for q in range(NY):
        pairs_ref[pl.ds(q * SUB, SUB), :] = first[q][pl.ds(2 * X, SUB), :]
    columns = pairs_ref[...].T
    lane_t = lane_ids(X)
    node = lax.broadcasted_iota(jnp.int32, (X, X), 0).astype(F32)
    for q in range(NY):
        for e in range(INTERSECTIONS):
            base, s = q * SUB, q * INTERSECTIONS + e
            off = jnp.broadcast_to(columns[:, base + 2 + e : base + 3 + e], (X, LANES))
            index[pl.ds(s * X, X), :] = (lane_t + off.astype(jnp.int32)) & (LANES - 1)
            weight = jnp.where(
                pairs_ref[base + 6 + e : base + 7 + e, :] == me_f,
                pairs_ref[base + 4 + e : base + 5 + e, :],
                0.0,
            )
            mark = jnp.where(node == pairs_ref[base + e : base + e + 1, :], weight, 0.0)
            hot[:, pl.ds(s * X, X)] = mark.astype(BF16)
            hot_t[pl.ds(s * X, X), :] = mark.T.astype(BF16)


def contact_forces(L, X, NY, first, later, own_s, row_s, m_ref, tables, whole, grow, work, cm):
    index, hot, hot_t = tables
    me = lax.axis_index("gy")
    straight = wide(m_ref[...])
    flipped = wide(m_ref[...].T)
    my_chip, my_core = me // 2, me % 2
    for q in range(NY):
        chip = lax.bitwise_xor(my_chip, q // 2)
        core = my_core if q % 2 == 0 else 1 - my_core
        owner = chip * 2 + core
        whole[pl.ds(pl.multiple_of(owner * X, X), X), :] = later[q][pl.ds(0, X), :]

    def gather(i, _):
        for k in range(SUB):
            p = i * SUB + k
            at = own_s[0, p] * X + row_s[0, p]
            to = (k % INTERSECTIONS) * X + i * (SUB // INTERSECTIONS) + k // INTERSECTIONS
            grow[pl.ds(to, 1), :] = whole[pl.ds(at, 1), :]
        return 0

    lax.fori_loop(0, INTERSECTIONS * X // SUB, gather, 0)

    P2 = INTERSECTIONS * X

    def tractions(rows, gap):
        t = jnp.concatenate([gap] * INTERSECTIONS, axis=0) - project(rows, straight)
        return penalty_stiffness * jnp.maximum(0.0, -t)

    slave = None
    t = tractions(take_lanes(grow[...], index[pl.ds(0, P2), :]), later[0][pl.ds(X, X), :])
    active = first[0][pl.ds(2 * X + 2 * INTERSECTIONS, SUB - 2 * INTERSECTIONS), :]
    work[pl.ds(0, LANES), :] = jnp.zeros((LANES, LANES), F32)
    work[pl.ds(0, SUB - 2 * INTERSECTIONS), :] = active
    turned = work[pl.ds(0, LANES), :].T
    for e in range(INTERSECTIONS):
        part = jnp.broadcast_to(turned[:, e : e + 1], (X, LANES)) * t[e * X : (e + 1) * X]
        slave = part if slave is None else slave + part
    cm[1] = slave

    face = wide(later[0][pl.ds(0, X), :])
    for q in range(NY):
        at = pl.ds(q * P2, P2)
        work[at, :] = take_lanes(halves(dot(hot_t[at, :], face)), index[at, :])
    for q in range(NY):
        at = pl.ds(q * P2, P2)
        work[at, :] = tractions(work[at, :], later[q][pl.ds(X, X), :])
    master = None
    lane_2 = 2 * lane_ids(P2)
    for q in range(NY):
        at = pl.ds(q * P2, P2)
        back = project(work[at, :], flipped)
        back = take_lanes(back, (lane_2 - index[at, :]) & (LANES - 1))
        term = dot(hot[:, at], wide(back))
        master = term if master is None else master + term
    cm[0] = -halves(master)


def edge_forces(L, X, GX, NY, n, gathered, yc, ct_s, xc):
    oxl, oxh, oy, rx1, rx2, ry1, ry2, exl, exh, ey, erx1, erx2, ery1, ery2 = gathered
    half, ne = LANES // 2, 8 * L
    gx, me = lax.axis_index("gx"), lax.axis_index("gy")
    lane, sub = lane_ids(), sub_ids()
    inside = (gx > 0, gx < GX - 1, me > 0, me < NY - 1)
    ok = [jnp.where(x, 1.0, 0.0).astype(F32) for x in inside]

    def edge(own_e, own_u, near_e, near_u, corner_e, corner_u, put):
        near = {}
        for d in (-1, 0, 1):
            value_e, value_u = near_e, list(near_u)
            if d:
                value_e = pltpu.roll(near_e, (-d) % LANES, 1)
                value_u = [pltpu.roll(x, (-d) % LANES, 1) for x in near_u]
                at = lane == (0 if d < 0 else LANES - 1)
                if corner_e is None:
                    value_e = jnp.where(at, 0.0, value_e)
                else:
                    value_e = jnp.where(at, corner_e, value_e)
                    value_u = [jnp.where(at, c, x) for c, x in zip(corner_u, value_u)]
            near[d] = (value_e, value_u)
        sums = [None] * 3
        for dz in (-1, 0, 1):
            for d in (-1, 0, 1):
                o, us = near[d]
                if dz:
                    o = pltpu.roll(o, (-dz) % SUB, 0)
                    o = jnp.where(sub == (0 if dz < 0 else SUB - 1), 0.0, o)
                    us = [pltpu.roll(x, (-dz) % SUB, 0) for x in us]
                c = (own_e * twice_weight(1 + abs(dz) + abs(d))) * o / (own_e + o)
                for comp in range(3):
                    term = c * (us[comp] - own_u[comp])
                    sums[comp] = term if sums[comp] is None else sums[comp] + term
        for comp in range(3):
            put(comp, sums[comp])

    def rows(ref, k):
        return ref[pl.ds(k, L), :]

    def got(refs, k, axis):
        return choose(odd[axis], rows(refs[0], k), rows(refs[1], k))

    odd = gx % 2, me % 2

    yc[...] = jnp.zeros((LANES, LANES), F32)
    for b in range(2):
        ue = [(b * 3 + c) * L for c in range(3)]
        ee = (6 + b) * L
        for s, (own_x, got_x, own_xe, got_xe) in enumerate(
            ((oxl, (rx1, rx2), exl, (erx1, erx2)), (oxh, (rx2, rx1), exh, (erx2, erx1)))
        ):
            edge(
                rows(own_xe, ee),
                [rows(own_x, k) for k in ue],
                got(got_xe, ee, 0) * ok[s],
                [got(got_x, k, 0) for k in ue],
                None,
                None,
                lambda c, v, s=s, ue=ue: xc.__setitem__((s, pl.ds(ue[c], L), slice(None)), v),
            )
        for s, (got_y, got_ye) in enumerate((((ry1, ry2), (ery1, ery2)), ((ry2, ry1), (ery2, ery1)))):
            corner_ok = jnp.where(lane == 0, ok[0], ok[1]) * ok[2 + s]
            edge(
                rows(ey, s * half + ee),
                [rows(oy, s * half + k) for k in ue],
                got(got_ye, ee, 1) * ok[2 + s],
                [got(got_y, k, 1) for k in ue],
                got(got_ye, ne + ee, 1) * corner_ok,
                [got(got_y, n + k, 1) for k in ue],
                lambda c, v, s=s, ue=ue: yc.__setitem__((pl.ds(s * half + ue[c], L), slice(None)), v),
            )
    ct_s[...] = yc[...].T


def forced(L, X, k, f, face, base, ct, xc, cm_tile):
    lane, sub = lane_ids(), sub_ids()
    half = LANES // 2
    pick = jnp.where(lane == 0, f, jnp.where(lane == LANES - 1, half + f, half - 1))
    force = base + take_lanes(ct, pick)
    if k == 0:
        force = force + jnp.where(sub == 0, xc[0, pl.ds(f, 1), :], 0.0)
    if k == X // SUB - 1:
        force = force + jnp.where(sub == SUB - 1, xc[1, pl.ds(f, 1), :], 0.0)
    if cm_tile is not None:
        force = force + face * cm_tile
    return force


def advance(
    L, X, last, v_ref, u_ref, rho_ref, forces, ct_s, xc, cm, u1_ref, v1_ref, w_s, sinks, sems, before_face=None
):
    nt, half = X // SUB, LANES // 2
    S, pad = spaced(X)
    index = edge_index()
    slot = lane_ids() % half
    if not last:
        w_s[...] = jnp.zeros((X, LANES), F32)

    def layer_of(i, _):
        b, layer = i // L, lax.rem(i, L)
        face = jnp.where(layer == 0, 1.0, 0.0).astype(F32)
        for k in range(nt):
            rr = pl.multiple_of(i * X, X) + k * SUB
            scale = time_step / rho_ref[pl.ds(rr, SUB), :]
            ct = ct_s[pl.ds(k * SUB, SUB), :]
            if not last:
                w = w_s[pl.ds(k * SUB, SUB), :]
            for c in range(3):
                f = (b * 3 + c) * L + layer
                r = pl.multiple_of(f * X, X) + k * SUB
                if len(forces) == 2:
                    fr = pl.multiple_of(((b * 2 + c) if c < 2 else b) * L * X + layer * X, X)
                    base = forces[0 if c < 2 else 1][pl.ds(fr + k * SUB, SUB), :]
                else:
                    base = forces[0][pl.ds(r, SUB), :]
                tile = cm[b, pl.ds(k * SUB, SUB), :] if c == 2 and not last else None
                grown = pl.multiple_of(f * S, SUB) + pad + k * SUB
                vel = v_ref[pl.ds(r, SUB), :] + scale * forced(L, X, k, f, face, base, ct, xc, tile)
                disp = u_ref[pl.ds(grown if last else r, SUB), :] + time_step * vel
                v1_ref[pl.ds(r, SUB), :] = vel
                u1_ref[pl.ds(r if last else grown, SUB), :] = disp
                if not last:
                    w = jnp.where(slot == f, take_lanes(disp, index), w)
            if not last:
                w_s[pl.ds(k * SUB, SUB), :] = w
        if last:
            send(b * 3 * L + layer)
            send((b * 3 + 1) * L + layer)
            pl.when(layer > 0)(lambda: send((b * 3 + 2) * L + layer))
        return 0

    def send(f):
        at = pl.ds(pl.multiple_of(f * X, X), X)
        for s, ref in enumerate((u1_ref, v1_ref)):
            pltpu.make_async_copy(ref.at[at], sinks[s].at[at], sems.at[s]).start()

    lax.fori_loop(0, 2 * L, layer_of, 0)
    if last:
        before_face()
        for b in range(2):
            f = (b * 3 + 2) * L
            for k in range(nt):
                at, part = pl.ds(f * X + k * SUB, SUB), pl.ds(k * SUB, SUB)
                rr = pl.ds(b * L * X + k * SUB, SUB)
                force = forced(L, X, k, f, 1.0, forces[-1][rr, :], ct_s[part, :], xc, cm[b, part, :])
                vel = v_ref[at, :] + (time_step / rho_ref[rr, :]) * force
                v1_ref[at, :] = vel
                u1_ref[at, :] = u_ref[pl.ds(pad + f * S + k * SUB, SUB), :] + time_step * vel
            send(f)
        for s, ref in enumerate((u1_ref, v1_ref)):
            pltpu.make_async_copy(ref, sinks[s], sems.at[s]).wait()


NGOT = 14


def contact_kernel(L, X, GX, NY, n, own_s, row_s, m_ref, gap_ref, v_ref, u_ref, rho_ref, f_ref, *rest):
    gathered, first = rest[:NGOT], rest[NGOT : NGOT + NY]
    cm, ct_s, xc, face_out, index, hot, hot_t, whole, grow, work, yc = rest[NGOT + NY :]
    tables = index, hot, hot_t
    pair_tables(L, X, NY, first, *tables, yc)
    contact_forces(L, X, NY, first, first, own_s, row_s, m_ref, tables, whole, grow, work, cm)
    edge_forces(L, X, GX, NY, n, gathered, yc, ct_s, xc)
    for b in range(2):
        f = (b * 3 + 2) * L
        for k in range(X // SUB):
            at = pl.ds(f * X + k * SUB, SUB)
            part = pl.ds(k * SUB, SUB)
            force = forced(L, X, k, f, 1.0, f_ref[at, :], ct_s[part, :], xc, cm[b, part, :])
            scale = time_step / rho_ref[pl.ds(b * L * X + k * SUB, SUB), :]
            disp = u_ref[at, :] + time_step * (v_ref[at, :] + scale * force)
            if b == 1:
                disp = disp + gap_ref[part, :]
            face_out[pl.ds(b * X + k * SUB, SUB), :] = disp


def contact_scratch(L, X, NY):
    vm = pltpu.VMEM
    return [
        vm((NY * X, LANES), F32),
        vm((INTERSECTIONS * X, LANES), F32),
        vm((NY * INTERSECTIONS * X, LANES), F32),
        vm((LANES, LANES), F32),
    ]


def grant(X, NY):
    return (3 << 20) + 2 * NY * INTERSECTIONS * X * LANES * 4 * max(1, NY // 8)


def contact(L, X, GX, NY, n, args):
    return call(
        functools.partial(contact_kernel, L, X, GX, NY, n),
        [sds(2, X, LANES), sds(X, LANES), sds(2, 6 * L, LANES), sds(2 * X, LANES)]
        + [
            jax.ShapeDtypeStruct((NY * INTERSECTIONS * X, LANES), jnp.int32),
            jax.ShapeDtypeStruct((X, NY * INTERSECTIONS * X), BF16),
            jax.ShapeDtypeStruct((NY * INTERSECTIONS * X, X), BF16),
        ],
        args,
        specs=[SMEM] * 2 + [VMEM] * (len(args) - 2),
        scratch=contact_scratch(L, X, NY),
        limit=grant(X, NY),
        flops=60 * NY * INTERSECTIONS * X * LANES,
        name="contact",
    )


def step_kernel(L, X, v_ref, u_ref, rho_ref, f_ref, cm, ct_s, xc, *rest):
    u1_ref, v1_ref, xl_ref, xh_ref, x1_ref, x2_ref, y_ref, w_s = rest
    S, pad = spaced(X)
    advance(L, X, False, v_ref, u_ref, rho_ref, (f_ref,), ct_s, xc, cm, u1_ref, v1_ref, w_s, None, None)
    zero = jnp.zeros((pad, LANES), F32)
    u1_ref[pl.ds(0, pad), :] = zero
    u1_ref[pl.ds(pad + 6 * L * S, pad), :] = zero
    for f in range(6 * L):
        u1_ref[pl.ds(pad + f * S + X, SUB), :] = zero[:SUB]
    x_rows(L, X, S, pad, 6, u1_ref, xl_ref, xh_ref, 0)
    pair_rows(lax.axis_index("gx") % 2, xl_ref[...], xh_ref[...], x1_ref, x2_ref)
    y_ref[...] = w_s[...].T


def step(L, X, args):
    R = 6 * L * X
    S, pad = spaced(X)
    return call(
        functools.partial(step_kernel, L, X),
        [sds(6 * L * S + 2 * pad, LANES), sds(R, LANES)] + [sds(6 * L, LANES)] * 4 + [sds(LANES, LANES)],
        args,
        scratch=[pltpu.VMEM((X, LANES), F32)],
        limit=2 << 20,
        flops=20 * R * LANES,
        name="step",
    )


def last_kernel(L, X, GX, NY, n, own_s, row_s, m_ref, v_ref, u_ref, rho_ref, f_ref, g_ref, *rest):
    gathered, rest = rest[:NGOT], rest[NGOT:]
    tables, message, later, rest = rest[:3], rest[3], rest[4 : 4 + NY], rest[4 + NY :]
    sinks, scratch = rest[:2], rest[2:]
    whole, grow, work, yc, ct_s, xc, cm, u1_s, v1_s, sems = scratch
    edge_forces(L, X, GX, NY, n, gathered, yc, ct_s, xc)
    advance(
        L, X, True, v_ref, u_ref, rho_ref, (f_ref, g_ref), ct_s, xc, cm, u1_s, v1_s, None, sinks, sems,
        lambda: contact_forces(
            L, X, NY, (message,), later, own_s, row_s, m_ref, tables, whole, grow, work, cm
        ),
    )


def last_step(L, X, GX, NY, n, args):
    R = 6 * L * X
    vm = pltpu.VMEM
    return call(
        functools.partial(last_kernel, L, X, GX, NY, n),
        [sds(R, LANES), sds(R, LANES)],
        args,
        specs=[SMEM] * 2 + [VMEM] * (len(args) - 2),
        scratch=contact_scratch(L, X, NY)
        + [
            vm((X, LANES), F32),
            vm((2, 6 * L, LANES), F32),
            vm((2, X, LANES), F32),
            vm((R, LANES), F32),
            vm((R, LANES), F32),
            pltpu.SemaphoreType.DMA((2,)),
        ],
        limit=grant(X, NY) + 2 * R * LANES * 4,
        out_spec=pl.BlockSpec(memory_space=pl.ANY),
        flops=80 * R * LANES,
        name="last",
    )


def swap(x, axis="gy"):
    return lax.ppermute(x, axis, [(i, i ^ 1) for i in range(lax.axis_size(axis))])


def cross(x, axis="gy"):
    n = lax.axis_size(axis)
    return lax.ppermute(x, axis, [(i, (i + 1) % n if i % 2 else (i - 1) % n) for i in range(n)])


def far(x):
    n = lax.axis_size("gy")
    return [x] + [
        lax.ppermute(x, "gy", [(i, i ^ (2 * k)) for i in range(n)]) for k in range(1, n // 2)
    ]


def both(parts):
    return [p for part in parts for p in (part, swap(part))]


def body(
    displacement,
    velocity,
    modulus,
    density,
    clearance,
    mortar_coupling,
    pair_owner,
    pair_row,
    pair_offset,
    pair_active,
):
    L, X, Y = displacement.shape[2:]
    assert Y == LANES and L == SUB and X == LANES
    GX, NY = lax.axis_size("gx"), lax.axis_size("gy")

    u, v = displacement.reshape(-1, Y), velocity.reshape(-1, Y)
    e, rho = modulus.reshape(-1, Y), density.reshape(-1, Y)
    own, row, off, act = (
        a.transpose(0, 2, 1).reshape(1, -1)
        for a in (pair_owner, pair_row, pair_offset, pair_active)
    )
    parts = far(first_message(u, clearance, (own, row, off, act), L, X))
    xl, xh, x1, x2, y = pack(u, e, L, X)
    rx1, rx2 = swap(x1, "gx"), cross(x2, "gx")
    coef, diag = coupling(e, L, X)
    diag, rx1, rx2, *parts = lax.optimization_barrier((diag, rx1, rx2, *parts))
    m1, m2 = corners(8 * L, y, rx1, rx2)
    f = stencil(u, coef, diag, L, X, (0, 1, 2), False, (m1, *parts[1:]))
    stiff = (xl, xh, y, rx1, rx2, swap(m1), cross(m2))
    messages = both(parts)
    cm, ct, xc, face, *tables = contact(
        L, X, GX, NY, 8 * L,
        (own, row, mortar_coupling, clearance, v, u, rho, f, *stiff, *stiff, *messages),
    )
    parts = far(face)
    u, v, xl, xh, x1, x2, y = step(L, X, (v, u, rho, f, cm, ct, xc))
    rx1, rx2 = swap(x1, "gx"), cross(x2, "gx")
    f = stencil(u, coef, diag, L, X, (0, 1), True)
    f, rx1, rx2, *parts = lax.optimization_barrier((f, rx1, rx2, *parts))
    m1, m2 = corners(6 * L, y, rx1, rx2)
    g = stencil(u, coef, diag, L, X, (2,), True, (m1, f, *parts[1:]))
    edges = (xl, xh, y, rx1, rx2, swap(m1), cross(m2))
    u, v = last_step(
        L, X, GX, NY, 6 * L,
        (own, row, mortar_coupling, v, u, rho, f, g, *edges, *stiff, *tables, messages[0], *both(parts)),
    )
    return u.reshape(displacement.shape), v.reshape(velocity.shape)


def solution(mesh):
    return jax.shard_map(
        body,
        mesh=mesh,
        in_specs=(
            P(None, None, None, "gx", "gy"),
            P(None, None, None, "gx", "gy"),
            P(None, None, "gx", "gy"),
            P(None, None, "gx", "gy"),
            P("gx", "gy"),
            P(),
            P("gx", "gy", None),
            P("gx", "gy", None),
            P("gx", "gy", None),
            P("gx", "gy", None),
        ),
        out_specs=(P(None, None, None, "gx", "gy"), P(None, None, None, "gx", "gy")),
        check_vma=False,
    )
```

```python
import functools

import jax
import jax.numpy as jnp
from jax import lax
from jax.experimental import pallas as pl
from jax.experimental.pallas import tpu as pltpu
from jax.sharding import PartitionSpec as P

F32 = jnp.float32
BF16 = jnp.bfloat16
INTERSECTIONS = 2
STEPS = 2
time_step = 0.2
penalty_stiffness = 4.0

SUB = 8
LANES = 128
FLAT = [(0, 1, 0), (1, -1, 0), (1, 0, 0), (1, 1, 0)]
SIDE = [(dz, dx, 1) for dz in (-1, 0, 1) for dx in (-1, 0, 1)]
HALF = FLAT + SIDE
NSIDE = len(SIDE)
NHALF = len(HALF)
NCOEF = NHALF + NSIDE

VMEM = pl.BlockSpec(memory_space=pltpu.VMEM)
SMEM = pl.BlockSpec(memory_space=pltpu.SMEM)


def twice_weight(nonzero):
    return 2.0 * 0.5 ** (nonzero - 1)


def lane_ids(rows=SUB):
    return lax.broadcasted_iota(jnp.int32, (rows, LANES), 1)


def sub_ids(rows=SUB):
    return lax.broadcasted_iota(jnp.int32, (rows, LANES), 0)


def take_lanes(values, index):
    return jnp.take_along_axis(values, index, axis=1)


def call(
    kernel, out_shape, args, specs=None, scratch=(), limit=None, flops=0, name=None, out_spec=VMEM
):
    nbytes = sum(a.size * 4 for a in args)
    return pl.pallas_call(
        kernel,
        out_shape=out_shape,
        in_specs=specs or [VMEM] * len(args),
        out_specs=jax.tree.map(lambda _: out_spec, out_shape),
        scratch_shapes=scratch,
        name=name,
        cost_estimate=pl.CostEstimate(flops=flops, bytes_accessed=nbytes, transcendentals=0),
        compiler_params=pltpu.CompilerParams(vmem_limit_bytes=limit),
    )(*args)


def sds(*shape):
    return jax.ShapeDtypeStruct(shape, F32)


def coupling_kernel(L, X, e_ref, c_ref, d_ref, ep, ey):
    rows, pad, nt = 2 * L * X, X + SUB, X // SUB
    zero = jnp.zeros((pad, LANES), F32)
    for s in (ep, ey):
        s[pl.ds(0, pad), :] = zero
        s[pl.ds(pad + rows, pad), :] = zero
    for j in range(NHALF):
        c_ref[j, pl.ds(0, pad), :] = zero
        c_ref[j, pl.ds(pad + rows, pad), :] = zero
    lane, sub = lane_ids(), sub_ids()

    def fill(i, _):
        for k in range(nt):
            r = pl.multiple_of(i * X, X) + k * SUB
            e = e_ref[pl.ds(r, SUB), :]
            ep[pl.ds(r + pad, SUB), :] = e
            ey[pl.ds(r + pad, SUB), :] = jnp.where(
                lane == LANES - 1, 0.0, pltpu.roll(e, LANES - 1, 1)
            )
        return 0

    lax.fori_loop(0, 2 * L, fill, 0)

    def block(i, _):
        layer = lax.rem(i, L)
        up = jnp.where(layer < L - 1, 1.0, 0.0).astype(F32)
        down = jnp.where(layer > 0, 1.0, 0.0).astype(F32)
        for k in range(nt):
            r = pl.multiple_of(i * X, X) + k * SUB + pad
            e = ep[pl.ds(r, SUB), :]
            for j, (dz, dx, dy) in enumerate(HALF):
                o = (ey if dy else ep)[pl.ds(r + dz * X + dx, SUB), :]
                c = (e * twice_weight(abs(dz) + abs(dx) + dy)) * o / (e + o)
                if dz == 1:
                    c = c * up
                if dz == -1:
                    c = c * down
                if dx == 1 and k == nt - 1:
                    c = jnp.where(sub == SUB - 1, 0.0, c)
                if dx == -1 and k == 0:
                    c = jnp.where(sub == 0, 0.0, c)
                c_ref[j, pl.ds(r, SUB), :] = c
                if dy:
                    c_ref[NSIDE + j, pl.ds(r, SUB), :] = pltpu.roll(c, 1, 1)
        return 0

    lax.fori_loop(0, 2 * L, block, 0)

    def total(i, _):
        for k in range(nt):
            r = pl.multiple_of(i * X, X) + k * SUB + pad
            own, back = None, None
            for j, (dz, dx, dy) in enumerate(HALF):
                f = c_ref[j, pl.ds(r, SUB), :]
                b = c_ref[j, pl.ds(r - dz * X - dx, SUB), :]
                own = f if own is None else own + f
                if dy:
                    back = b if back is None else back + b
                else:
                    own = own + b
            d_ref[pl.ds(r - pad, SUB), :] = own + pltpu.roll(back, 1, 1)
        return 0

    lax.fori_loop(0, 2 * L, total, 0)


def coupling(modulus, L, X):
    rows, pad = 2 * L * X, X + SUB
    return call(
        functools.partial(coupling_kernel, L, X),
        [sds(NCOEF, rows + 2 * pad + SUB, LANES), sds(rows, LANES)],
        [modulus],
        scratch=[pltpu.VMEM((rows + 2 * pad, LANES), F32)] * 2,
        limit=5 << 20,
        flops=200 * rows * LANES,
        name="coupling",
    )


def spaced(X):
    return X + SUB, X + 2 * SUB


def stencil_kernel(L, X, group, comps, u_ref, c_ref, d_ref, *rest):
    f_ref, up = rest[-2:]
    nt, count, lowest = X // SUB, len(comps), comps[0]
    S, pad = spaced(X)
    zero = jnp.zeros((pad, LANES), F32)
    up[pl.ds(0, pad), :] = zero
    up[pl.ds(pad + 2 * count * L * S, pad), :] = zero

    def field(which):
        return which // count * 3 + lowest + lax.rem(which, count)

    def fill(i, _):
        source = field(i // L) * L + lax.rem(i, L)
        to = pl.multiple_of(i * S, SUB) + pad
        for k in range(nt):
            r = pl.multiple_of(source * X, X) + k * SUB
            up[pl.ds(to + k * SUB, SUB), :] = u_ref[pl.ds(r, SUB), :]
        up[pl.ds(to + X, SUB), :] = jnp.zeros((SUB, LANES), F32)
        return 0

    lax.fori_loop(0, 2 * count * L, fill, 0)

    def block(i, _):
        which = i // (nt // group)
        first = lax.rem(i, nt // group) * group * SUB
        body = which // count
        for k in range(group):
            for layer in range(L):
                ru = pl.multiple_of(which * L * S + layer * S + first, SUB) + k * SUB + pad
                rf = pl.multiple_of(which * L * X + layer * X + first, SUB) + k * SUB
                rd = pl.multiple_of(body * L * X + layer * X + first, SUB) + k * SUB
                rc = rd + X + SUB
                t = {
                    (dz, dx): up[pl.ds(ru + dz * S + dx, SUB), :]
                    for dz in (-1, 0, 1)
                    for dx in (-1, 0, 1)
                }
                acc = -d_ref[pl.ds(rd, SUB), :] * t[0, 0]
                ahead, behind = None, None
                for j, (dz, dx, dy) in enumerate(HALF):
                    back = c_ref[j, pl.ds(rc - dz * X - dx, SUB), :] * t[-dz, -dx]
                    near = c_ref[j + NSIDE * dy, pl.ds(rc, SUB), :] * t[dz, dx]
                    if dy:
                        ahead = near if ahead is None else ahead + near
                        behind = back if behind is None else behind + back
                    else:
                        acc = acc + near
                        acc = acc + back
                f_ref[pl.ds(rf, SUB), :] = (
                    acc + pltpu.roll(ahead, LANES - 1, 1) + pltpu.roll(behind, 1, 1)
                )
        return 0

    lax.fori_loop(0, 2 * count * (nt // group), block, 0)


def stencil(u, coef, diag, L, X, comps, after=()):
    S, pad = spaced(X)
    rows = 2 * len(comps) * L * X
    return call(
        functools.partial(stencil_kernel, L, X, X // SUB, comps),
        sds(rows, LANES),
        [u, coef, diag, *after],
        specs=[VMEM] * 3 + [pl.BlockSpec(memory_space=pl.ANY)] * len(after),
        scratch=[pltpu.VMEM((2 * len(comps) * L * S + 2 * pad, LANES), F32)],
        limit=5 << 20,
        flops=60 * rows * LANES,
        name="stencil",
    )


def message_kernel(L, X, u_ref, gap_ref, own, row, off, act, out_ref, tile, gap, words, sems):
    copies = [
        pltpu.make_async_copy(u_ref.at[pl.ds(2 * L * X, X)], out_ref.at[pl.ds(0, X)], sems.at[0]),
        pltpu.make_async_copy(u_ref.at[pl.ds(5 * L * X, X)], tile, sems.at[1]),
        pltpu.make_async_copy(gap_ref, gap, sems.at[2]),
    ]
    small = [
        pltpu.make_async_copy(ref, words.at[pl.ds(k, 1)], sems.at[3 + k])
        for k, ref in enumerate((row, off, act, own))
    ]
    for c in small + copies:
        c.start()
    for c in small:
        c.wait()
    lane = lane_ids()
    for k in range(4):
        halves = [
            jnp.broadcast_to(words[pl.ds(k, 1), pl.ds(h * LANES, LANES)].astype(F32), (SUB, LANES))
            for h in range(INTERSECTIONS)
        ]
        for e in range(INTERSECTIONS):
            index = (lane * INTERSECTIONS + e) & (LANES - 1)
            picked = [take_lanes(x, index) for x in halves]
            value = jnp.where(lane < LANES // INTERSECTIONS, picked[0], picked[1])
            out_ref[pl.ds(2 * X + INTERSECTIONS * k + e, 1), :] = value[:1]
    for c in copies:
        c.wait()
    out_ref[pl.ds(X, X), :] = tile[...] + gap[...]


def first_message(u, clearance, pairs, L, X):
    return call(
        functools.partial(message_kernel, L, X),
        sds(2 * X + 4 * INTERSECTIONS, LANES),
        [u, clearance, *pairs],
        specs=[pl.BlockSpec(memory_space=pl.ANY)] * 6,
        scratch=[
            pltpu.VMEM((X, LANES), F32),
            pltpu.VMEM((X, LANES), F32),
            pltpu.VMEM((4, INTERSECTIONS * X), jnp.int32),
            pltpu.SemaphoreType.DMA((7,)),
        ],
        limit=58 << 20,
        name="message",
    )


def edge_index():
    return jnp.where(lane_ids() < LANES // 2, 0, LANES - 1)


def choose(flag, a, b):
    return jnp.where(jnp.broadcast_to(flag, a.shape) == 1, a, b)


def pair_rows(odd, low, high, first_ref, second_ref):
    first_ref[...] = choose(odd, low, high)
    second_ref[...] = choose(odd, high, low)


def x_rows(L, X, start, count, src, xl_ref, xh_ref, at):
    for bc in range(count):
        base = start + bc * L * X
        xl_ref[pl.ds((at + bc) * L, L), :] = src[pl.ds(base, L, stride=X), :]
        xh_ref[pl.ds((at + bc) * L, L), :] = src[pl.ds(base + X - 1, L, stride=X), :]


def pack_kernel(L, X, u_ref, e_ref, xl_ref, xh_ref, x1_ref, x2_ref, y_ref, w_ref):
    nt = X // SUB
    x_rows(L, X, 0, 6, u_ref, xl_ref, xh_ref, 0)
    x_rows(L, X, 0, 2, e_ref, xl_ref, xh_ref, 6)
    pair_rows(lax.axis_index("gx") % 2, xl_ref[...], xh_ref[...], x1_ref, x2_ref)
    index = edge_index()
    slot = lane_ids() % (LANES // 2)

    def tile(k, _):
        r = pl.multiple_of(k * SUB, SUB)
        w = jnp.zeros((SUB, LANES), F32)
        for f in range(8 * L):
            src, row = (u_ref, f) if f < 6 * L else (e_ref, f - 6 * L)
            v = src[pl.ds(row * X + r, SUB), :]
            w = jnp.where(slot == f, take_lanes(v, index), w)
        w_ref[pl.ds(r, SUB), :] = w
        return 0

    lax.fori_loop(0, nt, tile, 0)
    y_ref[...] = w_ref[...].T


def pack(u, e, L, X):
    return call(
        functools.partial(pack_kernel, L, X),
        [sds(8 * L, LANES)] * 4 + [sds(LANES, LANES)],
        [u, e],
        scratch=[pltpu.VMEM((X, LANES), F32)],
        limit=1 << 20,
        flops=u.size,
        name="pack",
    )


def corner_kernel(n, y_ref, r1_ref, r2_ref, m1_ref, m2_ref):
    half = LANES // 2
    odd_x, odd_y = lax.axis_index("gx") % 2, lax.axis_index("gy") % 2
    lane = lane_ids(n)
    r1, r2 = r1_ref[...], r2_ref[...]
    low, high = choose(odd_x, r1, r2), choose(odd_x, r2, r1)
    left = y_ref[pl.ds(0, n), :], jnp.where(lane == 0, low, pltpu.roll(high, LANES - 1, 1))
    right = y_ref[pl.ds(half, n), :], jnp.where(lane == 0, pltpu.roll(low, 1, 1), high)
    for k in range(2):
        at = pl.ds(k * n, n)
        pair_rows(odd_y, left[k], right[k], m1_ref.at[at], m2_ref.at[at])


def corners(n, y, r1, r2):
    return call(
        functools.partial(corner_kernel, n),
        [sds(2 * n, LANES), sds(2 * n, LANES)],
        [y, r1, r2],
        limit=1 << 20,
        name="corners",
    )


def split(x):
    high = x.astype(BF16)
    return high, (x - high.astype(F32)).astype(BF16)


def dot(a, b, dims=((1,), (0,))):
    return lax.dot_general(a, b, (dims, ((), ())), preferred_element_type=F32)


def project(x, pair, dims):
    high, low = split(x)
    return x + (dot(high, pair[0], dims) + dot(high, pair[1], dims) + dot(low, pair[0], dims))


def contact_and_edges(L, X, GX, NY, n, first, later, own_s, row_s, m_ref, gathered, whole, grow, work, pairs_ref, yc, ct_s, xc, cm):
    oxl, oxh, oy, rx1, rx2, ry1, ry2, exl, exh, ey, erx1, erx2, ery1, ery2 = gathered
    nt, half, ne = X // SUB, LANES // 2, 8 * L
    gx, me = lax.axis_index("gx"), lax.axis_index("gy")
    lane, sub = lane_ids(), sub_ids()
    lane_t = lane_ids(X)

    mh, ml = split(m_ref[...])
    straight, flipped = ((1,), (0,)), ((1,), (1,))
    pairs_ref[...] = jnp.zeros((LANES, LANES), F32)
    for q in range(NY):
        pairs_ref[pl.ds(q * SUB, SUB), :] = first[q][pl.ds(2 * X, SUB), :]
    columns = pairs_ref[...].T
    my_chip, my_core = me // 2, me % 2
    for q in range(NY):
        chip = lax.bitwise_xor(my_chip, q // 2)
        core = my_core if q % 2 == 0 else 1 - my_core
        owner = chip * 2 + core
        whole[pl.ds(pl.multiple_of(owner * X, X), X), :] = later[q][pl.ds(0, X), :]

    def gather(i, _):
        for k in range(SUB):
            p = i * SUB + k
            at = own_s[0, p] * X + row_s[0, p]
            to = (k % INTERSECTIONS) * X + i * (SUB // INTERSECTIONS) + k // INTERSECTIONS
            grow[pl.ds(to, 1), :] = whole[pl.ds(at, 1), :]
        return 0

    lax.fori_loop(0, INTERSECTIONS * X // SUB, gather, 0)

    def column(f):
        return jnp.broadcast_to(columns[:, f : f + 1], (X, LANES))

    slave = None
    for e in range(INTERSECTIONS):
        off = column(2 + e).astype(jnp.int32)
        moved = take_lanes(grow[pl.ds(e * X, X), :], (lane_t + off) & (LANES - 1))
        gap = later[0][pl.ds(X, X), :] - project(moved, (mh, ml), straight)
        t = column(4 + e) * (penalty_stiffness * jnp.maximum(0.0, -gap))
        slave = t if slave is None else slave + t
    cm[1] = slave

    fh, fl = split(later[0][pl.ds(0, X), :])
    me_f = me.astype(F32)
    node = lax.broadcasted_iota(jnp.int32, (X, X), 0).astype(F32)
    master = jnp.zeros((X, LANES), F32)
    blocks = [(q, e) for q in range(NY) for e in range(INTERSECTIONS)]
    for s, (q, e) in enumerate(blocks):
        base = q * SUB
        hot = jnp.where(node == pairs_ref[base + e : base + e + 1, :], 1.0, 0.0).astype(BF16)
        rows = dot(hot, fh, ((0,), (0,))) + dot(hot, fl, ((0,), (0,)))
        off = column(base + 2 + e).astype(jnp.int32)
        work[pl.ds(s * X, X), :] = take_lanes(rows, (lane_t + off) & (LANES - 1))
    for s, (q, e) in enumerate(blocks):
        gap = later[q][pl.ds(X, X), :] - project(
            work[pl.ds(s * X, X), :], (mh, ml), straight
        )
        work[pl.ds(s * X, X), :] = penalty_stiffness * jnp.maximum(0.0, -gap)
    for s, (q, e) in enumerate(blocks):
        base = q * SUB
        back = project(work[pl.ds(s * X, X), :], (mh, ml), flipped)
        off = column(base + 2 + e).astype(jnp.int32)
        work[pl.ds(s * X, X), :] = take_lanes(back, (lane_t - off) & (LANES - 1))
    for s, (q, e) in enumerate(blocks):
        base = q * SUB
        weight = jnp.where(
            pairs_ref[base + 6 + e : base + 7 + e, :] == me_f,
            pairs_ref[base + 4 + e : base + 5 + e, :],
            0.0,
        )
        hot = jnp.where(node == pairs_ref[base + e : base + e + 1, :], weight, 0.0).astype(BF16)
        bh, bl = split(work[pl.ds(s * X, X), :])
        master = master + (dot(hot, bh) + dot(hot, bl))
    cm[0] = -master

    inside = (gx > 0, gx < GX - 1, me > 0, me < NY - 1)
    ok = [jnp.where(x, 1.0, 0.0).astype(F32) for x in inside]

    def edge(own_e, own_u, near_e, near_u, corner_e, corner_u, put):
        near = {}
        for d in (-1, 0, 1):
            value_e, value_u = near_e, list(near_u)
            if d:
                value_e = pltpu.roll(near_e, (-d) % LANES, 1)
                value_u = [pltpu.roll(x, (-d) % LANES, 1) for x in near_u]
                at = lane == (0 if d < 0 else LANES - 1)
                if corner_e is None:
                    value_e = jnp.where(at, 0.0, value_e)
                else:
                    value_e = jnp.where(at, corner_e, value_e)
                    value_u = [jnp.where(at, c, x) for c, x in zip(corner_u, value_u)]
            near[d] = (value_e, value_u)
        sums = [None] * 3
        for dz in (-1, 0, 1):
            for d in (-1, 0, 1):
                o, us = near[d]
                if dz:
                    o = pltpu.roll(o, (-dz) % SUB, 0)
                    o = jnp.where(sub == (0 if dz < 0 else SUB - 1), 0.0, o)
                    us = [pltpu.roll(x, (-dz) % SUB, 0) for x in us]
                c = (own_e * twice_weight(1 + abs(dz) + abs(d))) * o / (own_e + o)
                for comp in range(3):
                    term = c * (us[comp] - own_u[comp])
                    sums[comp] = term if sums[comp] is None else sums[comp] + term
        for comp in range(3):
            put(comp, sums[comp])

    def rows(ref, k):
        return ref[pl.ds(k, L), :]

    def got(refs, k, axis):
        return choose(odd[axis], rows(refs[0], k), rows(refs[1], k))

    odd = gx % 2, me % 2

    yc[...] = jnp.zeros((LANES, LANES), F32)
    for b in range(2):
        ue = [(b * 3 + c) * L for c in range(3)]
        ee = (6 + b) * L
        for s, (own_x, got_x, own_xe, got_xe) in enumerate(
            ((oxl, (rx1, rx2), exl, (erx1, erx2)), (oxh, (rx2, rx1), exh, (erx2, erx1)))
        ):
            edge(
                rows(own_xe, ee),
                [rows(own_x, k) for k in ue],
                got(got_xe, ee, 0) * ok[s],
                [got(got_x, k, 0) for k in ue],
                None,
                None,
                lambda c, v, s=s, ue=ue: xc.__setitem__((s, pl.ds(ue[c], L), slice(None)), v),
            )
        for s, (got_y, got_ye) in enumerate((((ry1, ry2), (ery1, ery2)), ((ry2, ry1), (ery2, ery1)))):
            corner_ok = jnp.where(lane == 0, ok[0], ok[1]) * ok[2 + s]
            edge(
                rows(ey, s * half + ee),
                [rows(oy, s * half + k) for k in ue],
                got(got_ye, ee, 1) * ok[2 + s],
                [got(got_y, k, 1) for k in ue],
                got(got_ye, ne + ee, 1) * corner_ok,
                [got(got_y, n + k, 1) for k in ue],
                lambda c, v, s=s, ue=ue: yc.__setitem__((pl.ds(s * half + ue[c], L), slice(None)), v),
            )
    ct_s[...] = yc[...].T


def forced(L, X, k, f, face, base, ct, xc, cm_tile):
    lane, sub = lane_ids(), sub_ids()
    half = LANES // 2
    pick = jnp.where(lane == 0, f, jnp.where(lane == LANES - 1, half + f, half - 1))
    force = base + take_lanes(ct, pick)
    if k == 0:
        force = force + jnp.where(sub == 0, xc[0, pl.ds(f, 1), :], 0.0)
    if k == X // SUB - 1:
        force = force + jnp.where(sub == SUB - 1, xc[1, pl.ds(f, 1), :], 0.0)
    if cm_tile is not None:
        force = force + face * cm_tile
    return force


def advance(L, X, last, v_ref, u_ref, rho_ref, forces, ct_s, xc, cm, u1_ref, v1_ref, w_s, sinks, sems):
    nt, half = X // SUB, LANES // 2
    index = edge_index()
    slot = lane_ids() % half
    if not last:
        w_s[...] = jnp.zeros((X, LANES), F32)

    def layer_of(i, _):
        b, layer = i // L, lax.rem(i, L)
        face = jnp.where(layer == 0, 1.0, 0.0).astype(F32)
        for k in range(nt):
            rr = pl.multiple_of(i * X, X) + k * SUB
            scale = time_step / rho_ref[pl.ds(rr, SUB), :]
            ct = ct_s[pl.ds(k * SUB, SUB), :]
            if not last:
                w = w_s[pl.ds(k * SUB, SUB), :]
            for c in range(3):
                f = (b * 3 + c) * L + layer
                r = pl.multiple_of(f * X, X) + k * SUB
                if len(forces) == 2:
                    fr = pl.multiple_of(((b * 2 + c) if c < 2 else b) * L * X + layer * X, X)
                    base = forces[0 if c < 2 else 1][pl.ds(fr + k * SUB, SUB), :]
                else:
                    base = forces[0][pl.ds(r, SUB), :]
                tile = cm[b, pl.ds(k * SUB, SUB), :] if c == 2 else None
                vel = v_ref[pl.ds(r, SUB), :] + scale * forced(L, X, k, f, face, base, ct, xc, tile)
                disp = u_ref[pl.ds(r, SUB), :] + time_step * vel
                v1_ref[pl.ds(r, SUB), :] = vel
                u1_ref[pl.ds(r, SUB), :] = disp
                if not last:
                    w = jnp.where(slot == f, take_lanes(disp, index), w)
            if not last:
                w_s[pl.ds(k * SUB, SUB), :] = w
        if last:
            for c in range(3):
                at = pl.ds(pl.multiple_of(((b * 3 + c) * L + layer) * X, X), X)
                for s, ref in enumerate((u1_ref, v1_ref)):
                    pltpu.make_async_copy(ref.at[at], sinks[s].at[at], sems.at[s]).start()
        return 0

    lax.fori_loop(0, 2 * L, layer_of, 0)
    if last:
        for s, ref in enumerate((u1_ref, v1_ref)):
            pltpu.make_async_copy(ref, sinks[s], sems.at[s]).wait()


NGOT = 14


def contact_kernel(L, X, GX, NY, n, own_s, row_s, m_ref, gap_ref, v_ref, u_ref, rho_ref, f_ref, *rest):
    gathered, first = rest[:NGOT], rest[NGOT : NGOT + NY]
    cm, ct_s, xc, face_out, whole, grow, work, pairs_ref, yc = rest[NGOT + NY :]
    contact_and_edges(
        L, X, GX, NY, n, first, first, own_s, row_s, m_ref, gathered,
        whole, grow, work, pairs_ref, yc, ct_s, xc, cm,
    )
    for b in range(2):
        f = (b * 3 + 2) * L
        for k in range(X // SUB):
            at = pl.ds(f * X + k * SUB, SUB)
            part = pl.ds(k * SUB, SUB)
            force = forced(L, X, k, f, 1.0, f_ref[at, :], ct_s[part, :], xc, cm[b, part, :])
            scale = time_step / rho_ref[pl.ds(b * L * X + k * SUB, SUB), :]
            disp = u_ref[at, :] + time_step * (v_ref[at, :] + scale * force)
            if b == 1:
                disp = disp + gap_ref[part, :]
            face_out[pl.ds(b * X + k * SUB, SUB), :] = disp


def contact_scratch(L, X, NY):
    vm = pltpu.VMEM
    return [
        vm((NY * X, LANES), F32),
        vm((INTERSECTIONS * X, LANES), F32),
        vm((NY * INTERSECTIONS * X, LANES), F32),
        vm((LANES, LANES), F32),
        vm((LANES, LANES), F32),
    ]


def grant(X, NY):
    return (3 << 20) + 2 * NY * INTERSECTIONS * X * LANES * 4 * max(1, NY // 8)


def contact(L, X, GX, NY, n, args):
    return call(
        functools.partial(contact_kernel, L, X, GX, NY, n),
        [sds(2, X, LANES), sds(X, LANES), sds(2, 6 * L, LANES), sds(2 * X, LANES)],
        args,
        specs=[SMEM] * 2 + [VMEM] * (len(args) - 2),
        scratch=contact_scratch(L, X, NY),
        limit=grant(X, NY),
        flops=60 * NY * INTERSECTIONS * X * LANES,
        name="contact",
    )


def step_kernel(L, X, v_ref, u_ref, rho_ref, f_ref, cm, ct_s, xc, *rest):
    u1_ref, v1_ref, xl_ref, xh_ref, x1_ref, x2_ref, y_ref, w_s = rest
    advance(L, X, False, v_ref, u_ref, rho_ref, (f_ref,), ct_s, xc, cm, u1_ref, v1_ref, w_s, None, None)
    x_rows(L, X, 0, 6, u1_ref, xl_ref, xh_ref, 0)
    pair_rows(lax.axis_index("gx") % 2, xl_ref[...], xh_ref[...], x1_ref, x2_ref)
    y_ref[...] = w_s[...].T


def step(L, X, args):
    R = 6 * L * X
    return call(
        functools.partial(step_kernel, L, X),
        [sds(R, LANES), sds(R, LANES)] + [sds(6 * L, LANES)] * 4 + [sds(LANES, LANES)],
        args,
        scratch=[pltpu.VMEM((X, LANES), F32)],
        limit=2 << 20,
        flops=20 * R * LANES,
        name="step",
    )


def last_kernel(L, X, GX, NY, n, own_s, row_s, m_ref, v_ref, u_ref, rho_ref, f_ref, g_ref, *rest):
    gathered, rest = rest[:NGOT], rest[NGOT:]
    first, later, rest = rest[:NY], rest[NY : 2 * NY], rest[2 * NY :]
    sinks, scratch = rest[:2], rest[2:]
    whole, grow, work, pairs_ref, yc, ct_s, xc, cm, u1_s, v1_s, sems = scratch
    contact_and_edges(
        L, X, GX, NY, n, first, later, own_s, row_s, m_ref, gathered,
        whole, grow, work, pairs_ref, yc, ct_s, xc, cm,
    )
    advance(
        L, X, True, v_ref, u_ref, rho_ref, (f_ref, g_ref), ct_s, xc, cm, u1_s, v1_s, None, sinks, sems
    )


def last_step(L, X, GX, NY, n, args):
    R = 6 * L * X
    vm = pltpu.VMEM
    return call(
        functools.partial(last_kernel, L, X, GX, NY, n),
        [sds(R, LANES), sds(R, LANES)],
        args,
        specs=[SMEM] * 2 + [VMEM] * (len(args) - 2),
        scratch=contact_scratch(L, X, NY)
        + [
            vm((X, LANES), F32),
            vm((2, 6 * L, LANES), F32),
            vm((2, X, LANES), F32),
            vm((R, LANES), F32),
            vm((R, LANES), F32),
            pltpu.SemaphoreType.DMA((2,)),
        ],
        limit=grant(X, NY) + 2 * R * LANES * 4,
        out_spec=pl.BlockSpec(memory_space=pl.ANY),
        flops=80 * R * LANES,
        name="last",
    )


def swap(x, axis="gy"):
    return lax.ppermute(x, axis, [(i, i ^ 1) for i in range(lax.axis_size(axis))])


def cross(x, axis="gy"):
    n = lax.axis_size(axis)
    return lax.ppermute(x, axis, [(i, (i + 1) % n if i % 2 else (i - 1) % n) for i in range(n)])


def far(x):
    n = lax.axis_size("gy")
    return [x] + [
        lax.ppermute(x, "gy", [(i, i ^ (2 * k)) for i in range(n)]) for k in range(1, n // 2)
    ]


def both(parts):
    return [p for part in parts for p in (part, swap(part))]


def body(
    displacement,
    velocity,
    modulus,
    density,
    clearance,
    mortar_coupling,
    pair_owner,
    pair_row,
    pair_offset,
    pair_active,
):
    L, X, Y = displacement.shape[2:]
    assert Y == LANES and L == SUB and X == LANES
    GX, NY = lax.axis_size("gx"), lax.axis_size("gy")

    u, v = displacement.reshape(-1, Y), velocity.reshape(-1, Y)
    e, rho = modulus.reshape(-1, Y), density.reshape(-1, Y)
    own, row, off, act = (
        a.transpose(0, 2, 1).reshape(1, -1)
        for a in (pair_owner, pair_row, pair_offset, pair_active)
    )
    parts = far(first_message(u, clearance, (own, row, off, act), L, X))
    xl, xh, x1, x2, y = pack(u, e, L, X)
    rx1, rx2 = swap(x1, "gx"), cross(x2, "gx")
    coef, diag = coupling(e, L, X)
    diag, rx1, rx2, *parts = lax.optimization_barrier((diag, rx1, rx2, *parts))
    m1, m2 = corners(8 * L, y, rx1, rx2)
    f = stencil(u, coef, diag, L, X, (0, 1, 2), (m1, *parts[1:]))
    stiff = (xl, xh, y, rx1, rx2, swap(m1), cross(m2))
    messages = both(parts)
    cm, ct, xc, face = contact(
        L, X, GX, NY, 8 * L,
        (own, row, mortar_coupling, clearance, v, u, rho, f, *stiff, *stiff, *messages),
    )
    parts = far(face)
    u, v, xl, xh, x1, x2, y = step(L, X, (v, u, rho, f, cm, ct, xc))
    rx1, rx2 = swap(x1, "gx"), cross(x2, "gx")
    f = stencil(u, coef, diag, L, X, (0, 1))
    f, rx1, rx2, *parts = lax.optimization_barrier((f, rx1, rx2, *parts))
    m1, m2 = corners(6 * L, y, rx1, rx2)
    g = stencil(u, coef, diag, L, X, (2,), (m1, f, *parts[1:]))
    edges = (xl, xh, y, rx1, rx2, swap(m1), cross(m2))
    u, v = last_step(
        L, X, GX, NY, 6 * L,
        (own, row, mortar_coupling, v, u, rho, f, g, *edges, *stiff, *messages, *both(parts)),
    )
    return u.reshape(displacement.shape), v.reshape(velocity.shape)


def solution(mesh):
    return jax.shard_map(
        body,
        mesh=mesh,
        in_specs=(
            P(None, None, None, "gx", "gy"),
            P(None, None, None, "gx", "gy"),
            P(None, None, "gx", "gy"),
            P(None, None, "gx", "gy"),
            P("gx", "gy"),
            P(),
            P("gx", "gy", None),
            P("gx", "gy", None),
            P("gx", "gy", None),
            P("gx", "gy", None),
        ),
        out_specs=(P(None, None, None, "gx", "gy"), P(None, None, None, "gx", "gy")),
        check_vma=False,
    )
```

```python
import functools

import jax
import jax.numpy as jnp
from jax import lax
from jax.experimental import pallas as pl
from jax.experimental.pallas import tpu as pltpu
from jax.sharding import PartitionSpec as P

F32 = jnp.float32
BF16 = jnp.bfloat16
INTERSECTIONS = 2
STEPS = 2
time_step = 0.2
penalty_stiffness = 4.0

SUB = 8
LANES = 128
FLAT = [(0, 1, 0), (1, -1, 0), (1, 0, 0), (1, 1, 0)]
SIDE = [(dz, dx, 1) for dz in (-1, 0, 1) for dx in (-1, 0, 1)]
HALF = FLAT + SIDE
NSIDE = len(SIDE)
NHALF = len(HALF)
NCOEF = NHALF + NSIDE

VMEM = pl.BlockSpec(memory_space=pltpu.VMEM)
SMEM = pl.BlockSpec(memory_space=pltpu.SMEM)


def twice_weight(nonzero):
    return 2.0 * 0.5 ** (nonzero - 1)


def lane_ids(rows=SUB):
    return lax.broadcasted_iota(jnp.int32, (rows, LANES), 1)


def sub_ids(rows=SUB):
    return lax.broadcasted_iota(jnp.int32, (rows, LANES), 0)


def take_lanes(values, index):
    return jnp.take_along_axis(values, index, axis=1)


def call(
    kernel, out_shape, args, specs=None, scratch=(), limit=None, flops=0, name=None, out_spec=VMEM
):
    nbytes = sum(a.size * 4 for a in args)
    return pl.pallas_call(
        kernel,
        out_shape=out_shape,
        in_specs=specs or [VMEM] * len(args),
        out_specs=jax.tree.map(lambda _: out_spec, out_shape),
        scratch_shapes=scratch,
        name=name,
        cost_estimate=pl.CostEstimate(flops=flops, bytes_accessed=nbytes, transcendentals=0),
        compiler_params=pltpu.CompilerParams(vmem_limit_bytes=limit),
    )(*args)


def sds(*shape):
    return jax.ShapeDtypeStruct(shape, F32)


def coupling_kernel(L, X, e_ref, c_ref, d_ref, ep, ey):
    rows, pad, nt = 2 * L * X, X + SUB, X // SUB
    zero = jnp.zeros((pad, LANES), F32)
    for s in (ep, ey):
        s[pl.ds(0, pad), :] = zero
        s[pl.ds(pad + rows, pad), :] = zero
    for j in range(NHALF):
        c_ref[j, pl.ds(0, pad), :] = zero
        c_ref[j, pl.ds(pad + rows, pad), :] = zero
    lane, sub = lane_ids(), sub_ids()

    def fill(i, _):
        for k in range(nt):
            r = pl.multiple_of(i * X, X) + k * SUB
            e = e_ref[pl.ds(r, SUB), :]
            ep[pl.ds(r + pad, SUB), :] = e
            ey[pl.ds(r + pad, SUB), :] = jnp.where(
                lane == LANES - 1, 0.0, pltpu.roll(e, LANES - 1, 1)
            )
        return 0

    lax.fori_loop(0, 2 * L, fill, 0)

    def block(i, _):
        layer = lax.rem(i, L)
        up = jnp.where(layer < L - 1, 1.0, 0.0).astype(F32)
        down = jnp.where(layer > 0, 1.0, 0.0).astype(F32)
        for k in range(nt):
            r = pl.multiple_of(i * X, X) + k * SUB + pad
            e = ep[pl.ds(r, SUB), :]
            for j, (dz, dx, dy) in enumerate(HALF):
                o = (ey if dy else ep)[pl.ds(r + dz * X + dx, SUB), :]
                c = (e * twice_weight(abs(dz) + abs(dx) + dy)) * o / (e + o)
                if dz == 1:
                    c = c * up
                if dz == -1:
                    c = c * down
                if dx == 1 and k == nt - 1:
                    c = jnp.where(sub == SUB - 1, 0.0, c)
                if dx == -1 and k == 0:
                    c = jnp.where(sub == 0, 0.0, c)
                c_ref[j, pl.ds(r, SUB), :] = c
                if dy:
                    c_ref[NSIDE + j, pl.ds(r, SUB), :] = pltpu.roll(c, 1, 1)
        return 0

    lax.fori_loop(0, 2 * L, block, 0)

    def total(i, _):
        for k in range(nt):
            r = pl.multiple_of(i * X, X) + k * SUB + pad
            own, back = None, None
            for j, (dz, dx, dy) in enumerate(HALF):
                f = c_ref[j, pl.ds(r, SUB), :]
                b = c_ref[j, pl.ds(r - dz * X - dx, SUB), :]
                own = f if own is None else own + f
                if dy:
                    back = b if back is None else back + b
                else:
                    own = own + b
            d_ref[pl.ds(r - pad, SUB), :] = own + pltpu.roll(back, 1, 1)
        return 0

    lax.fori_loop(0, 2 * L, total, 0)


def coupling(modulus, L, X):
    rows, pad = 2 * L * X, X + SUB
    return call(
        functools.partial(coupling_kernel, L, X),
        [sds(NCOEF, rows + 2 * pad + SUB, LANES), sds(rows, LANES)],
        [modulus],
        scratch=[pltpu.VMEM((rows + 2 * pad, LANES), F32)] * 2,
        limit=5 << 20,
        flops=200 * rows * LANES,
        name="coupling",
    )


def spaced(X):
    return X + SUB, X + 2 * SUB


def stencil_kernel(L, X, group, comps, u_ref, c_ref, d_ref, *rest):
    f_ref, up = rest[-2:]
    nt, count, lowest = X // SUB, len(comps), comps[0]
    S, pad = spaced(X)
    zero = jnp.zeros((pad, LANES), F32)
    up[pl.ds(0, pad), :] = zero
    up[pl.ds(pad + 2 * count * L * S, pad), :] = zero

    def field(which):
        return which // count * 3 + lowest + lax.rem(which, count)

    def fill(i, _):
        source = field(i // L) * L + lax.rem(i, L)
        to = pl.multiple_of(i * S, SUB) + pad
        for k in range(nt):
            r = pl.multiple_of(source * X, X) + k * SUB
            up[pl.ds(to + k * SUB, SUB), :] = u_ref[pl.ds(r, SUB), :]
        up[pl.ds(to + X, SUB), :] = jnp.zeros((SUB, LANES), F32)
        return 0

    lax.fori_loop(0, 2 * count * L, fill, 0)

    def block(i, _):
        which = i // (nt // group)
        first = lax.rem(i, nt // group) * group * SUB
        body = which // count
        for k in range(group):
            for layer in range(L):
                ru = pl.multiple_of(which * L * S + layer * S + first, SUB) + k * SUB + pad
                rf = pl.multiple_of(which * L * X + layer * X + first, SUB) + k * SUB
                rd = pl.multiple_of(body * L * X + layer * X + first, SUB) + k * SUB
                rc = rd + X + SUB
                t = {
                    (dz, dx): up[pl.ds(ru + dz * S + dx, SUB), :]
                    for dz in (-1, 0, 1)
                    for dx in (-1, 0, 1)
                }
                acc = -d_ref[pl.ds(rd, SUB), :] * t[0, 0]
                ahead, behind = None, None
                for j, (dz, dx, dy) in enumerate(HALF):
                    back = c_ref[j, pl.ds(rc - dz * X - dx, SUB), :] * t[-dz, -dx]
                    near = c_ref[j + NSIDE * dy, pl.ds(rc, SUB), :] * t[dz, dx]
                    if dy:
                        ahead = near if ahead is None else ahead + near
                        behind = back if behind is None else behind + back
                    else:
                        acc = acc + near
                        acc = acc + back
                f_ref[pl.ds(rf, SUB), :] = (
                    acc + pltpu.roll(ahead, LANES - 1, 1) + pltpu.roll(behind, 1, 1)
                )
        return 0

    lax.fori_loop(0, 2 * count * (nt // group), block, 0)


def stencil(u, coef, diag, L, X, comps, after=()):
    S, pad = spaced(X)
    rows = 2 * len(comps) * L * X
    return call(
        functools.partial(stencil_kernel, L, X, X // SUB, comps),
        sds(rows, LANES),
        [u, coef, diag, *after],
        specs=[VMEM] * 3 + [pl.BlockSpec(memory_space=pl.ANY)] * len(after),
        scratch=[pltpu.VMEM((2 * len(comps) * L * S + 2 * pad, LANES), F32)],
        limit=5 << 20,
        flops=60 * rows * LANES,
        name="stencil",
    )


def message_kernel(L, X, u_ref, gap_ref, own, row, off, act, out_ref, tile, gap, words, sems):
    copies = [
        pltpu.make_async_copy(u_ref.at[pl.ds(2 * L * X, X)], out_ref.at[pl.ds(0, X)], sems.at[0]),
        pltpu.make_async_copy(u_ref.at[pl.ds(5 * L * X, X)], tile, sems.at[1]),
        pltpu.make_async_copy(gap_ref, gap, sems.at[2]),
    ]
    small = [
        pltpu.make_async_copy(ref, words.at[pl.ds(k, 1)], sems.at[3 + k])
        for k, ref in enumerate((row, off, act, own))
    ]
    for c in small + copies:
        c.start()
    for c in small:
        c.wait()
    lane = lane_ids()
    for k in range(4):
        halves = [
            jnp.broadcast_to(words[pl.ds(k, 1), pl.ds(h * LANES, LANES)].astype(F32), (SUB, LANES))
            for h in range(INTERSECTIONS)
        ]
        for e in range(INTERSECTIONS):
            index = (lane * INTERSECTIONS + e) & (LANES - 1)
            picked = [take_lanes(x, index) for x in halves]
            value = jnp.where(lane < LANES // INTERSECTIONS, picked[0], picked[1])
            out_ref[pl.ds(2 * X + INTERSECTIONS * k + e, 1), :] = value[:1]
    for c in copies:
        c.wait()
    out_ref[pl.ds(X, X), :] = tile[...] + gap[...]


def first_message(u, clearance, pairs, L, X):
    return call(
        functools.partial(message_kernel, L, X),
        sds(2 * X + 4 * INTERSECTIONS, LANES),
        [u, clearance, *pairs],
        specs=[pl.BlockSpec(memory_space=pl.ANY)] * 6,
        scratch=[
            pltpu.VMEM((X, LANES), F32),
            pltpu.VMEM((X, LANES), F32),
            pltpu.VMEM((4, INTERSECTIONS * X), jnp.int32),
            pltpu.SemaphoreType.DMA((7,)),
        ],
        limit=58 << 20,
        name="message",
    )


def edge_index():
    return jnp.where(lane_ids() < LANES // 2, 0, LANES - 1)


def choose(flag, a, b):
    return jnp.where(jnp.broadcast_to(flag, a.shape) == 1, a, b)


def pair_rows(odd, low, high, first_ref, second_ref):
    first_ref[...] = choose(odd, low, high)
    second_ref[...] = choose(odd, high, low)


def x_rows(L, X, start, count, src, xl_ref, xh_ref, at):
    for bc in range(count):
        base = start + bc * L * X
        xl_ref[pl.ds((at + bc) * L, L), :] = src[pl.ds(base, L, stride=X), :]
        xh_ref[pl.ds((at + bc) * L, L), :] = src[pl.ds(base + X - 1, L, stride=X), :]


def pack_kernel(L, X, u_ref, e_ref, xl_ref, xh_ref, x1_ref, x2_ref, y_ref, w_ref):
    nt = X // SUB
    x_rows(L, X, 0, 6, u_ref, xl_ref, xh_ref, 0)
    x_rows(L, X, 0, 2, e_ref, xl_ref, xh_ref, 6)
    pair_rows(lax.axis_index("gx") % 2, xl_ref[...], xh_ref[...], x1_ref, x2_ref)
    index = edge_index()
    slot = lane_ids() % (LANES // 2)

    def tile(k, _):
        r = pl.multiple_of(k * SUB, SUB)
        w = jnp.zeros((SUB, LANES), F32)
        for f in range(8 * L):
            src, row = (u_ref, f) if f < 6 * L else (e_ref, f - 6 * L)
            v = src[pl.ds(row * X + r, SUB), :]
            w = jnp.where(slot == f, take_lanes(v, index), w)
        w_ref[pl.ds(r, SUB), :] = w
        return 0

    lax.fori_loop(0, nt, tile, 0)
    y_ref[...] = w_ref[...].T


def pack(u, e, L, X):
    return call(
        functools.partial(pack_kernel, L, X),
        [sds(8 * L, LANES)] * 4 + [sds(LANES, LANES)],
        [u, e],
        scratch=[pltpu.VMEM((X, LANES), F32)],
        limit=1 << 20,
        flops=u.size,
        name="pack",
    )


def corner_kernel(n, y_ref, r1_ref, r2_ref, m1_ref, m2_ref):
    half = LANES // 2
    odd_x, odd_y = lax.axis_index("gx") % 2, lax.axis_index("gy") % 2
    lane = lane_ids(n)
    r1, r2 = r1_ref[...], r2_ref[...]
    low, high = choose(odd_x, r1, r2), choose(odd_x, r2, r1)
    left = y_ref[pl.ds(0, n), :], jnp.where(lane == 0, low, pltpu.roll(high, LANES - 1, 1))
    right = y_ref[pl.ds(half, n), :], jnp.where(lane == 0, pltpu.roll(low, 1, 1), high)
    for k in range(2):
        at = pl.ds(k * n, n)
        pair_rows(odd_y, left[k], right[k], m1_ref.at[at], m2_ref.at[at])


def corners(n, y, r1, r2):
    return call(
        functools.partial(corner_kernel, n),
        [sds(2 * n, LANES), sds(2 * n, LANES)],
        [y, r1, r2],
        limit=1 << 20,
        name="corners",
    )


def split(x):
    high = x.astype(BF16)
    return high, (x - high.astype(F32)).astype(BF16)


def dot(a, b, dims=((1,), (0,))):
    return lax.dot_general(a, b, (dims, ((), ())), preferred_element_type=F32)


def project(x, pair, dims):
    high, low = split(x)
    return x + (dot(high, pair[0], dims) + dot(high, pair[1], dims) + dot(low, pair[0], dims))


def contact_and_edges(L, X, GX, NY, n, first, later, own_s, row_s, m_ref, gathered, whole, grow, work, pairs_ref, yc, ct_s, xc, cm):
    oxl, oxh, oy, rx1, rx2, ry1, ry2, exl, exh, ey, erx1, erx2, ery1, ery2 = gathered
    nt, half, ne = X // SUB, LANES // 2, 8 * L
    gx, me = lax.axis_index("gx"), lax.axis_index("gy")
    lane, sub = lane_ids(), sub_ids()
    lane_t = lane_ids(X)

    mh, ml = split(m_ref[...])
    straight, flipped = ((1,), (0,)), ((1,), (1,))
    pairs_ref[...] = jnp.zeros((LANES, LANES), F32)
    for q in range(NY):
        pairs_ref[pl.ds(q * SUB, SUB), :] = first[q][pl.ds(2 * X, SUB), :]
    columns = pairs_ref[...].T
    my_chip, my_core = me // 2, me % 2
    for q in range(NY):
        chip = lax.bitwise_xor(my_chip, q // 2)
        core = my_core if q % 2 == 0 else 1 - my_core
        owner = chip * 2 + core
        whole[pl.ds(pl.multiple_of(owner * X, X), X), :] = later[q][pl.ds(0, X), :]

    def gather(i, _):
        for k in range(SUB):
            p = i * SUB + k
            at = own_s[0, p] * X + row_s[0, p]
            to = (k % INTERSECTIONS) * X + i * (SUB // INTERSECTIONS) + k // INTERSECTIONS
            grow[pl.ds(to, 1), :] = whole[pl.ds(at, 1), :]
        return 0

    lax.fori_loop(0, INTERSECTIONS * X // SUB, gather, 0)

    def column(f):
        return jnp.broadcast_to(columns[:, f : f + 1], (X, LANES))

    slave = None
    for e in range(INTERSECTIONS):
        off = column(2 + e).astype(jnp.int32)
        moved = take_lanes(grow[pl.ds(e * X, X), :], (lane_t + off) & (LANES - 1))
        gap = later[0][pl.ds(X, X), :] - project(moved, (mh, ml), straight)
        t = column(4 + e) * (penalty_stiffness * jnp.maximum(0.0, -gap))
        slave = t if slave is None else slave + t
    cm[1] = slave

    fh, fl = split(later[0][pl.ds(0, X), :])
    me_f = me.astype(F32)
    node = lax.broadcasted_iota(jnp.int32, (X, X), 0).astype(F32)
    master = jnp.zeros((X, LANES), F32)
    blocks = [(q, e) for q in range(NY) for e in range(INTERSECTIONS)]
    for s, (q, e) in enumerate(blocks):
        base = q * SUB
        hot = jnp.where(node == pairs_ref[base + e : base + e + 1, :], 1.0, 0.0).astype(BF16)
        rows = dot(hot, fh, ((0,), (0,))) + dot(hot, fl, ((0,), (0,)))
        off = column(base + 2 + e).astype(jnp.int32)
        work[pl.ds(s * X, X), :] = take_lanes(rows, (lane_t + off) & (LANES - 1))
    for s, (q, e) in enumerate(blocks):
        gap = later[q][pl.ds(X, X), :] - project(
            work[pl.ds(s * X, X), :], (mh, ml), straight
        )
        work[pl.ds(s * X, X), :] = penalty_stiffness * jnp.maximum(0.0, -gap)
    for s, (q, e) in enumerate(blocks):
        base = q * SUB
        back = project(work[pl.ds(s * X, X), :], (mh, ml), flipped)
        off = column(base + 2 + e).astype(jnp.int32)
        work[pl.ds(s * X, X), :] = take_lanes(back, (lane_t - off) & (LANES - 1))
    for s, (q, e) in enumerate(blocks):
        base = q * SUB
        weight = jnp.where(
            pairs_ref[base + 6 + e : base + 7 + e, :] == me_f,
            pairs_ref[base + 4 + e : base + 5 + e, :],
            0.0,
        )
        hot = jnp.where(node == pairs_ref[base + e : base + e + 1, :], weight, 0.0).astype(BF16)
        bh, bl = split(work[pl.ds(s * X, X), :])
        master = master + (dot(hot, bh) + dot(hot, bl))
    cm[0] = -master

    inside = (gx > 0, gx < GX - 1, me > 0, me < NY - 1)
    ok = [jnp.where(x, 1.0, 0.0).astype(F32) for x in inside]

    def edge(own_e, own_u, near_e, near_u, corner_e, corner_u, put):
        near = {}
        for d in (-1, 0, 1):
            value_e, value_u = near_e, list(near_u)
            if d:
                value_e = pltpu.roll(near_e, (-d) % LANES, 1)
                value_u = [pltpu.roll(x, (-d) % LANES, 1) for x in near_u]
                at = lane == (0 if d < 0 else LANES - 1)
                if corner_e is None:
                    value_e = jnp.where(at, 0.0, value_e)
                else:
                    value_e = jnp.where(at, corner_e, value_e)
                    value_u = [jnp.where(at, c, x) for c, x in zip(corner_u, value_u)]
            near[d] = (value_e, value_u)
        sums = [None] * 3
        for dz in (-1, 0, 1):
            for d in (-1, 0, 1):
                o, us = near[d]
                if dz:
                    o = pltpu.roll(o, (-dz) % SUB, 0)
                    o = jnp.where(sub == (0 if dz < 0 else SUB - 1), 0.0, o)
                    us = [pltpu.roll(x, (-dz) % SUB, 0) for x in us]
                c = (own_e * twice_weight(1 + abs(dz) + abs(d))) * o / (own_e + o)
                for comp in range(3):
                    term = c * (us[comp] - own_u[comp])
                    sums[comp] = term if sums[comp] is None else sums[comp] + term
        for comp in range(3):
            put(comp, sums[comp])

    def rows(ref, k):
        return ref[pl.ds(k, L), :]

    def got(refs, k, axis):
        return choose(odd[axis], rows(refs[0], k), rows(refs[1], k))

    odd = gx % 2, me % 2

    yc[...] = jnp.zeros((LANES, LANES), F32)
    for b in range(2):
        ue = [(b * 3 + c) * L for c in range(3)]
        ee = (6 + b) * L
        for s, (own_x, got_x, own_xe, got_xe) in enumerate(
            ((oxl, (rx1, rx2), exl, (erx1, erx2)), (oxh, (rx2, rx1), exh, (erx2, erx1)))
        ):
            edge(
                rows(own_xe, ee),
                [rows(own_x, k) for k in ue],
                got(got_xe, ee, 0) * ok[s],
                [got(got_x, k, 0) for k in ue],
                None,
                None,
                lambda c, v, s=s, ue=ue: xc.__setitem__((s, pl.ds(ue[c], L), slice(None)), v),
            )
        for s, (got_y, got_ye) in enumerate((((ry1, ry2), (ery1, ery2)), ((ry2, ry1), (ery2, ery1)))):
            corner_ok = jnp.where(lane == 0, ok[0], ok[1]) * ok[2 + s]
            edge(
                rows(ey, s * half + ee),
                [rows(oy, s * half + k) for k in ue],
                got(got_ye, ee, 1) * ok[2 + s],
                [got(got_y, k, 1) for k in ue],
                got(got_ye, ne + ee, 1) * corner_ok,
                [got(got_y, n + k, 1) for k in ue],
                lambda c, v, s=s, ue=ue: yc.__setitem__((pl.ds(s * half + ue[c], L), slice(None)), v),
            )
    ct_s[...] = yc[...].T


def forced(L, X, k, f, face, base, ct, xc, cm_tile):
    lane, sub = lane_ids(), sub_ids()
    half = LANES // 2
    pick = jnp.where(lane == 0, f, jnp.where(lane == LANES - 1, half + f, half - 1))
    force = base + take_lanes(ct, pick)
    if k == 0:
        force = force + jnp.where(sub == 0, xc[0, pl.ds(f, 1), :], 0.0)
    if k == X // SUB - 1:
        force = force + jnp.where(sub == SUB - 1, xc[1, pl.ds(f, 1), :], 0.0)
    if cm_tile is not None:
        force = force + face * cm_tile
    return force


def advance(L, X, last, v_ref, u_ref, rho_ref, forces, ct_s, xc, cm, u1_ref, v1_ref, w_s, sinks, sems):
    nt, half = X // SUB, LANES // 2
    index = edge_index()
    slot = lane_ids() % half
    if not last:
        w_s[...] = jnp.zeros((X, LANES), F32)

    def layer_of(i, _):
        b, layer = i // L, lax.rem(i, L)
        face = jnp.where(layer == 0, 1.0, 0.0).astype(F32)
        for k in range(nt):
            rr = pl.multiple_of(i * X, X) + k * SUB
            scale = time_step / rho_ref[pl.ds(rr, SUB), :]
            ct = ct_s[pl.ds(k * SUB, SUB), :]
            if not last:
                w = w_s[pl.ds(k * SUB, SUB), :]
            for c in range(3):
                f = (b * 3 + c) * L + layer
                r = pl.multiple_of(f * X, X) + k * SUB
                if len(forces) == 2:
                    fr = pl.multiple_of(((b * 2 + c) if c < 2 else b) * L * X + layer * X, X)
                    base = forces[0 if c < 2 else 1][pl.ds(fr + k * SUB, SUB), :]
                else:
                    base = forces[0][pl.ds(r, SUB), :]
                tile = cm[b, pl.ds(k * SUB, SUB), :] if c == 2 else None
                vel = v_ref[pl.ds(r, SUB), :] + scale * forced(L, X, k, f, face, base, ct, xc, tile)
                disp = u_ref[pl.ds(r, SUB), :] + time_step * vel
                v1_ref[pl.ds(r, SUB), :] = vel
                u1_ref[pl.ds(r, SUB), :] = disp
                if not last:
                    w = jnp.where(slot == f, take_lanes(disp, index), w)
            if not last:
                w_s[pl.ds(k * SUB, SUB), :] = w
        if last:
            for c in range(3):
                at = pl.ds(pl.multiple_of(((b * 3 + c) * L + layer) * X, X), X)
                for s, ref in enumerate((u1_ref, v1_ref)):
                    pltpu.make_async_copy(ref.at[at], sinks[s].at[at], sems.at[s]).start()
        return 0

    lax.fori_loop(0, 2 * L, layer_of, 0)
    if last:
        for s, ref in enumerate((u1_ref, v1_ref)):
            pltpu.make_async_copy(ref, sinks[s], sems.at[s]).wait()


NGOT = 14


def contact_kernel(L, X, GX, NY, n, own_s, row_s, m_ref, gap_ref, v_ref, u_ref, rho_ref, f_ref, *rest):
    gathered, first = rest[:NGOT], rest[NGOT : NGOT + NY]
    cm, ct_s, xc, face_out, whole, grow, work, pairs_ref, yc = rest[NGOT + NY :]
    contact_and_edges(
        L, X, GX, NY, n, first, first, own_s, row_s, m_ref, gathered,
        whole, grow, work, pairs_ref, yc, ct_s, xc, cm,
    )
    for b in range(2):
        f = (b * 3 + 2) * L
        for k in range(X // SUB):
            at = pl.ds(f * X + k * SUB, SUB)
            part = pl.ds(k * SUB, SUB)
            force = forced(L, X, k, f, 1.0, f_ref[at, :], ct_s[part, :], xc, cm[b, part, :])
            scale = time_step / rho_ref[pl.ds(b * L * X + k * SUB, SUB), :]
            disp = u_ref[at, :] + time_step * (v_ref[at, :] + scale * force)
            if b == 1:
                disp = disp + gap_ref[part, :]
            face_out[pl.ds(b * X + k * SUB, SUB), :] = disp


def contact_scratch(L, X, NY):
    vm = pltpu.VMEM
    return [
        vm((NY * X, LANES), F32),
        vm((INTERSECTIONS * X, LANES), F32),
        vm((NY * INTERSECTIONS * X, LANES), F32),
        vm((LANES, LANES), F32),
        vm((LANES, LANES), F32),
    ]


def grant(X, NY):
    return (3 << 20) + 2 * NY * INTERSECTIONS * X * LANES * 4 * max(1, NY // 8)


def contact(L, X, GX, NY, n, args):
    return call(
        functools.partial(contact_kernel, L, X, GX, NY, n),
        [sds(2, X, LANES), sds(X, LANES), sds(2, 6 * L, LANES), sds(2 * X, LANES)],
        args,
        specs=[SMEM] * 2 + [VMEM] * (len(args) - 2),
        scratch=contact_scratch(L, X, NY),
        limit=grant(X, NY),
        flops=60 * NY * INTERSECTIONS * X * LANES,
        name="contact",
    )


def step_kernel(L, X, v_ref, u_ref, rho_ref, f_ref, cm, ct_s, xc, *rest):
    u1_ref, v1_ref, xl_ref, xh_ref, x1_ref, x2_ref, y_ref, w_s = rest
    advance(L, X, False, v_ref, u_ref, rho_ref, (f_ref,), ct_s, xc, cm, u1_ref, v1_ref, w_s, None, None)
    x_rows(L, X, 0, 6, u1_ref, xl_ref, xh_ref, 0)
    pair_rows(lax.axis_index("gx") % 2, xl_ref[...], xh_ref[...], x1_ref, x2_ref)
    y_ref[...] = w_s[...].T


def step(L, X, args):
    R = 6 * L * X
    return call(
        functools.partial(step_kernel, L, X),
        [sds(R, LANES), sds(R, LANES)] + [sds(6 * L, LANES)] * 4 + [sds(LANES, LANES)],
        args,
        scratch=[pltpu.VMEM((X, LANES), F32)],
        limit=2 << 20,
        flops=20 * R * LANES,
        name="step",
    )


def last_kernel(L, X, GX, NY, n, own_s, row_s, m_ref, v_ref, u_ref, rho_ref, f_ref, g_ref, *rest):
    gathered, rest = rest[:NGOT], rest[NGOT:]
    first, later, rest = rest[:NY], rest[NY : 2 * NY], rest[2 * NY :]
    sinks, scratch = rest[:2], rest[2:]
    whole, grow, work, pairs_ref, yc, ct_s, xc, cm, u1_s, v1_s, sems = scratch
    contact_and_edges(
        L, X, GX, NY, n, first, later, own_s, row_s, m_ref, gathered,
        whole, grow, work, pairs_ref, yc, ct_s, xc, cm,
    )
    advance(
        L, X, True, v_ref, u_ref, rho_ref, (f_ref, g_ref), ct_s, xc, cm, u1_s, v1_s, None, sinks, sems
    )


def last_step(L, X, GX, NY, n, args):
    R = 6 * L * X
    vm = pltpu.VMEM
    return call(
        functools.partial(last_kernel, L, X, GX, NY, n),
        [sds(R, LANES), sds(R, LANES)],
        args,
        specs=[SMEM] * 2 + [VMEM] * (len(args) - 2),
        scratch=contact_scratch(L, X, NY)
        + [
            vm((X, LANES), F32),
            vm((2, 6 * L, LANES), F32),
            vm((2, X, LANES), F32),
            vm((R, LANES), F32),
            vm((R, LANES), F32),
            pltpu.SemaphoreType.DMA((2,)),
        ],
        limit=grant(X, NY) + 2 * R * LANES * 4,
        out_spec=pl.BlockSpec(memory_space=pl.ANY),
        flops=80 * R * LANES,
        name="last",
    )


def swap(x, axis="gy"):
    return lax.ppermute(x, axis, [(i, i ^ 1) for i in range(lax.axis_size(axis))])


def cross(x, axis="gy", wrap=False):
    n = lax.axis_size(axis)
    to = [i + 1 if i % 2 else i - 1 for i in range(n)]
    to = [t % n if wrap else min(max(t, 0), n - 1) for t in to]
    return lax.ppermute(x, axis, list(enumerate(to)))


def far(x):
    n = lax.axis_size("gy")
    return [x] + [
        lax.ppermute(x, "gy", [(i, i ^ (2 * k)) for i in range(n)]) for k in range(1, n // 2)
    ]


def both(parts):
    return [p for part in parts for p in (part, swap(part))]


def body(
    displacement,
    velocity,
    modulus,
    density,
    clearance,
    mortar_coupling,
    pair_owner,
    pair_row,
    pair_offset,
    pair_active,
):
    L, X, Y = displacement.shape[2:]
    assert Y == LANES and L == SUB and X == LANES
    GX, NY = lax.axis_size("gx"), lax.axis_size("gy")

    u, v = displacement.reshape(-1, Y), velocity.reshape(-1, Y)
    e, rho = modulus.reshape(-1, Y), density.reshape(-1, Y)
    own, row, off, act = (
        a.transpose(0, 2, 1).reshape(1, -1)
        for a in (pair_owner, pair_row, pair_offset, pair_active)
    )
    parts = far(first_message(u, clearance, (own, row, off, act), L, X))
    xl, xh, x1, x2, y = pack(u, e, L, X)
    rx1, rx2 = swap(x1, "gx"), cross(x2, "gx", True)
    coef, diag = coupling(e, L, X)
    diag, rx1, rx2, *parts = lax.optimization_barrier((diag, rx1, rx2, *parts))
    m1, m2 = corners(8 * L, y, rx1, rx2)
    f = stencil(u, coef, diag, L, X, (0, 1, 2), (m1, *parts[1:]))
    stiff = (xl, xh, y, rx1, rx2, swap(m1), cross(m2))
    messages = both(parts)
    cm, ct, xc, face = contact(
        L, X, GX, NY, 8 * L,
        (own, row, mortar_coupling, clearance, v, u, rho, f, *stiff, *stiff, *messages),
    )
    parts = far(face)
    u, v, xl, xh, x1, x2, y = step(L, X, (v, u, rho, f, cm, ct, xc))
    rx1, rx2 = swap(x1, "gx"), cross(x2, "gx", True)
    f = stencil(u, coef, diag, L, X, (0, 1))
    f, rx1, rx2, *parts = lax.optimization_barrier((f, rx1, rx2, *parts))
    m1, m2 = corners(6 * L, y, rx1, rx2)
    g = stencil(u, coef, diag, L, X, (2,), (m1, f, *parts[1:]))
    edges = (xl, xh, y, rx1, rx2, swap(m1), cross(m2))
    u, v = last_step(
        L, X, GX, NY, 6 * L,
        (own, row, mortar_coupling, v, u, rho, f, g, *edges, *stiff, *messages, *both(parts)),
    )
    return u.reshape(displacement.shape), v.reshape(velocity.shape)


def solution(mesh):
    return jax.shard_map(
        body,
        mesh=mesh,
        in_specs=(
            P(None, None, None, "gx", "gy"),
            P(None, None, None, "gx", "gy"),
            P(None, None, "gx", "gy"),
            P(None, None, "gx", "gy"),
            P("gx", "gy"),
            P(),
            P("gx", "gy", None),
            P("gx", "gy", None),
            P("gx", "gy", None),
            P("gx", "gy", None),
        ),
        out_specs=(P(None, None, None, "gx", "gy"), P(None, None, None, "gx", "gy")),
        check_vma=False,
    )
```

```python
import functools

import jax
import jax.numpy as jnp
from jax import lax
from jax.experimental import pallas as pl
from jax.experimental.pallas import tpu as pltpu
from jax.sharding import PartitionSpec as P

F32 = jnp.float32
BF16 = jnp.bfloat16
INTERSECTIONS = 2
STEPS = 2
time_step = 0.2
penalty_stiffness = 4.0

SUB = 8
LANES = 128
FLAT = [(0, 1, 0), (1, -1, 0), (1, 0, 0), (1, 1, 0)]
SIDE = [(dz, dx, 1) for dz in (-1, 0, 1) for dx in (-1, 0, 1)]
HALF = FLAT + SIDE
NSIDE = len(SIDE)
NHALF = len(HALF)
NCOEF = NHALF + NSIDE

VMEM = pl.BlockSpec(memory_space=pltpu.VMEM)
SMEM = pl.BlockSpec(memory_space=pltpu.SMEM)


def twice_weight(nonzero):
    return 2.0 * 0.5 ** (nonzero - 1)


def lane_ids(rows=SUB):
    return lax.broadcasted_iota(jnp.int32, (rows, LANES), 1)


def sub_ids(rows=SUB):
    return lax.broadcasted_iota(jnp.int32, (rows, LANES), 0)


def take_lanes(values, index):
    return jnp.take_along_axis(values, index, axis=1)


def call(
    kernel, out_shape, args, specs=None, scratch=(), limit=None, flops=0, name=None, out_spec=VMEM
):
    nbytes = sum(a.size * 4 for a in args)
    return pl.pallas_call(
        kernel,
        out_shape=out_shape,
        in_specs=specs or [VMEM] * len(args),
        out_specs=jax.tree.map(lambda _: out_spec, out_shape),
        scratch_shapes=scratch,
        name=name,
        cost_estimate=pl.CostEstimate(flops=flops, bytes_accessed=nbytes, transcendentals=0),
        compiler_params=pltpu.CompilerParams(vmem_limit_bytes=limit),
    )(*args)


def sds(*shape):
    return jax.ShapeDtypeStruct(shape, F32)


def coupling_kernel(L, X, e_ref, c_ref, d_ref, ep, ey):
    rows, pad, nt = 2 * L * X, X + SUB, X // SUB
    zero = jnp.zeros((pad, LANES), F32)
    for s in (ep, ey):
        s[pl.ds(0, pad), :] = zero
        s[pl.ds(pad + rows, pad), :] = zero
    for j in range(NHALF):
        c_ref[j, pl.ds(0, pad), :] = zero
        c_ref[j, pl.ds(pad + rows, pad), :] = zero
    lane, sub = lane_ids(), sub_ids()

    def fill(i, _):
        for k in range(nt):
            r = pl.multiple_of(i * X, X) + k * SUB
            e = e_ref[pl.ds(r, SUB), :]
            ep[pl.ds(r + pad, SUB), :] = e
            ey[pl.ds(r + pad, SUB), :] = jnp.where(
                lane == LANES - 1, 0.0, pltpu.roll(e, LANES - 1, 1)
            )
        return 0

    lax.fori_loop(0, 2 * L, fill, 0)

    def block(i, _):
        layer = lax.rem(i, L)
        up = jnp.where(layer < L - 1, 1.0, 0.0).astype(F32)
        down = jnp.where(layer > 0, 1.0, 0.0).astype(F32)
        for k in range(nt):
            r = pl.multiple_of(i * X, X) + k * SUB + pad
            e = ep[pl.ds(r, SUB), :]
            for j, (dz, dx, dy) in enumerate(HALF):
                o = (ey if dy else ep)[pl.ds(r + dz * X + dx, SUB), :]
                c = (e * twice_weight(abs(dz) + abs(dx) + dy)) * o / (e + o)
                if dz == 1:
                    c = c * up
                if dz == -1:
                    c = c * down
                if dx == 1 and k == nt - 1:
                    c = jnp.where(sub == SUB - 1, 0.0, c)
                if dx == -1 and k == 0:
                    c = jnp.where(sub == 0, 0.0, c)
                c_ref[j, pl.ds(r, SUB), :] = c
                if dy:
                    c_ref[NSIDE + j, pl.ds(r, SUB), :] = pltpu.roll(c, 1, 1)
        return 0

    lax.fori_loop(0, 2 * L, block, 0)

    def total(i, _):
        for k in range(nt):
            r = pl.multiple_of(i * X, X) + k * SUB + pad
            own, back = None, None
            for j, (dz, dx, dy) in enumerate(HALF):
                f = c_ref[j, pl.ds(r, SUB), :]
                b = c_ref[j, pl.ds(r - dz * X - dx, SUB), :]
                own = f if own is None else own + f
                if dy:
                    back = b if back is None else back + b
                else:
                    own = own + b
            d_ref[pl.ds(r - pad, SUB), :] = own + pltpu.roll(back, 1, 1)
        return 0

    lax.fori_loop(0, 2 * L, total, 0)


def coupling(modulus, L, X):
    rows, pad = 2 * L * X, X + SUB
    return call(
        functools.partial(coupling_kernel, L, X),
        [sds(NCOEF, rows + 2 * pad + SUB, LANES), sds(rows, LANES)],
        [modulus],
        scratch=[pltpu.VMEM((rows + 2 * pad, LANES), F32)] * 2,
        limit=5 << 20,
        flops=200 * rows * LANES,
        name="coupling",
    )


def spaced(X):
    return X + SUB, X + 5 * SUB


def stencil_kernel(L, X, group, comps, u_ref, c_ref, d_ref, *rest):
    f_ref, up = rest[-2:]
    nt, count, lowest = X // SUB, len(comps), comps[0]
    S, pad = spaced(X)
    zero = jnp.zeros((pad, LANES), F32)
    up[pl.ds(0, pad), :] = zero
    up[pl.ds(pad + 2 * count * L * S, pad), :] = zero

    def field(which):
        return which // count * 3 + lowest + lax.rem(which, count)

    def fill(i, _):
        source = field(i // L) * L + lax.rem(i, L)
        to = pl.multiple_of(i * S, SUB) + pad
        for k in range(nt):
            r = pl.multiple_of(source * X, X) + k * SUB
            up[pl.ds(to + k * SUB, SUB), :] = u_ref[pl.ds(r, SUB), :]
        up[pl.ds(to + X, SUB), :] = jnp.zeros((SUB, LANES), F32)
        return 0

    lax.fori_loop(0, 2 * count * L, fill, 0)

    def block(i, _):
        which = i // (nt // group)
        first = lax.rem(i, nt // group) * group * SUB
        body = which // count
        for k in range(group):
            for layer in range(L):
                ru = pl.multiple_of(which * L * S + layer * S + first, SUB) + k * SUB + pad
                rf = pl.multiple_of(which * L * X + layer * X + first, SUB) + k * SUB
                rd = pl.multiple_of(body * L * X + layer * X + first, SUB) + k * SUB
                rc = rd + X + SUB
                t = {
                    (dz, dx): up[pl.ds(ru + dz * S + dx, SUB), :]
                    for dz in (-1, 0, 1)
                    for dx in (-1, 0, 1)
                }
                acc = -d_ref[pl.ds(rd, SUB), :] * t[0, 0]
                ahead, behind = None, None
                for j, (dz, dx, dy) in enumerate(HALF):
                    back = c_ref[j, pl.ds(rc - dz * X - dx, SUB), :] * t[-dz, -dx]
                    near = c_ref[j + NSIDE * dy, pl.ds(rc, SUB), :] * t[dz, dx]
                    if dy:
                        ahead = near if ahead is None else ahead + near
                        behind = back if behind is None else behind + back
                    else:
                        acc = acc + near
                        acc = acc + back
                f_ref[pl.ds(rf, SUB), :] = (
                    acc + pltpu.roll(ahead, LANES - 1, 1) + pltpu.roll(behind, 1, 1)
                )
        return 0

    lax.fori_loop(0, 2 * count * (nt // group), block, 0)


def stencil(u, coef, diag, L, X, comps, after=()):
    S, pad = spaced(X)
    rows = 2 * len(comps) * L * X
    return call(
        functools.partial(stencil_kernel, L, X, X // SUB // 2, comps),
        sds(rows, LANES),
        [u, coef, diag, *after],
        specs=[VMEM] * 3 + [pl.BlockSpec(memory_space=pl.ANY)] * len(after),
        scratch=[pltpu.VMEM((2 * len(comps) * L * S + 2 * pad, LANES), F32)],
        limit=5 << 20,
        flops=60 * rows * LANES,
        name="stencil",
    )


def message_kernel(L, X, u_ref, gap_ref, own, row, off, act, out_ref, tile, gap, words, sems):
    copies = [
        pltpu.make_async_copy(u_ref.at[pl.ds(2 * L * X, X)], out_ref.at[pl.ds(0, X)], sems.at[0]),
        pltpu.make_async_copy(u_ref.at[pl.ds(5 * L * X, X)], tile, sems.at[1]),
        pltpu.make_async_copy(gap_ref, gap, sems.at[2]),
    ]
    small = [
        pltpu.make_async_copy(ref, words.at[pl.ds(k, 1)], sems.at[3 + k])
        for k, ref in enumerate((row, off, act, own))
    ]
    for c in small + copies:
        c.start()
    for c in small:
        c.wait()
    lane = lane_ids()
    for k in range(4):
        halves = [
            jnp.broadcast_to(words[pl.ds(k, 1), pl.ds(h * LANES, LANES)].astype(F32), (SUB, LANES))
            for h in range(INTERSECTIONS)
        ]
        for e in range(INTERSECTIONS):
            index = (lane * INTERSECTIONS + e) & (LANES - 1)
            picked = [take_lanes(x, index) for x in halves]
            value = jnp.where(lane < LANES // INTERSECTIONS, picked[0], picked[1])
            out_ref[pl.ds(2 * X + INTERSECTIONS * k + e, 1), :] = value[:1]
    for c in copies:
        c.wait()
    out_ref[pl.ds(X, X), :] = tile[...] + gap[...]


def first_message(u, clearance, pairs, L, X):
    return call(
        functools.partial(message_kernel, L, X),
        sds(2 * X + 4 * INTERSECTIONS, LANES),
        [u, clearance, *pairs],
        specs=[pl.BlockSpec(memory_space=pl.ANY)] * 6,
        scratch=[
            pltpu.VMEM((X, LANES), F32),
            pltpu.VMEM((X, LANES), F32),
            pltpu.VMEM((4, INTERSECTIONS * X), jnp.int32),
            pltpu.SemaphoreType.DMA((7,)),
        ],
        limit=58 << 20,
        name="message",
    )


def edge_index():
    return jnp.where(lane_ids() < LANES // 2, 0, LANES - 1)


def choose(flag, a, b):
    return jnp.where(jnp.broadcast_to(flag, a.shape) == 1, a, b)


def pair_rows(odd, low, high, first_ref, second_ref):
    first_ref[...] = choose(odd, low, high)
    second_ref[...] = choose(odd, high, low)


def x_rows(L, X, start, count, src, xl_ref, xh_ref, at):
    for bc in range(count):
        base = start + bc * L * X
        xl_ref[pl.ds((at + bc) * L, L), :] = src[pl.ds(base, L, stride=X), :]
        xh_ref[pl.ds((at + bc) * L, L), :] = src[pl.ds(base + X - 1, L, stride=X), :]


def pack_kernel(L, X, u_ref, e_ref, xl_ref, xh_ref, x1_ref, x2_ref, y_ref, w_ref):
    nt = X // SUB
    x_rows(L, X, 0, 6, u_ref, xl_ref, xh_ref, 0)
    x_rows(L, X, 0, 2, e_ref, xl_ref, xh_ref, 6)
    pair_rows(lax.axis_index("gx") % 2, xl_ref[...], xh_ref[...], x1_ref, x2_ref)
    index = edge_index()
    slot = lane_ids() % (LANES // 2)

    def tile(k, _):
        r = pl.multiple_of(k * SUB, SUB)
        w = jnp.zeros((SUB, LANES), F32)
        for f in range(8 * L):
            src, row = (u_ref, f) if f < 6 * L else (e_ref, f - 6 * L)
            v = src[pl.ds(row * X + r, SUB), :]
            w = jnp.where(slot == f, take_lanes(v, index), w)
        w_ref[pl.ds(r, SUB), :] = w
        return 0

    lax.fori_loop(0, nt, tile, 0)
    y_ref[...] = w_ref[...].T


def pack(u, e, L, X):
    return call(
        functools.partial(pack_kernel, L, X),
        [sds(8 * L, LANES)] * 4 + [sds(LANES, LANES)],
        [u, e],
        scratch=[pltpu.VMEM((X, LANES), F32)],
        limit=1 << 20,
        flops=u.size,
        name="pack",
    )


def corner_kernel(n, y_ref, r1_ref, r2_ref, m1_ref, m2_ref):
    half = LANES // 2
    odd_x, odd_y = lax.axis_index("gx") % 2, lax.axis_index("gy") % 2
    lane = lane_ids(n)
    r1, r2 = r1_ref[...], r2_ref[...]
    low, high = choose(odd_x, r1, r2), choose(odd_x, r2, r1)
    left = y_ref[pl.ds(0, n), :], jnp.where(lane == 0, low, pltpu.roll(high, LANES - 1, 1))
    right = y_ref[pl.ds(half, n), :], jnp.where(lane == 0, pltpu.roll(low, 1, 1), high)
    for k in range(2):
        at = pl.ds(k * n, n)
        pair_rows(odd_y, left[k], right[k], m1_ref.at[at], m2_ref.at[at])


def corners(n, y, r1, r2):
    return call(
        functools.partial(corner_kernel, n),
        [sds(2 * n, LANES), sds(2 * n, LANES)],
        [y, r1, r2],
        limit=1 << 20,
        name="corners",
    )


def split(x):
    high = x.astype(BF16)
    return high, (x - high.astype(F32)).astype(BF16)


def dot(a, b, dims=((1,), (0,))):
    return lax.dot_general(a, b, (dims, ((), ())), preferred_element_type=F32)


def project(x, pair, dims):
    high, low = split(x)
    return x + (dot(high, pair[0], dims) + dot(high, pair[1], dims) + dot(low, pair[0], dims))


def contact_and_edges(L, X, GX, NY, n, first, later, own_s, row_s, m_ref, gathered, whole, grow, work, pairs_ref, yc, ct_s, xc, cm):
    oxl, oxh, oy, rx1, rx2, ry1, ry2, exl, exh, ey, erx1, erx2, ery1, ery2 = gathered
    nt, half, ne = X // SUB, LANES // 2, 8 * L
    gx, me = lax.axis_index("gx"), lax.axis_index("gy")
    lane, sub = lane_ids(), sub_ids()
    lane_t = lane_ids(X)

    mh, ml = split(m_ref[...])
    straight, flipped = ((1,), (0,)), ((1,), (1,))
    pairs_ref[...] = jnp.zeros((LANES, LANES), F32)
    for q in range(NY):
        pairs_ref[pl.ds(q * SUB, SUB), :] = first[q][pl.ds(2 * X, SUB), :]
    columns = pairs_ref[...].T
    my_chip, my_core = me // 2, me % 2
    for q in range(NY):
        chip = lax.bitwise_xor(my_chip, q // 2)
        core = my_core if q % 2 == 0 else 1 - my_core
        owner = chip * 2 + core
        whole[pl.ds(pl.multiple_of(owner * X, X), X), :] = later[q][pl.ds(0, X), :]

    def gather(i, _):
        for k in range(SUB):
            p = i * SUB + k
            at = own_s[0, p] * X + row_s[0, p]
            to = (k % INTERSECTIONS) * X + i * (SUB // INTERSECTIONS) + k // INTERSECTIONS
            grow[pl.ds(to, 1), :] = whole[pl.ds(at, 1), :]
        return 0

    lax.fori_loop(0, INTERSECTIONS * X // SUB, gather, 0)

    def column(f):
        return jnp.broadcast_to(columns[:, f : f + 1], (X, LANES))

    slave = None
    for e in range(INTERSECTIONS):
        off = column(2 + e).astype(jnp.int32)
        moved = take_lanes(grow[pl.ds(e * X, X), :], (lane_t + off) & (LANES - 1))
        gap = later[0][pl.ds(X, X), :] - project(moved, (mh, ml), straight)
        t = column(4 + e) * (penalty_stiffness * jnp.maximum(0.0, -gap))
        slave = t if slave is None else slave + t
    cm[1] = slave

    fh, fl = split(later[0][pl.ds(0, X), :])
    me_f = me.astype(F32)
    node = lax.broadcasted_iota(jnp.int32, (X, X), 0).astype(F32)
    master = jnp.zeros((X, LANES), F32)
    blocks = [(q, e) for q in range(NY) for e in range(INTERSECTIONS)]
    for s, (q, e) in enumerate(blocks):
        base = q * SUB
        hot = jnp.where(node == pairs_ref[base + e : base + e + 1, :], 1.0, 0.0).astype(BF16)
        rows = dot(hot, fh, ((0,), (0,))) + dot(hot, fl, ((0,), (0,)))
        off = column(base + 2 + e).astype(jnp.int32)
        work[pl.ds(s * X, X), :] = take_lanes(rows, (lane_t + off) & (LANES - 1))
    for s, (q, e) in enumerate(blocks):
        gap = later[q][pl.ds(X, X), :] - project(
            work[pl.ds(s * X, X), :], (mh, ml), straight
        )
        work[pl.ds(s * X, X), :] = penalty_stiffness * jnp.maximum(0.0, -gap)
    for s, (q, e) in enumerate(blocks):
        base = q * SUB
        back = project(work[pl.ds(s * X, X), :], (mh, ml), flipped)
        off = column(base + 2 + e).astype(jnp.int32)
        work[pl.ds(s * X, X), :] = take_lanes(back, (lane_t - off) & (LANES - 1))
    for s, (q, e) in enumerate(blocks):
        base = q * SUB
        weight = jnp.where(
            pairs_ref[base + 6 + e : base + 7 + e, :] == me_f,
            pairs_ref[base + 4 + e : base + 5 + e, :],
            0.0,
        )
        hot = jnp.where(node == pairs_ref[base + e : base + e + 1, :], weight, 0.0).astype(BF16)
        bh, bl = split(work[pl.ds(s * X, X), :])
        master = master + (dot(hot, bh) + dot(hot, bl))
    cm[0] = -master

    inside = (gx > 0, gx < GX - 1, me > 0, me < NY - 1)
    ok = [jnp.where(x, 1.0, 0.0).astype(F32) for x in inside]

    def edge(own_e, own_u, near_e, near_u, corner_e, corner_u, put):
        near = {}
        for d in (-1, 0, 1):
            value_e, value_u = near_e, list(near_u)
            if d:
                value_e = pltpu.roll(near_e, (-d) % LANES, 1)
                value_u = [pltpu.roll(x, (-d) % LANES, 1) for x in near_u]
                at = lane == (0 if d < 0 else LANES - 1)
                if corner_e is None:
                    value_e = jnp.where(at, 0.0, value_e)
                else:
                    value_e = jnp.where(at, corner_e, value_e)
                    value_u = [jnp.where(at, c, x) for c, x in zip(corner_u, value_u)]
            near[d] = (value_e, value_u)
        sums = [None] * 3
        for dz in (-1, 0, 1):
            for d in (-1, 0, 1):
                o, us = near[d]
                if dz:
                    o = pltpu.roll(o, (-dz) % SUB, 0)
                    o = jnp.where(sub == (0 if dz < 0 else SUB - 1), 0.0, o)
                    us = [pltpu.roll(x, (-dz) % SUB, 0) for x in us]
                c = (own_e * twice_weight(1 + abs(dz) + abs(d))) * o / (own_e + o)
                for comp in range(3):
                    term = c * (us[comp] - own_u[comp])
                    sums[comp] = term if sums[comp] is None else sums[comp] + term
        for comp in range(3):
            put(comp, sums[comp])

    def rows(ref, k):
        return ref[pl.ds(k, L), :]

    def got(refs, k, axis):
        return choose(odd[axis], rows(refs[0], k), rows(refs[1], k))

    odd = gx % 2, me % 2

    yc[...] = jnp.zeros((LANES, LANES), F32)
    for b in range(2):
        ue = [(b * 3 + c) * L for c in range(3)]
        ee = (6 + b) * L
        for s, (own_x, got_x, own_xe, got_xe) in enumerate(
            ((oxl, (rx1, rx2), exl, (erx1, erx2)), (oxh, (rx2, rx1), exh, (erx2, erx1)))
        ):
            edge(
                rows(own_xe, ee),
                [rows(own_x, k) for k in ue],
                got(got_xe, ee, 0) * ok[s],
                [got(got_x, k, 0) for k in ue],
                None,
                None,
                lambda c, v, s=s, ue=ue: xc.__setitem__((s, pl.ds(ue[c], L), slice(None)), v),
            )
        for s, (got_y, got_ye) in enumerate((((ry1, ry2), (ery1, ery2)), ((ry2, ry1), (ery2, ery1)))):
            corner_ok = jnp.where(lane == 0, ok[0], ok[1]) * ok[2 + s]
            edge(
                rows(ey, s * half + ee),
                [rows(oy, s * half + k) for k in ue],
                got(got_ye, ee, 1) * ok[2 + s],
                [got(got_y, k, 1) for k in ue],
                got(got_ye, ne + ee, 1) * corner_ok,
                [got(got_y, n + k, 1) for k in ue],
                lambda c, v, s=s, ue=ue: yc.__setitem__((pl.ds(s * half + ue[c], L), slice(None)), v),
            )
    ct_s[...] = yc[...].T


def forced(L, X, k, f, face, base, ct, xc, cm_tile):
    lane, sub = lane_ids(), sub_ids()
    half = LANES // 2
    pick = jnp.where(lane == 0, f, jnp.where(lane == LANES - 1, half + f, half - 1))
    force = base + take_lanes(ct, pick)
    if k == 0:
        force = force + jnp.where(sub == 0, xc[0, pl.ds(f, 1), :], 0.0)
    if k == X // SUB - 1:
        force = force + jnp.where(sub == SUB - 1, xc[1, pl.ds(f, 1), :], 0.0)
    if cm_tile is not None:
        force = force + face * cm_tile
    return force


def advance(L, X, last, v_ref, u_ref, rho_ref, forces, ct_s, xc, cm, u1_ref, v1_ref, w_s, sinks, sems):
    nt, half = X // SUB, LANES // 2
    index = edge_index()
    slot = lane_ids() % half
    if not last:
        w_s[...] = jnp.zeros((X, LANES), F32)

    def layer_of(i, _):
        b, layer = i // L, lax.rem(i, L)
        face = jnp.where(layer == 0, 1.0, 0.0).astype(F32)
        for k in range(nt):
            rr = pl.multiple_of(i * X, X) + k * SUB
            scale = time_step / rho_ref[pl.ds(rr, SUB), :]
            ct = ct_s[pl.ds(k * SUB, SUB), :]
            if not last:
                w = w_s[pl.ds(k * SUB, SUB), :]
            for c in range(3):
                f = (b * 3 + c) * L + layer
                r = pl.multiple_of(f * X, X) + k * SUB
                if len(forces) == 2:
                    fr = pl.multiple_of(((b * 2 + c) if c < 2 else b) * L * X + layer * X, X)
                    base = forces[0 if c < 2 else 1][pl.ds(fr + k * SUB, SUB), :]
                else:
                    base = forces[0][pl.ds(r, SUB), :]
                tile = cm[b, pl.ds(k * SUB, SUB), :] if c == 2 else None
                vel = v_ref[pl.ds(r, SUB), :] + scale * forced(L, X, k, f, face, base, ct, xc, tile)
                disp = u_ref[pl.ds(r, SUB), :] + time_step * vel
                v1_ref[pl.ds(r, SUB), :] = vel
                u1_ref[pl.ds(r, SUB), :] = disp
                if not last:
                    w = jnp.where(slot == f, take_lanes(disp, index), w)
            if not last:
                w_s[pl.ds(k * SUB, SUB), :] = w
        if last:
            for c in range(3):
                at = pl.ds(pl.multiple_of(((b * 3 + c) * L + layer) * X, X), X)
                for s, ref in enumerate((u1_ref, v1_ref)):
                    pltpu.make_async_copy(ref.at[at], sinks[s].at[at], sems.at[s]).start()
        return 0

    lax.fori_loop(0, 2 * L, layer_of, 0)
    if last:
        for s, ref in enumerate((u1_ref, v1_ref)):
            pltpu.make_async_copy(ref, sinks[s], sems.at[s]).wait()


NGOT = 14


def contact_kernel(L, X, GX, NY, n, own_s, row_s, m_ref, gap_ref, v_ref, u_ref, rho_ref, f_ref, *rest):
    gathered, first = rest[:NGOT], rest[NGOT : NGOT + NY]
    cm, ct_s, xc, face_out, whole, grow, work, pairs_ref, yc = rest[NGOT + NY :]
    contact_and_edges(
        L, X, GX, NY, n, first, first, own_s, row_s, m_ref, gathered,
        whole, grow, work, pairs_ref, yc, ct_s, xc, cm,
    )
    for b in range(2):
        f = (b * 3 + 2) * L
        for k in range(X // SUB):
            at = pl.ds(f * X + k * SUB, SUB)
            part = pl.ds(k * SUB, SUB)
            force = forced(L, X, k, f, 1.0, f_ref[at, :], ct_s[part, :], xc, cm[b, part, :])
            scale = time_step / rho_ref[pl.ds(b * L * X + k * SUB, SUB), :]
            disp = u_ref[at, :] + time_step * (v_ref[at, :] + scale * force)
            if b == 1:
                disp = disp + gap_ref[part, :]
            face_out[pl.ds(b * X + k * SUB, SUB), :] = disp


def contact_scratch(L, X, NY):
    vm = pltpu.VMEM
    return [
        vm((NY * X, LANES), F32),
        vm((INTERSECTIONS * X, LANES), F32),
        vm((NY * INTERSECTIONS * X, LANES), F32),
        vm((LANES, LANES), F32),
        vm((LANES, LANES), F32),
    ]


def grant(X, NY):
    return (3 << 20) + 2 * NY * INTERSECTIONS * X * LANES * 4 * max(1, NY // 8)


def contact(L, X, GX, NY, n, args):
    return call(
        functools.partial(contact_kernel, L, X, GX, NY, n),
        [sds(2, X, LANES), sds(X, LANES), sds(2, 6 * L, LANES), sds(2 * X, LANES)],
        args,
        specs=[SMEM] * 2 + [VMEM] * (len(args) - 2),
        scratch=contact_scratch(L, X, NY),
        limit=grant(X, NY),
        flops=60 * NY * INTERSECTIONS * X * LANES,
        name="contact",
    )


def step_kernel(L, X, v_ref, u_ref, rho_ref, f_ref, cm, ct_s, xc, *rest):
    u1_ref, v1_ref, xl_ref, xh_ref, x1_ref, x2_ref, y_ref, w_s = rest
    advance(L, X, False, v_ref, u_ref, rho_ref, (f_ref,), ct_s, xc, cm, u1_ref, v1_ref, w_s, None, None)
    x_rows(L, X, 0, 6, u1_ref, xl_ref, xh_ref, 0)
    pair_rows(lax.axis_index("gx") % 2, xl_ref[...], xh_ref[...], x1_ref, x2_ref)
    y_ref[...] = w_s[...].T


def step(L, X, args):
    R = 6 * L * X
    return call(
        functools.partial(step_kernel, L, X),
        [sds(R, LANES), sds(R, LANES)] + [sds(6 * L, LANES)] * 4 + [sds(LANES, LANES)],
        args,
        scratch=[pltpu.VMEM((X, LANES), F32)],
        limit=2 << 20,
        flops=20 * R * LANES,
        name="step",
    )


def last_kernel(L, X, GX, NY, n, own_s, row_s, m_ref, v_ref, u_ref, rho_ref, f_ref, g_ref, *rest):
    gathered, rest = rest[:NGOT], rest[NGOT:]
    first, later, rest = rest[:NY], rest[NY : 2 * NY], rest[2 * NY :]
    sinks, scratch = rest[:2], rest[2:]
    whole, grow, work, pairs_ref, yc, ct_s, xc, cm, u1_s, v1_s, sems = scratch
    contact_and_edges(
        L, X, GX, NY, n, first, later, own_s, row_s, m_ref, gathered,
        whole, grow, work, pairs_ref, yc, ct_s, xc, cm,
    )
    advance(
        L, X, True, v_ref, u_ref, rho_ref, (f_ref, g_ref), ct_s, xc, cm, u1_s, v1_s, None, sinks, sems
    )


def last_step(L, X, GX, NY, n, args):
    R = 6 * L * X
    vm = pltpu.VMEM
    return call(
        functools.partial(last_kernel, L, X, GX, NY, n),
        [sds(R, LANES), sds(R, LANES)],
        args,
        specs=[SMEM] * 2 + [VMEM] * (len(args) - 2),
        scratch=contact_scratch(L, X, NY)
        + [
            vm((X, LANES), F32),
            vm((2, 6 * L, LANES), F32),
            vm((2, X, LANES), F32),
            vm((R, LANES), F32),
            vm((R, LANES), F32),
            pltpu.SemaphoreType.DMA((2,)),
        ],
        limit=grant(X, NY) + 2 * R * LANES * 4,
        out_spec=pl.BlockSpec(memory_space=pl.ANY),
        flops=80 * R * LANES,
        name="last",
    )


def swap(x, axis="gy"):
    return lax.ppermute(x, axis, [(i, i ^ 1) for i in range(lax.axis_size(axis))])


def cross(x, axis="gy", wrap=False):
    n = lax.axis_size(axis)
    to = [i + 1 if i % 2 else i - 1 for i in range(n)]
    to = [t % n if wrap else min(max(t, 0), n - 1) for t in to]
    return lax.ppermute(x, axis, list(enumerate(to)))


def far(x):
    n = lax.axis_size("gy")
    return [x] + [
        lax.ppermute(x, "gy", [(i, i ^ (2 * k)) for i in range(n)]) for k in range(1, n // 2)
    ]


def both(parts):
    return [p for part in parts for p in (part, swap(part))]


def body(
    displacement,
    velocity,
    modulus,
    density,
    clearance,
    mortar_coupling,
    pair_owner,
    pair_row,
    pair_offset,
    pair_active,
):
    L, X, Y = displacement.shape[2:]
    assert Y == LANES and L == SUB and X == LANES
    GX, NY = lax.axis_size("gx"), lax.axis_size("gy")

    u, v = displacement.reshape(-1, Y), velocity.reshape(-1, Y)
    e, rho = modulus.reshape(-1, Y), density.reshape(-1, Y)
    own, row, off, act = (
        a.transpose(0, 2, 1).reshape(1, -1)
        for a in (pair_owner, pair_row, pair_offset, pair_active)
    )
    parts = far(first_message(u, clearance, (own, row, off, act), L, X))
    xl, xh, x1, x2, y = pack(u, e, L, X)
    rx1, rx2 = swap(x1, "gx"), cross(x2, "gx", True)
    coef, diag = coupling(e, L, X)
    diag, rx1, rx2, *parts = lax.optimization_barrier((diag, rx1, rx2, *parts))
    m1, m2 = corners(8 * L, y, rx1, rx2)
    f = stencil(u, coef, diag, L, X, (0, 1, 2), (m1, *parts[1:]))
    stiff = (xl, xh, y, rx1, rx2, swap(m1), cross(m2))
    messages = both(parts)
    cm, ct, xc, face = contact(
        L, X, GX, NY, 8 * L,
        (own, row, mortar_coupling, clearance, v, u, rho, f, *stiff, *stiff, *messages),
    )
    parts = far(face)
    u, v, xl, xh, x1, x2, y = step(L, X, (v, u, rho, f, cm, ct, xc))
    rx1, rx2 = swap(x1, "gx"), cross(x2, "gx", True)
    f = stencil(u, coef, diag, L, X, (0, 1))
    f, rx1, rx2, *parts = lax.optimization_barrier((f, rx1, rx2, *parts))
    m1, m2 = corners(6 * L, y, rx1, rx2)
    g = stencil(u, coef, diag, L, X, (2,), (m1, f, *parts[1:]))
    edges = (xl, xh, y, rx1, rx2, swap(m1), cross(m2))
    u, v = last_step(
        L, X, GX, NY, 6 * L,
        (own, row, mortar_coupling, v, u, rho, f, g, *edges, *stiff, *messages, *both(parts)),
    )
    return u.reshape(displacement.shape), v.reshape(velocity.shape)


def solution(mesh):
    return jax.shard_map(
        body,
        mesh=mesh,
        in_specs=(
            P(None, None, None, "gx", "gy"),
            P(None, None, None, "gx", "gy"),
            P(None, None, "gx", "gy"),
            P(None, None, "gx", "gy"),
            P("gx", "gy"),
            P(),
            P("gx", "gy", None),
            P("gx", "gy", None),
            P("gx", "gy", None),
            P("gx", "gy", None),
        ),
        out_specs=(P(None, None, None, "gx", "gy"), P(None, None, None, "gx", "gy")),
        check_vma=False,
    )
```

```python
import functools

import jax
import jax.numpy as jnp
from jax import lax
from jax.experimental import pallas as pl
from jax.experimental.pallas import tpu as pltpu
from jax.sharding import PartitionSpec as P

F32 = jnp.float32
BF16 = jnp.bfloat16
INTERSECTIONS = 2
STEPS = 2
time_step = 0.2
penalty_stiffness = 4.0

SUB = 8
LANES = 128
FLAT = [(0, 1, 0), (1, -1, 0), (1, 0, 0), (1, 1, 0)]
SIDE = [(dz, dx, 1) for dz in (-1, 0, 1) for dx in (-1, 0, 1)]
HALF = FLAT + SIDE
NSIDE = len(SIDE)
NHALF = len(HALF)
NCOEF = NHALF + NSIDE

VMEM = pl.BlockSpec(memory_space=pltpu.VMEM)
SMEM = pl.BlockSpec(memory_space=pltpu.SMEM)


def twice_weight(nonzero):
    return 2.0 * 0.5 ** (nonzero - 1)


def lane_ids(rows=SUB):
    return lax.broadcasted_iota(jnp.int32, (rows, LANES), 1)


def sub_ids(rows=SUB):
    return lax.broadcasted_iota(jnp.int32, (rows, LANES), 0)


def take_lanes(values, index):
    return jnp.take_along_axis(values, index, axis=1)


def call(
    kernel, out_shape, args, specs=None, scratch=(), limit=None, flops=0, name=None, out_spec=VMEM
):
    nbytes = sum(a.size * 4 for a in args)
    return pl.pallas_call(
        kernel,
        out_shape=out_shape,
        in_specs=specs or [VMEM] * len(args),
        out_specs=jax.tree.map(lambda _: out_spec, out_shape),
        scratch_shapes=scratch,
        name=name,
        cost_estimate=pl.CostEstimate(flops=flops, bytes_accessed=nbytes, transcendentals=0),
        compiler_params=pltpu.CompilerParams(vmem_limit_bytes=limit),
    )(*args)


def sds(*shape):
    return jax.ShapeDtypeStruct(shape, F32)


def coupling_kernel(L, X, e_ref, c_ref, d_ref, ep, ey):
    rows, pad, nt = 2 * L * X, X + SUB, X // SUB
    zero = jnp.zeros((pad, LANES), F32)
    for s in (ep, ey):
        s[pl.ds(0, pad), :] = zero
        s[pl.ds(pad + rows, pad), :] = zero
    for j in range(NHALF):
        c_ref[j, pl.ds(0, pad), :] = zero
        c_ref[j, pl.ds(pad + rows, pad), :] = zero
    lane, sub = lane_ids(), sub_ids()

    def fill(i, _):
        for k in range(nt):
            r = pl.multiple_of(i * X, X) + k * SUB
            e = e_ref[pl.ds(r, SUB), :]
            ep[pl.ds(r + pad, SUB), :] = e
            ey[pl.ds(r + pad, SUB), :] = jnp.where(
                lane == LANES - 1, 0.0, pltpu.roll(e, LANES - 1, 1)
            )
        return 0

    lax.fori_loop(0, 2 * L, fill, 0)

    def block(i, _):
        layer = lax.rem(i, L)
        up = jnp.where(layer < L - 1, 1.0, 0.0).astype(F32)
        down = jnp.where(layer > 0, 1.0, 0.0).astype(F32)
        for k in range(nt):
            r = pl.multiple_of(i * X, X) + k * SUB + pad
            e = ep[pl.ds(r, SUB), :]
            for j, (dz, dx, dy) in enumerate(HALF):
                o = (ey if dy else ep)[pl.ds(r + dz * X + dx, SUB), :]
                c = (e * twice_weight(abs(dz) + abs(dx) + dy)) * o / (e + o)
                if dz == 1:
                    c = c * up
                if dz == -1:
                    c = c * down
                if dx == 1 and k == nt - 1:
                    c = jnp.where(sub == SUB - 1, 0.0, c)
                if dx == -1 and k == 0:
                    c = jnp.where(sub == 0, 0.0, c)
                c_ref[j, pl.ds(r, SUB), :] = c
                if dy:
                    c_ref[NSIDE + j, pl.ds(r, SUB), :] = pltpu.roll(c, 1, 1)
        return 0

    lax.fori_loop(0, 2 * L, block, 0)

    def total(i, _):
        for k in range(nt):
            r = pl.multiple_of(i * X, X) + k * SUB + pad
            own, back = None, None
            for j, (dz, dx, dy) in enumerate(HALF):
                f = c_ref[j, pl.ds(r, SUB), :]
                b = c_ref[j, pl.ds(r - dz * X - dx, SUB), :]
                own = f if own is None else own + f
                if dy:
                    back = b if back is None else back + b
                else:
                    own = own + b
            d_ref[pl.ds(r - pad, SUB), :] = own + pltpu.roll(back, 1, 1)
        return 0

    lax.fori_loop(0, 2 * L, total, 0)


def coupling(modulus, L, X):
    rows, pad = 2 * L * X, X + SUB
    return call(
        functools.partial(coupling_kernel, L, X),
        [sds(NCOEF, rows + 2 * pad + SUB, LANES), sds(rows, LANES)],
        [modulus],
        scratch=[pltpu.VMEM((rows + 2 * pad, LANES), F32)] * 2,
        limit=5 << 20,
        flops=200 * rows * LANES,
        name="coupling",
    )


def spaced(X):
    return X + SUB, X + 5 * SUB


def stencil_kernel(L, X, group, comps, u_ref, c_ref, d_ref, *rest):
    f_ref, up = rest[-2:]
    nt, count, lowest = X // SUB, len(comps), comps[0]
    S, pad = spaced(X)
    zero = jnp.zeros((pad, LANES), F32)
    up[pl.ds(0, pad), :] = zero
    up[pl.ds(pad + 2 * count * L * S, pad), :] = zero

    def field(which):
        return which // count * 3 + lowest + lax.rem(which, count)

    def fill(i, _):
        source = field(i // L) * L + lax.rem(i, L)
        to = pl.multiple_of(i * S, SUB) + pad
        for k in range(nt):
            r = pl.multiple_of(source * X, X) + k * SUB
            up[pl.ds(to + k * SUB, SUB), :] = u_ref[pl.ds(r, SUB), :]
        up[pl.ds(to + X, SUB), :] = jnp.zeros((SUB, LANES), F32)
        return 0

    lax.fori_loop(0, 2 * count * L, fill, 0)

    def block(i, _):
        which = i // (nt // group)
        first = lax.rem(i, nt // group) * group * SUB
        body = which // count
        for k in range(group):
            for layer in range(L):
                ru = pl.multiple_of(which * L * S + layer * S + first, SUB) + k * SUB + pad
                rf = pl.multiple_of(which * L * X + layer * X + first, SUB) + k * SUB
                rd = pl.multiple_of(body * L * X + layer * X + first, SUB) + k * SUB
                rc = rd + X + SUB
                t = {
                    (dz, dx): up[pl.ds(ru + dz * S + dx, SUB), :]
                    for dz in (-1, 0, 1)
                    for dx in (-1, 0, 1)
                }
                acc = -d_ref[pl.ds(rd, SUB), :] * t[0, 0]
                ahead, behind = None, None
                for j, (dz, dx, dy) in enumerate(HALF):
                    back = c_ref[j, pl.ds(rc - dz * X - dx, SUB), :] * t[-dz, -dx]
                    near = c_ref[j + NSIDE * dy, pl.ds(rc, SUB), :] * t[dz, dx]
                    if dy:
                        ahead = near if ahead is None else ahead + near
                        behind = back if behind is None else behind + back
                    else:
                        acc = acc + near
                        acc = acc + back
                f_ref[pl.ds(rf, SUB), :] = (
                    acc + pltpu.roll(ahead, LANES - 1, 1) + pltpu.roll(behind, 1, 1)
                )
        return 0

    lax.fori_loop(0, 2 * count * (nt // group), block, 0)


def stencil(u, coef, diag, L, X, comps, after=()):
    S, pad = spaced(X)
    rows = 2 * len(comps) * L * X
    return call(
        functools.partial(stencil_kernel, L, X, X // SUB // 2, comps),
        sds(rows, LANES),
        [u, coef, diag, *after],
        specs=[VMEM] * 3 + [pl.BlockSpec(memory_space=pl.ANY)] * len(after),
        scratch=[pltpu.VMEM((2 * len(comps) * L * S + 2 * pad, LANES), F32)],
        limit=5 << 20,
        flops=60 * rows * LANES,
        name="stencil",
    )


def message_kernel(L, X, u_ref, gap_ref, own, row, off, act, out_ref, tile, gap, words, sems):
    copies = [
        pltpu.make_async_copy(u_ref.at[pl.ds(2 * L * X, X)], out_ref.at[pl.ds(0, X)], sems.at[0]),
        pltpu.make_async_copy(u_ref.at[pl.ds(5 * L * X, X)], tile, sems.at[1]),
        pltpu.make_async_copy(gap_ref, gap, sems.at[2]),
    ]
    small = [
        pltpu.make_async_copy(ref, words.at[pl.ds(k, 1)], sems.at[3 + k])
        for k, ref in enumerate((row, off, act, own))
    ]
    for c in small + copies:
        c.start()
    for c in small:
        c.wait()
    lane = lane_ids()
    for k in range(4):
        halves = [
            jnp.broadcast_to(words[pl.ds(k, 1), pl.ds(h * LANES, LANES)].astype(F32), (SUB, LANES))
            for h in range(INTERSECTIONS)
        ]
        for e in range(INTERSECTIONS):
            index = (lane * INTERSECTIONS + e) & (LANES - 1)
            picked = [take_lanes(x, index) for x in halves]
            value = jnp.where(lane < LANES // INTERSECTIONS, picked[0], picked[1])
            out_ref[pl.ds(2 * X + INTERSECTIONS * k + e, 1), :] = value[:1]
    for c in copies:
        c.wait()
    out_ref[pl.ds(X, X), :] = tile[...] + gap[...]


def first_message(u, clearance, pairs, L, X):
    return call(
        functools.partial(message_kernel, L, X),
        sds(2 * X + 4 * INTERSECTIONS, LANES),
        [u, clearance, *pairs],
        specs=[pl.BlockSpec(memory_space=pl.ANY)] * 6,
        scratch=[
            pltpu.VMEM((X, LANES), F32),
            pltpu.VMEM((X, LANES), F32),
            pltpu.VMEM((4, INTERSECTIONS * X), jnp.int32),
            pltpu.SemaphoreType.DMA((7,)),
        ],
        limit=57 << 20,
        name="message",
    )


def edge_index():
    return jnp.where(lane_ids() < LANES // 2, 0, LANES - 1)


def choose(flag, a, b):
    return jnp.where(jnp.broadcast_to(flag, a.shape) == 1, a, b)


def pair_rows(odd, low, high, first_ref, second_ref):
    first_ref[...] = choose(odd, low, high)
    second_ref[...] = choose(odd, high, low)


def x_rows(L, X, start, count, src, xl_ref, xh_ref, at):
    for bc in range(count):
        base = start + bc * L * X
        xl_ref[pl.ds((at + bc) * L, L), :] = src[pl.ds(base, L, stride=X), :]
        xh_ref[pl.ds((at + bc) * L, L), :] = src[pl.ds(base + X - 1, L, stride=X), :]


def pack_kernel(L, X, u_ref, e_ref, xl_ref, xh_ref, x1_ref, x2_ref, y_ref, w_ref):
    nt = X // SUB
    x_rows(L, X, 0, 6, u_ref, xl_ref, xh_ref, 0)
    x_rows(L, X, 0, 2, e_ref, xl_ref, xh_ref, 6)
    pair_rows(lax.axis_index("gx") % 2, xl_ref[...], xh_ref[...], x1_ref, x2_ref)
    index = edge_index()
    slot = lane_ids() % (LANES // 2)

    def tile(k, _):
        r = pl.multiple_of(k * SUB, SUB)
        w = jnp.zeros((SUB, LANES), F32)
        for f in range(8 * L):
            src, row = (u_ref, f) if f < 6 * L else (e_ref, f - 6 * L)
            v = src[pl.ds(row * X + r, SUB), :]
            w = jnp.where(slot == f, take_lanes(v, index), w)
        w_ref[pl.ds(r, SUB), :] = w
        return 0

    lax.fori_loop(0, nt, tile, 0)
    y_ref[...] = w_ref[...].T


def pack(u, e, L, X):
    return call(
        functools.partial(pack_kernel, L, X),
        [sds(8 * L, LANES)] * 4 + [sds(LANES, LANES)],
        [u, e],
        scratch=[pltpu.VMEM((X, LANES), F32)],
        limit=1 << 20,
        flops=u.size,
        name="pack",
    )


def corner_kernel(n, y_ref, r1_ref, r2_ref, m1_ref, m2_ref):
    half = LANES // 2
    odd_x, odd_y = lax.axis_index("gx") % 2, lax.axis_index("gy") % 2
    lane = lane_ids(n)
    r1, r2 = r1_ref[...], r2_ref[...]
    low, high = choose(odd_x, r1, r2), choose(odd_x, r2, r1)
    left = y_ref[pl.ds(0, n), :], jnp.where(lane == 0, low, pltpu.roll(high, LANES - 1, 1))
    right = y_ref[pl.ds(half, n), :], jnp.where(lane == 0, pltpu.roll(low, 1, 1), high)
    for k in range(2):
        at = pl.ds(k * n, n)
        pair_rows(odd_y, left[k], right[k], m1_ref.at[at], m2_ref.at[at])


def corners(n, y, r1, r2):
    return call(
        functools.partial(corner_kernel, n),
        [sds(2 * n, LANES), sds(2 * n, LANES)],
        [y, r1, r2],
        limit=1 << 20,
        name="corners",
    )


def split(x):
    high = x.astype(BF16)
    return high, (x - high.astype(F32)).astype(BF16)


def dot(a, b, dims=((1,), (0,))):
    return lax.dot_general(a, b, (dims, ((), ())), preferred_element_type=F32)


def project(x, pair, dims):
    high, low = split(x)
    return x + (dot(high, pair[0], dims) + dot(high, pair[1], dims) + dot(low, pair[0], dims))


def contact_and_edges(L, X, GX, NY, n, first, later, own_s, row_s, m_ref, gathered, whole, grow, work, pairs_ref, yc, ct_s, xc, cm):
    oxl, oxh, oy, rx1, rx2, ry1, ry2, exl, exh, ey, erx1, erx2, ery1, ery2 = gathered
    nt, half, ne = X // SUB, LANES // 2, 8 * L
    gx, me = lax.axis_index("gx"), lax.axis_index("gy")
    lane, sub = lane_ids(), sub_ids()
    lane_t = lane_ids(X)

    mh, ml = split(m_ref[...])
    straight, flipped = ((1,), (0,)), ((1,), (1,))
    pairs_ref[...] = jnp.zeros((LANES, LANES), F32)
    for q in range(NY):
        pairs_ref[pl.ds(q * SUB, SUB), :] = first[q][pl.ds(2 * X, SUB), :]
    columns = pairs_ref[...].T
    my_chip, my_core = me // 2, me % 2
    for q in range(NY):
        chip = lax.bitwise_xor(my_chip, q // 2)
        core = my_core if q % 2 == 0 else 1 - my_core
        owner = chip * 2 + core
        whole[pl.ds(pl.multiple_of(owner * X, X), X), :] = later[q][pl.ds(0, X), :]

    def gather(i, _):
        for k in range(SUB):
            p = i * SUB + k
            at = own_s[0, p] * X + row_s[0, p]
            to = (k % INTERSECTIONS) * X + i * (SUB // INTERSECTIONS) + k // INTERSECTIONS
            grow[pl.ds(to, 1), :] = whole[pl.ds(at, 1), :]
        return 0

    lax.fori_loop(0, INTERSECTIONS * X // SUB, gather, 0)

    def column(f):
        return jnp.broadcast_to(columns[:, f : f + 1], (X, LANES))

    slave = None
    for e in range(INTERSECTIONS):
        off = column(2 + e).astype(jnp.int32)
        moved = take_lanes(grow[pl.ds(e * X, X), :], (lane_t + off) & (LANES - 1))
        gap = later[0][pl.ds(X, X), :] - project(moved, (mh, ml), straight)
        t = column(4 + e) * (penalty_stiffness * jnp.maximum(0.0, -gap))
        slave = t if slave is None else slave + t
    cm[1] = slave

    fh, fl = split(later[0][pl.ds(0, X), :])
    me_f = me.astype(F32)
    node = lax.broadcasted_iota(jnp.int32, (X, X), 0).astype(F32)
    master = jnp.zeros((X, LANES), F32)
    blocks = [(q, e) for q in range(NY) for e in range(INTERSECTIONS)]
    for s, (q, e) in enumerate(blocks):
        base = q * SUB
        hot = jnp.where(node == pairs_ref[base + e : base + e + 1, :], 1.0, 0.0).astype(BF16)
        rows = dot(hot, fh, ((0,), (0,))) + dot(hot, fl, ((0,), (0,)))
        off = column(base + 2 + e).astype(jnp.int32)
        work[pl.ds(s * X, X), :] = take_lanes(rows, (lane_t + off) & (LANES - 1))
    for s, (q, e) in enumerate(blocks):
        gap = later[q][pl.ds(X, X), :] - project(
            work[pl.ds(s * X, X), :], (mh, ml), straight
        )
        work[pl.ds(s * X, X), :] = penalty_stiffness * jnp.maximum(0.0, -gap)
    for s, (q, e) in enumerate(blocks):
        base = q * SUB
        back = project(work[pl.ds(s * X, X), :], (mh, ml), flipped)
        off = column(base + 2 + e).astype(jnp.int32)
        work[pl.ds(s * X, X), :] = take_lanes(back, (lane_t - off) & (LANES - 1))
    for s, (q, e) in enumerate(blocks):
        base = q * SUB
        weight = jnp.where(
            pairs_ref[base + 6 + e : base + 7 + e, :] == me_f,
            pairs_ref[base + 4 + e : base + 5 + e, :],
            0.0,
        )
        hot = jnp.where(node == pairs_ref[base + e : base + e + 1, :], weight, 0.0).astype(BF16)
        bh, bl = split(work[pl.ds(s * X, X), :])
        master = master + (dot(hot, bh) + dot(hot, bl))
    cm[0] = -master

    inside = (gx > 0, gx < GX - 1, me > 0, me < NY - 1)
    ok = [jnp.where(x, 1.0, 0.0).astype(F32) for x in inside]

    def edge(own_e, own_u, near_e, near_u, corner_e, corner_u, put):
        near = {}
        for d in (-1, 0, 1):
            value_e, value_u = near_e, list(near_u)
            if d:
                value_e = pltpu.roll(near_e, (-d) % LANES, 1)
                value_u = [pltpu.roll(x, (-d) % LANES, 1) for x in near_u]
                at = lane == (0 if d < 0 else LANES - 1)
                if corner_e is None:
                    value_e = jnp.where(at, 0.0, value_e)
                else:
                    value_e = jnp.where(at, corner_e, value_e)
                    value_u = [jnp.where(at, c, x) for c, x in zip(corner_u, value_u)]
            near[d] = (value_e, value_u)
        sums = [None] * 3
        for dz in (-1, 0, 1):
            for d in (-1, 0, 1):
                o, us = near[d]
                if dz:
                    o = pltpu.roll(o, (-dz) % SUB, 0)
                    o = jnp.where(sub == (0 if dz < 0 else SUB - 1), 0.0, o)
                    us = [pltpu.roll(x, (-dz) % SUB, 0) for x in us]
                c = (own_e * twice_weight(1 + abs(dz) + abs(d))) * o / (own_e + o)
                for comp in range(3):
                    term = c * (us[comp] - own_u[comp])
                    sums[comp] = term if sums[comp] is None else sums[comp] + term
        for comp in range(3):
            put(comp, sums[comp])

    def rows(ref, k):
        return ref[pl.ds(k, L), :]

    def got(refs, k, axis):
        return choose(odd[axis], rows(refs[0], k), rows(refs[1], k))

    odd = gx % 2, me % 2

    yc[...] = jnp.zeros((LANES, LANES), F32)
    for b in range(2):
        ue = [(b * 3 + c) * L for c in range(3)]
        ee = (6 + b) * L
        for s, (own_x, got_x, own_xe, got_xe) in enumerate(
            ((oxl, (rx1, rx2), exl, (erx1, erx2)), (oxh, (rx2, rx1), exh, (erx2, erx1)))
        ):
            edge(
                rows(own_xe, ee),
                [rows(own_x, k) for k in ue],
                got(got_xe, ee, 0) * ok[s],
                [got(got_x, k, 0) for k in ue],
                None,
                None,
                lambda c, v, s=s, ue=ue: xc.__setitem__((s, pl.ds(ue[c], L), slice(None)), v),
            )
        for s, (got_y, got_ye) in enumerate((((ry1, ry2), (ery1, ery2)), ((ry2, ry1), (ery2, ery1)))):
            corner_ok = jnp.where(lane == 0, ok[0], ok[1]) * ok[2 + s]
            edge(
                rows(ey, s * half + ee),
                [rows(oy, s * half + k) for k in ue],
                got(got_ye, ee, 1) * ok[2 + s],
                [got(got_y, k, 1) for k in ue],
                got(got_ye, ne + ee, 1) * corner_ok,
                [got(got_y, n + k, 1) for k in ue],
                lambda c, v, s=s, ue=ue: yc.__setitem__((pl.ds(s * half + ue[c], L), slice(None)), v),
            )
    ct_s[...] = yc[...].T


def forced(L, X, k, f, face, base, ct, xc, cm_tile):
    lane, sub = lane_ids(), sub_ids()
    half = LANES // 2
    pick = jnp.where(lane == 0, f, jnp.where(lane == LANES - 1, half + f, half - 1))
    force = base + take_lanes(ct, pick)
    if k == 0:
        force = force + jnp.where(sub == 0, xc[0, pl.ds(f, 1), :], 0.0)
    if k == X // SUB - 1:
        force = force + jnp.where(sub == SUB - 1, xc[1, pl.ds(f, 1), :], 0.0)
    if cm_tile is not None:
        force = force + face * cm_tile
    return force


def advance(L, X, last, v_ref, u_ref, rho_ref, forces, ct_s, xc, cm, u1_ref, v1_ref, w_s, sinks, sems):
    nt, half = X // SUB, LANES // 2
    index = edge_index()
    slot = lane_ids() % half
    if not last:
        w_s[...] = jnp.zeros((X, LANES), F32)

    def layer_of(i, _):
        b, layer = i // L, lax.rem(i, L)
        face = jnp.where(layer == 0, 1.0, 0.0).astype(F32)
        for k in range(nt):
            rr = pl.multiple_of(i * X, X) + k * SUB
            scale = time_step / rho_ref[pl.ds(rr, SUB), :]
            ct = ct_s[pl.ds(k * SUB, SUB), :]
            if not last:
                w = w_s[pl.ds(k * SUB, SUB), :]
            for c in range(3):
                f = (b * 3 + c) * L + layer
                r = pl.multiple_of(f * X, X) + k * SUB
                if len(forces) == 2:
                    fr = pl.multiple_of(((b * 2 + c) if c < 2 else b) * L * X + layer * X, X)
                    base = forces[0 if c < 2 else 1][pl.ds(fr + k * SUB, SUB), :]
                else:
                    base = forces[0][pl.ds(r, SUB), :]
                tile = cm[b, pl.ds(k * SUB, SUB), :] if c == 2 else None
                vel = v_ref[pl.ds(r, SUB), :] + scale * forced(L, X, k, f, face, base, ct, xc, tile)
                disp = u_ref[pl.ds(r, SUB), :] + time_step * vel
                v1_ref[pl.ds(r, SUB), :] = vel
                u1_ref[pl.ds(r, SUB), :] = disp
                if not last:
                    w = jnp.where(slot == f, take_lanes(disp, index), w)
            if not last:
                w_s[pl.ds(k * SUB, SUB), :] = w
        if last:
            for c in range(3):
                at = pl.ds(pl.multiple_of(((b * 3 + c) * L + layer) * X, X), X)
                for s, ref in enumerate((u1_ref, v1_ref)):
                    pltpu.make_async_copy(ref.at[at], sinks[s].at[at], sems.at[s]).start()
        return 0

    lax.fori_loop(0, 2 * L, layer_of, 0)
    if last:
        for s, ref in enumerate((u1_ref, v1_ref)):
            pltpu.make_async_copy(ref, sinks[s], sems.at[s]).wait()


NGOT = 14


def contact_kernel(L, X, GX, NY, n, own_s, row_s, m_ref, gap_ref, v_ref, u_ref, rho_ref, f_ref, *rest):
    gathered, first = rest[:NGOT], rest[NGOT : NGOT + NY]
    cm, ct_s, xc, face_out, whole, grow, work, pairs_ref, yc = rest[NGOT + NY :]
    contact_and_edges(
        L, X, GX, NY, n, first, first, own_s, row_s, m_ref, gathered,
        whole, grow, work, pairs_ref, yc, ct_s, xc, cm,
    )
    for b in range(2):
        f = (b * 3 + 2) * L
        for k in range(X // SUB):
            at = pl.ds(f * X + k * SUB, SUB)
            part = pl.ds(k * SUB, SUB)
            force = forced(L, X, k, f, 1.0, f_ref[at, :], ct_s[part, :], xc, cm[b, part, :])
            scale = time_step / rho_ref[pl.ds(b * L * X + k * SUB, SUB), :]
            disp = u_ref[at, :] + time_step * (v_ref[at, :] + scale * force)
            if b == 1:
                disp = disp + gap_ref[part, :]
            face_out[pl.ds(b * X + k * SUB, SUB), :] = disp


def contact_scratch(L, X, NY):
    vm = pltpu.VMEM
    return [
        vm((NY * X, LANES), F32),
        vm((INTERSECTIONS * X, LANES), F32),
        vm((NY * INTERSECTIONS * X, LANES), F32),
        vm((LANES, LANES), F32),
        vm((LANES, LANES), F32),
    ]


def grant(X, NY):
    return (3 << 20) + 2 * NY * INTERSECTIONS * X * LANES * 4 * max(1, NY // 8)


def contact(L, X, GX, NY, n, args):
    return call(
        functools.partial(contact_kernel, L, X, GX, NY, n),
        [sds(2, X, LANES), sds(X, LANES), sds(2, 6 * L, LANES), sds(2 * X, LANES)],
        args,
        specs=[SMEM] * 2 + [VMEM] * (len(args) - 2),
        scratch=contact_scratch(L, X, NY),
        limit=grant(X, NY),
        flops=60 * NY * INTERSECTIONS * X * LANES,
        name="contact",
    )


def step_kernel(L, X, v_ref, u_ref, rho_ref, f_ref, cm, ct_s, xc, *rest):
    u1_ref, v1_ref, xl_ref, xh_ref, x1_ref, x2_ref, y_ref, w_s = rest
    advance(L, X, False, v_ref, u_ref, rho_ref, (f_ref,), ct_s, xc, cm, u1_ref, v1_ref, w_s, None, None)
    x_rows(L, X, 0, 6, u1_ref, xl_ref, xh_ref, 0)
    pair_rows(lax.axis_index("gx") % 2, xl_ref[...], xh_ref[...], x1_ref, x2_ref)
    y_ref[...] = w_s[...].T


def step(L, X, args):
    R = 6 * L * X
    return call(
        functools.partial(step_kernel, L, X),
        [sds(R, LANES), sds(R, LANES)] + [sds(6 * L, LANES)] * 4 + [sds(LANES, LANES)],
        args,
        scratch=[pltpu.VMEM((X, LANES), F32)],
        limit=2 << 20,
        flops=20 * R * LANES,
        name="step",
    )


def last_kernel(L, X, GX, NY, n, own_s, row_s, m_ref, v_ref, u_ref, rho_ref, f_ref, g_ref, *rest):
    gathered, rest = rest[:NGOT], rest[NGOT:]
    first, later, rest = rest[:NY], rest[NY : 2 * NY], rest[2 * NY :]
    sinks, scratch = rest[:2], rest[2:]
    whole, grow, work, pairs_ref, yc, ct_s, xc, cm, u1_s, v1_s, sems = scratch
    contact_and_edges(
        L, X, GX, NY, n, first, later, own_s, row_s, m_ref, gathered,
        whole, grow, work, pairs_ref, yc, ct_s, xc, cm,
    )
    advance(
        L, X, True, v_ref, u_ref, rho_ref, (f_ref, g_ref), ct_s, xc, cm, u1_s, v1_s, None, sinks, sems
    )


def last_step(L, X, GX, NY, n, args):
    R = 6 * L * X
    vm = pltpu.VMEM
    return call(
        functools.partial(last_kernel, L, X, GX, NY, n),
        [sds(R, LANES), sds(R, LANES)],
        args,
        specs=[SMEM] * 2 + [VMEM] * (len(args) - 2),
        scratch=contact_scratch(L, X, NY)
        + [
            vm((X, LANES), F32),
            vm((2, 6 * L, LANES), F32),
            vm((2, X, LANES), F32),
            vm((R, LANES), F32),
            vm((R, LANES), F32),
            pltpu.SemaphoreType.DMA((2,)),
        ],
        limit=grant(X, NY) + 2 * R * LANES * 4,
        out_spec=pl.BlockSpec(memory_space=pl.ANY),
        flops=80 * R * LANES,
        name="last",
    )


def swap(x, axis="gy"):
    return lax.ppermute(x, axis, [(i, i ^ 1) for i in range(lax.axis_size(axis))])


def cross(x, axis="gy", wrap=False):
    n = lax.axis_size(axis)
    to = [i + 1 if i % 2 else i - 1 for i in range(n)]
    to = [t % n if wrap else min(max(t, 0), n - 1) for t in to]
    return lax.ppermute(x, axis, list(enumerate(to)))


def far(x):
    n = lax.axis_size("gy")
    return [x] + [
        lax.ppermute(x, "gy", [(i, i ^ (2 * k)) for i in range(n)]) for k in range(1, n // 2)
    ]


def both(parts):
    return [p for part in parts for p in (part, swap(part))]


def body(
    displacement,
    velocity,
    modulus,
    density,
    clearance,
    mortar_coupling,
    pair_owner,
    pair_row,
    pair_offset,
    pair_active,
):
    L, X, Y = displacement.shape[2:]
    assert Y == LANES and L == SUB and X == LANES
    GX, NY = lax.axis_size("gx"), lax.axis_size("gy")

    u, v = displacement.reshape(-1, Y), velocity.reshape(-1, Y)
    e, rho = modulus.reshape(-1, Y), density.reshape(-1, Y)
    own, row, off, act = (
        a.transpose(0, 2, 1).reshape(1, -1)
        for a in (pair_owner, pair_row, pair_offset, pair_active)
    )
    parts = far(first_message(u, clearance, (own, row, off, act), L, X))
    xl, xh, x1, x2, y = pack(u, e, L, X)
    rx1, rx2 = swap(x1, "gx"), cross(x2, "gx", True)
    coef, diag = coupling(e, L, X)
    diag, rx1, rx2, *parts = lax.optimization_barrier((diag, rx1, rx2, *parts))
    m1, m2 = corners(8 * L, y, rx1, rx2)
    f = stencil(u, coef, diag, L, X, (0, 1, 2), (m1, *parts[1:]))
    stiff = (xl, xh, y, rx1, rx2, swap(m1), cross(m2))
    messages = both(parts)
    cm, ct, xc, face = contact(
        L, X, GX, NY, 8 * L,
        (own, row, mortar_coupling, clearance, v, u, rho, f, *stiff, *stiff, *messages),
    )
    parts = far(face)
    u, v, xl, xh, x1, x2, y = step(L, X, (v, u, rho, f, cm, ct, xc))
    rx1, rx2 = swap(x1, "gx"), cross(x2, "gx", True)
    f = stencil(u, coef, diag, L, X, (0, 1))
    f, rx1, rx2, *parts = lax.optimization_barrier((f, rx1, rx2, *parts))
    m1, m2 = corners(6 * L, y, rx1, rx2)
    g = stencil(u, coef, diag, L, X, (2,), (m1, f, *parts[1:]))
    edges = (xl, xh, y, rx1, rx2, swap(m1), cross(m2))
    u, v = last_step(
        L, X, GX, NY, 6 * L,
        (own, row, mortar_coupling, v, u, rho, f, g, *edges, *stiff, *messages, *both(parts)),
    )
    return u.reshape(displacement.shape), v.reshape(velocity.shape)


def solution(mesh):
    return jax.shard_map(
        body,
        mesh=mesh,
        in_specs=(
            P(None, None, None, "gx", "gy"),
            P(None, None, None, "gx", "gy"),
            P(None, None, "gx", "gy"),
            P(None, None, "gx", "gy"),
            P("gx", "gy"),
            P(),
            P("gx", "gy", None),
            P("gx", "gy", None),
            P("gx", "gy", None),
            P("gx", "gy", None),
        ),
        out_specs=(P(None, None, None, "gx", "gy"), P(None, None, None, "gx", "gy")),
        check_vma=False,
    )
```
